256 devices in a mesh: ctx: 64 (over x, z_hi, y), ch: 4 (over z_lo, core).
Axes of the slice: x: 4, y: 4, z: 8 (z_hi: 4, z_lo: 2; z = z_hi * 2 + z_lo), core: 2. Of those that a mesh axis runs over, the one named last changes fastest.
Arguments:
- tokens: int32 [8192], P('ctx'), may hold values from 0 to 511
- complement: int32 [512], replicated, may hold values from 0 to 511, each once
- seg_lengths: int32 [256], replicated, may hold values from 1 to 256, as said below
- owner: int32 [64], replicated, may hold values from 0 to 63, each once
- embed: bfloat16 [512, 4096], P(None, 'ch')
- norm_gain: float32 [4096], P('ch'), may hold values from 0.24 to 10.3
- taps: float32 [128, 4096], P(None, 'ch'), may hold values from -0.54 to 0.54
- w_out: bfloat16 [4096, 4096], P('ch', 'ctx'), may hold values from -2 to 2
Outputs:
- owned: float32 [256, 4096], P('ctx', 'ch')
The draws below stay inside these ranges and needn't reach their ends.
Inputs may be any that keep to these rules, and one draw needn't show every extreme that they name: `seg_lengths`: segment lengths sum to 8192; the first segment is exactly 256 long and no segment is longer. `complement`: a permutation of the token ids. `owner`: a permutation of the ctx indices.
All inputs are finite; a program needn't handle non-finite values.
Results may differ from the reference program's by a relative error of at most 0.0023.
Values may be sent and summed in bfloat16 or wider, within the bound.
A program may use at most 128 MiB of HBM per device.

```python
import math
import jax
import jax.numpy as jnp
from jax import lax

D = 4096
VOCAB = 512
L = 128
OUTW = 4096
TOK_DEV = 128
SEG_BLK = 4
TOKENS = 8192
SEGS = 256
SEG_MOST = 256
N_CTX = 64


def draw_seg_lengths(key, part):
    rest_total = TOKENS - SEG_MOST
    rest_count = SEGS - 1
    long_count = max(1, SEGS // 32)
    short_count = rest_count - long_count
    long_high = min(SEG_MOST, (rest_total - short_count) // long_count)
    long_low = min(TOK_DEV, long_high)
    key_long, key_order, key_jitter = jax.random.split(jax.random.fold_in(key, 23), 3)
    long_sizes = jax.random.randint(key_long, (long_count,), long_low, long_high + 1, dtype=jnp.int32)
    short_total = (rest_total - jnp.sum(long_sizes)).astype(jnp.int32)
    spacing = short_total // short_count
    wiggle = jnp.maximum(0, (spacing - 1) // 2).astype(jnp.int32)
    cut_index = jnp.arange(short_count - 1, dtype=jnp.int32)
    base_cuts = (cut_index + 1) * short_total // short_count
    jitter_raw = jax.random.randint(key_jitter, (short_count - 1,), 0, 1 << 20, dtype=jnp.int32)
    jitter = jitter_raw % (2 * wiggle + 1) - wiggle
    cut_points = (base_cuts + jitter).astype(jnp.int32)
    short_edges = jnp.concatenate([jnp.zeros((1,), jnp.int32), cut_points, jnp.reshape(short_total, (1,))])
    short_sizes = (short_edges[1:] - short_edges[:-1]).astype(jnp.int32)
    sizes_all = jnp.concatenate([long_sizes, short_sizes])
    shuffle_order = jax.random.permutation(key_order, rest_count)
    inverse = jnp.argsort(shuffle_order).astype(jnp.int32)
    rest_sizes = sizes_all[inverse]
    return jnp.concatenate([jnp.array([SEG_MOST], jnp.int32), rest_sizes]).astype(jnp.int32)


def column_scale(key):
    key_scale = jax.random.fold_in(jax.random.fold_in(key, 11), 0)
    columns = jnp.arange(D, dtype=jnp.float32)
    spread = jax.random.uniform(key_scale, (D,), jnp.float32, 0.0, math.log(10.0))
    return jnp.exp(columns / D * math.log(3.0) + spread)


def draw_embed(key, part):
    key_values = jax.random.fold_in(jax.random.fold_in(key, 11), 1)
    col_scale = column_scale(key)
    values = jax.random.normal(key_values, (VOCAB, D), jnp.float32)
    return (values * col_scale[None, :] * 0.3).astype(jnp.bfloat16)


def draw_norm_gain(key, part):
    col_scale = column_scale(key)
    jitter_gain = jax.random.uniform(jax.random.fold_in(key, 29), (D,), jnp.float32, 0.85, 1.15)
    level_gain = math.sqrt((9.0 - 1.0) / (2.0 * math.log(3.0)) * (100.0 - 1.0) / (2.0 * math.log(10.0)))
    return (jitter_gain * level_gain / col_scale).astype(jnp.float32)


def set_ends(result, rng, smallest, high):
    spot = [jax.random.randint(jax.random.fold_in(rng, axis), (), 0, length) for axis, length in enumerate(result.shape)]
    longest = result.shape.index(max(result.shape))
    beside = spot[:longest] + [(spot[longest] + 1) % result.shape[longest]] + spot[longest + 1:]
    return result.at[tuple(spot)].set(smallest).at[tuple(beside)].set(high)


def strengthened(values, key, source, target, shards_of, factor):
    def block_of(axis_at):
        return (jnp.arange(values.shape[axis_at]) // (values.shape[axis_at] // shards_of)).reshape((-1,) + (1,) * (values.ndim - 1 - axis_at))

    first = jax.random.permutation(key, shards_of)[block_of(target)]
    other_side = (block_of(target) + shards_of // 2) % shards_of
    return jnp.where((block_of(source) == first) | (block_of(source) == other_side), factor * values, values)


def block_levels(rng, dims, shards, smallest, high):
    factor_of, own = 1.0, jax.random.fold_in(rng, 6)
    for dim, blocks in shards:
        heights = jnp.exp(jax.random.uniform(jax.random.fold_in(own, dim), (blocks,), jnp.float32, smallest / len(shards), high / len(shards)))
        factor_of = factor_of * jnp.repeat(heights, dims[dim] // blocks).reshape([-1 if axis == dim else 1 for axis in range(len(dims))])
    return factor_of


def normal_values(stream_key, extent, scale, limit, shards=(), held_as=jnp.bfloat16):
    values = jax.random.normal(stream_key, extent, jnp.float32) * scale
    if len(shards) > 0:
        values = block_levels(stream_key, extent, shards, -0.22, 0.18) * values
    return jnp.clip(values, min=-limit, max=limit).astype(held_as)


def heavy_noise(stream_key, extent, deviation, reach, shards, heavy, kind=jnp.bfloat16):
    values = deviation * jax.random.normal(stream_key, extent, jnp.float32)
    if shards:
        values = values * block_levels(stream_key, extent, shards, -0.22, 0.18)
    return jnp.clip(strengthened(values, jax.random.fold_in(stream_key, 3), *heavy), -reach, reach).astype(kind)


def setup_inputs(seed: int = 0) -> dict:
    keys = jax.random.split(jax.random.key(seed), 9)
    return {
        "tokens": set_ends(jax.random.randint(keys[0], (TOKENS,), 0, VOCAB), jax.random.fold_in(keys[0], 1), 0, VOCAB - 1).astype(jnp.int32),
        "complement": jax.random.permutation(keys[1], VOCAB).astype(jnp.int32),
        "seg_lengths": draw_seg_lengths(jax.random.fold_in(keys[8], 71), 0),
        "owner": jax.random.permutation(keys[3], N_CTX).astype(jnp.int32),
        "embed": draw_embed(jax.random.fold_in(keys[8], 71), 0),
        "norm_gain": draw_norm_gain(jax.random.fold_in(keys[8], 71), 0),
        "taps": normal_values(keys[6], (L, D), 0.09, 0.54, ((1, 4),), jnp.float32),
        "w_out": heavy_noise(keys[7], (D, OUTW), (D // 64) ** -0.5, 2.0, ((0, 4), (1, 64)), (0, 1, 64, 4.0)),
    }


norm_eps = 1e-06

def causal_mix(extended, age_rows, filter_taps):
    count = age_rows.shape[0]
    span = filter_taps.shape[0]
    total_sum = jnp.zeros((count, extended.shape[1]), jnp.float32)
    for tap_index in range(span):
        window = extended[span - 1 - tap_index:span - 1 - tap_index + count].astype(jnp.float32)
        total_sum = total_sum + jnp.where(age_rows[:, None] >= tap_index, filter_taps[tap_index][None, :] * window, 0.0)
    return total_sum

def reference(tokens, complement, seg_lengths, owner, embed, norm_gain, taps, w_out):
    positions = jnp.arange(TOKENS, dtype=jnp.int32)
    seg_ends = jnp.cumsum(seg_lengths).astype(jnp.int32)
    seg_starts = (seg_ends - seg_lengths).astype(jnp.int32)
    seg_index = lax.optimization_barrier(jnp.sum((seg_ends[None, :] <= positions[:, None]).astype(jnp.int32), axis=1)).astype(jnp.int32)
    age_fwd = (positions - seg_starts[seg_index]).astype(jnp.int32)
    age_rev = (seg_ends[seg_index] - 1 - positions).astype(jnp.int32)
    comp_ids = complement[tokens]
    table_full = embed.astype(jnp.float32)
    row_power = lax.optimization_barrier(jnp.sum(table_full * table_full, axis=1))
    inv_fwd = lax.rsqrt(row_power[tokens] / D + norm_eps)
    inv_rev = lax.rsqrt(row_power[comp_ids] / D + norm_eps)
    block_width = min(512, D)
    block_count = D // block_width
    table_blocks = table_full.reshape(VOCAB, block_count, block_width).transpose(1, 0, 2)
    gain_blocks = norm_gain.reshape(block_count, block_width)
    tap_blocks = taps.reshape(L, block_count, block_width).transpose(1, 0, 2)
    weight_blocks = w_out.reshape(block_count, block_width, OUTW)

    def one_block(carry, pieces):
        table_piece, gain_piece, tap_piece, weight_piece = pieces
        normed_fwd = (table_piece[tokens] * inv_fwd[:, None] * gain_piece[None, :]).astype(jnp.bfloat16)
        normed_rev = (table_piece[comp_ids] * inv_rev[:, None] * gain_piece[None, :]).astype(jnp.bfloat16)
        mixed_fwd = causal_mix(jnp.pad(normed_fwd, ((L - 1, 0), (0, 0))), age_fwd, tap_piece)
        padded_rev = jnp.pad(normed_rev, ((0, L - 1), (0, 0)))
        mixed_rev = jnp.flip(causal_mix(jnp.flip(padded_rev, 0), jnp.flip(age_rev, 0), tap_piece), 0)
        gated_fwd = (normed_fwd.astype(jnp.float32) * mixed_fwd).astype(jnp.bfloat16)
        gated_rev = (normed_rev.astype(jnp.float32) * mixed_rev).astype(jnp.bfloat16)
        strand_mean = ((gated_fwd.astype(jnp.float32) + gated_rev.astype(jnp.float32)) * 0.5).astype(jnp.bfloat16)
        carry = carry + jnp.dot(strand_mean.astype(jnp.float32), weight_piece.astype(jnp.float32), precision=lax.Precision.HIGHEST)
        return (carry, None)
    scores, _ = lax.scan(one_block, jnp.zeros((TOKENS, OUTW), jnp.float32), (table_blocks, gain_blocks, tap_blocks, weight_blocks))
    active = jax.nn.softplus(scores)
    seg_sums = jax.ops.segment_sum(active, seg_index, num_segments=SEGS)
    seg_means = seg_sums / seg_lengths.astype(jnp.float32)[:, None]
    holder = jnp.argsort(owner).astype(jnp.int32)
    slots = jnp.arange(SEGS, dtype=jnp.int32)
    source = (holder[slots // SEG_BLK] * SEG_BLK + slots % SEG_BLK).astype(jnp.int32)
    return seg_means[source]
```

```python
import functools

import jax
import jax.numpy as jnp
from jax import lax
from jax.experimental import pallas as pl
from jax.experimental.pallas import tpu as pltpu
from jax.sharding import PartitionSpec as P

norm_eps = 1e-06
LANES = 128
SUB = 8


def passed_along(array, axis, by):
    peers = lax.axis_size(axis)
    pairs = [(i, i + by) for i in range(peers) if 0 <= i + by < peers]
    return lax.ppermute(array, axis, pairs)


def mix_kernel(tok_ref, comp_ref, start_ref, end_ref, embed_ref, inv_ref, gain_ref, taps_ref,
               out_ref, tab, ext_f, ext_r, taps_v, res):
    vocab, width = embed_ref.shape
    count = out_ref.shape[0]
    span = taps_ref.shape[0]
    blocks = count // SUB
    for s in range(SUB):
        cols = slice(s * LANES, (s + 1) * LANES)
        rows = embed_ref[:, cols].astype(jnp.float32) * inv_ref[...] * gain_ref[:, cols]
        tab[pl.ds(s, vocab, stride=SUB), :] = rows.astype(jnp.bfloat16).astype(jnp.float32)
        taps_v[pl.ds(s, span, stride=SUB), :] = taps_ref[:, cols]
    taps_v[pl.ds(span * SUB, SUB * SUB), :] = jnp.zeros((SUB * SUB, LANES), jnp.float32)

    def row_of(ref, k):
        return ref[pl.ds(pl.multiple_of(k * SUB, SUB), SUB), :]

    def put(ref, k, v):
        ref[pl.ds(pl.multiple_of(k * SUB, SUB), SUB), :] = v

    def fill(k8, carry):
        for u in range(SUB):
            k = k8 * SUB + u
            put(ext_f, k, row_of(tab, tok_ref[k]))
            put(ext_r, k, row_of(tab, comp_ref[tok_ref[count + k]]))
        return carry

    lax.fori_loop(0, 2 * count // SUB, fill, 0)

    def tree(terms):
        while len(terms) > 1:
            terms = [a + b for a, b in zip(terms[::2], terms[1::2])] + (
                [terms[-1]] if len(terms) % 2 else []
            )
        return terms[0]

    zero = jnp.zeros((SUB, LANES), jnp.float32)

    def block(i, carry):
        p0 = i * SUB
        s0 = start_ref[p0]
        e0 = end_ref[p0 + SUB - 1]

        def fwd_far(j, acc):
            q0 = j * SUB
            lag = (i - j) * SUB
            rows = [jnp.where(q0 + c >= s0, row_of(ext_f, count + q0 + c), zero) for c in range(SUB)]
            tap = {d: row_of(taps_v, lag + d) for d in range(1 - SUB, SUB)}
            return tuple(
                acc[r] + tree([tap[r - c] * rows[c] for c in range(SUB)]) for r in range(SUB)
            )

        low = jnp.maximum(lax.div(s0 + count, SUB) - blocks, i - span // SUB)
        far_f = lax.fori_loop(low, i, fwd_far, (zero,) * SUB)

        def rev_far(j, acc):
            q0 = j * SUB
            lag = (j - i) * SUB
            rows = [jnp.where(q0 + c < e0, row_of(ext_r, q0 + c), zero) for c in range(SUB)]
            tap = {d: row_of(taps_v, lag + d) for d in range(1 - SUB, SUB)}
            return tuple(
                acc[r] + tree([tap[c - r] * rows[c] for c in range(SUB)]) for r in range(SUB)
            )

        high = jnp.minimum(lax.div(e0 - 1, SUB), i + span // SUB)
        far_r = lax.fori_loop(i + 1, high + 1, rev_far, (zero,) * SUB)

        rows_f = [row_of(ext_f, count + p0 + c) for c in range(SUB)]
        rows_r = [row_of(ext_r, p0 + c) for c in range(SUB)]
        tap = [row_of(taps_v, d) for d in range(SUB)]
        for r in range(SUB):
            start = start_ref[p0 + r]
            end = end_ref[p0 + r]
            terms = [tap[0] * rows_f[r], jnp.where(start < p0, far_f[r], zero)]
            terms += [jnp.where(start <= p0 + c, tap[r - c] * rows_f[c], zero) for c in range(r)]
            gated_f = (rows_f[r] * tree(terms)).astype(jnp.bfloat16).astype(jnp.float32)
            terms = [tap[0] * rows_r[r], jnp.where(end > p0 + SUB, far_r[r], zero)]
            terms += [
                jnp.where(end > p0 + c, tap[c - r] * rows_r[c], zero) for c in range(r + 1, SUB)
            ]
            gated_r = (rows_r[r] * tree(terms)).astype(jnp.bfloat16).astype(jnp.float32)
            put(res, p0 + r, (gated_f + gated_r) * 0.5)
        return carry

    lax.fori_loop(0, blocks, block, 0)
    for s in range(SUB):
        out_ref[:, s * LANES : (s + 1) * LANES] = res[pl.ds(s, count, stride=SUB), :].astype(
            jnp.bfloat16
        )


def mix_strands(tok_ext, complement, starts, ends, embed, inv, gain, taps):
    vocab, width = embed.shape
    count = starts.shape[0]
    span = taps.shape[0]
    smem = pl.BlockSpec(memory_space=pltpu.SMEM)
    vmem = pl.BlockSpec(memory_space=pltpu.VMEM)
    return pl.pallas_call(
        mix_kernel,
        out_shape=jax.ShapeDtypeStruct((count, width), jnp.bfloat16),
        in_specs=[smem] * 4 + [vmem] * 4,
        out_specs=vmem,
        scratch_shapes=[
            pltpu.VMEM((vocab * SUB, LANES), jnp.float32),
            pltpu.VMEM((2 * count * SUB, LANES), jnp.float32),
            pltpu.VMEM((2 * count * SUB, LANES), jnp.float32),
            pltpu.VMEM(((span + SUB) * SUB, LANES), jnp.float32),
            pltpu.VMEM((count * SUB, LANES), jnp.float32),
        ],
        compiler_params=pltpu.CompilerParams(vmem_limit_bytes=32 << 20),
        cost_estimate=pl.CostEstimate(flops=2 * 2 * count * span * width, bytes_accessed=4 << 20, transcendentals=0),
    )(tok_ext, complement, starts, ends, embed, inv, gain, taps)


def body(tokens, complement, seg_lengths, owner, embed, norm_gain, taps, w_out):
    row_count = tokens.shape[0]
    vocab_size, width = embed.shape
    ctx_count = lax.axis_size("ctx")
    ch_count = lax.axis_size("ch")
    place = lax.axis_index("ctx")
    full_width = width * ch_count
    seg_count = seg_lengths.shape[0]
    block_total = owner.shape[0]
    per_block = seg_count // block_total
    near = 4
    far = ctx_count // near
    near_groups = [[near * m + y for y in range(near)] for m in range(far)]
    far_groups = [[near * m + y for m in range(far)] for y in range(near)]
    out_cols = w_out.shape[1]

    w_rows = lax.all_gather(
        w_out.T, "ctx", axis=0, tiled=True, axis_index_groups=far_groups
    )

    power = lax.psum(jnp.sum(jnp.square(embed.astype(jnp.float32)), axis=1), "ch")
    inv = lax.rsqrt(power / full_width + norm_eps)[:, None]

    seg_ids = jnp.arange(seg_count, dtype=jnp.int32)
    seg_ends = jnp.sum(
        jnp.where(seg_ids[None, :] <= seg_ids[:, None], seg_lengths[None, :], 0), axis=1
    )
    seg_starts = seg_ends - seg_lengths
    own_pos = place * row_count + jnp.arange(row_count, dtype=jnp.int32)
    inside = (seg_starts[None, :] <= own_pos[:, None]) & (own_pos[:, None] < seg_ends[None, :])
    first_pos = jnp.sum(jnp.where(inside, seg_starts[None, :], 0), axis=1)
    end_pos = jnp.sum(jnp.where(inside, seg_ends[None, :], 0), axis=1)
    base = place * row_count
    starts = jnp.maximum(first_pos - base, -row_count)
    ends = jnp.minimum(end_pos - base, 2 * row_count)

    tok_ext = jnp.concatenate(
        [passed_along(tokens, "ctx", 1), tokens, passed_along(tokens, "ctx", -1)]
    )
    strand_mean = mix_strands(
        tok_ext, complement, starts, ends, embed, inv, norm_gain[None, :], taps
    )
    rows = lax.all_gather(
        strand_mean, "ctx", axis=0, tiled=True, axis_index_groups=near_groups
    )
    terms = lax.dot_general(
        rows, w_rows, (((1,), (1,)), ((), ())), preferred_element_type=jnp.float32
    )
    col_share = lax.psum_scatter(terms, "ch", scatter_dimension=1, tiled=True)
    active = jax.nn.softplus(col_share)

    slots = jnp.arange(seg_count, dtype=jnp.int32)
    block_ids = jnp.arange(block_total, dtype=jnp.int32)
    holder = jnp.sum(
        jnp.where(owner[None, :] == (slots // per_block)[:, None], block_ids[None, :], 0), axis=1
    )
    seg_at = holder * per_block + slots % per_block
    same_seg = seg_at[:, None] == slots[None, :]
    slot_start = jnp.sum(jnp.where(same_seg, seg_starts[None, :], 0), axis=1)
    slot_end = jnp.sum(jnp.where(same_seg, seg_ends[None, :], 0), axis=1)
    group_pos = (place // near) * (near * row_count) + jnp.arange(near * row_count, dtype=jnp.int32)
    member = (
        (slot_start[:, None] <= group_pos[None, :]) & (group_pos[None, :] < slot_end[:, None])
    ).astype(jnp.float32)
    partial_sums = jnp.dot(member, active, precision=lax.Precision.HIGHEST)
    share = partial_sums.shape[1]
    received = lax.all_to_all(
        partial_sums.reshape(ctx_count, per_block, share),
        "ctx",
        split_axis=0,
        concat_axis=0,
        tiled=True,
    )
    sums = jnp.sum(received.reshape(far, near, per_block, share), axis=0)
    sums = sums.reshape(near, per_block, far // ch_count, out_cols)
    totals = sums.transpose(1, 2, 0, 3).reshape(per_block, width)
    own_lengths = lax.dynamic_slice_in_dim(slot_end - slot_start, place * per_block, per_block)
    return totals / own_lengths.astype(jnp.float32)[:, None]


def solution(mesh):
    in_specs = (P("ctx"), P(), P(), P(), P(None, "ch"), P("ch"), P(None, "ch"), P("ch", "ctx"))
    out_specs = P("ctx", "ch")
    return jax.shard_map(body, mesh=mesh, in_specs=in_specs, out_specs=out_specs, check_vma=False)
```

```python
import jax
import jax.numpy as jnp
from jax import lax
from jax.experimental import pallas as pl
from jax.experimental.pallas import tpu as pltpu
from jax.sharding import PartitionSpec as P

norm_eps = 1e-06
LANES = 128
SUB = 8
MESH = pl.DeviceIdType.MESH


def passed_along(array, axis, by):
    peers = lax.axis_size(axis)
    pairs = [(i, i + by) for i in range(peers) if 0 <= i + by < peers]
    return lax.ppermute(array, axis, pairs)


def mix_kernel(tok_ref, comp_ref, start_ref, end_ref, embed_ref, inv_ref, gain_ref, taps_ref,
               out_ref, tab, ext_f, ext_r, taps_v, res):
    vocab, width = embed_ref.shape
    count = out_ref.shape[0]
    span = taps_ref.shape[0]
    blocks = count // SUB
    for s in range(SUB):
        cols = slice(s * LANES, (s + 1) * LANES)
        rows = embed_ref[:, cols].astype(jnp.float32) * inv_ref[...] * gain_ref[:, cols]
        tab[pl.ds(s, vocab, stride=SUB), :] = rows.astype(jnp.bfloat16).astype(jnp.float32)
        taps_v[pl.ds(s, span, stride=SUB), :] = taps_ref[:, cols]
    taps_v[pl.ds(span * SUB, SUB * SUB), :] = jnp.zeros((SUB * SUB, LANES), jnp.float32)

    def row_of(ref, k):
        return ref[pl.ds(pl.multiple_of(k * SUB, SUB), SUB), :]

    def put(ref, k, v):
        ref[pl.ds(pl.multiple_of(k * SUB, SUB), SUB), :] = v

    def fill(k8, carry):
        for u in range(SUB):
            k = k8 * SUB + u
            put(ext_f, k, row_of(tab, tok_ref[k]))
            put(ext_r, k, row_of(tab, comp_ref[tok_ref[count + k]]))
        return carry

    lax.fori_loop(0, 2 * count // SUB, fill, 0)

    def tree(terms):
        while len(terms) > 1:
            terms = [a + b for a, b in zip(terms[::2], terms[1::2])] + (
                [terms[-1]] if len(terms) % 2 else []
            )
        return terms[0]

    zero = jnp.zeros((SUB, LANES), jnp.float32)

    def block(i, carry):
        p0 = i * SUB
        s0 = start_ref[p0]
        e0 = end_ref[p0 + SUB - 1]

        def fwd_far(j, acc):
            q0 = j * SUB
            lag = (i - j) * SUB
            rows = [jnp.where(q0 + c >= s0, row_of(ext_f, count + q0 + c), zero) for c in range(SUB)]
            tap = {d: row_of(taps_v, lag + d) for d in range(1 - SUB, SUB)}
            return tuple(
                acc[r] + tree([tap[r - c] * rows[c] for c in range(SUB)]) for r in range(SUB)
            )

        low = jnp.maximum(lax.div(s0 + count, SUB) - blocks, i - span // SUB)
        far_f = lax.fori_loop(low, i, fwd_far, (zero,) * SUB)

        def rev_far(j, acc):
            q0 = j * SUB
            lag = (j - i) * SUB
            rows = [jnp.where(q0 + c < e0, row_of(ext_r, q0 + c), zero) for c in range(SUB)]
            tap = {d: row_of(taps_v, lag + d) for d in range(1 - SUB, SUB)}
            return tuple(
                acc[r] + tree([tap[c - r] * rows[c] for c in range(SUB)]) for r in range(SUB)
            )

        high = jnp.minimum(lax.div(e0 - 1, SUB), i + span // SUB)
        far_r = lax.fori_loop(i + 1, high + 1, rev_far, (zero,) * SUB)

        rows_f = [row_of(ext_f, count + p0 + c) for c in range(SUB)]
        rows_r = [row_of(ext_r, p0 + c) for c in range(SUB)]
        tap = [row_of(taps_v, d) for d in range(SUB)]
        for r in range(SUB):
            start = start_ref[p0 + r]
            end = end_ref[p0 + r]
            terms = [tap[0] * rows_f[r], jnp.where(start < p0, far_f[r], zero)]
            terms += [jnp.where(start <= p0 + c, tap[r - c] * rows_f[c], zero) for c in range(r)]
            gated_f = (rows_f[r] * tree(terms)).astype(jnp.bfloat16).astype(jnp.float32)
            terms = [tap[0] * rows_r[r], jnp.where(end > p0 + SUB, far_r[r], zero)]
            terms += [
                jnp.where(end > p0 + c, tap[c - r] * rows_r[c], zero) for c in range(r + 1, SUB)
            ]
            gated_r = (rows_r[r] * tree(terms)).astype(jnp.bfloat16).astype(jnp.float32)
            put(res, p0 + r, (gated_f + gated_r) * 0.5)
        return carry

    lax.fori_loop(0, blocks, block, 0)
    for s in range(SUB):
        out_ref[:, s * LANES : (s + 1) * LANES] = res[pl.ds(s, count, stride=SUB), :].astype(
            jnp.bfloat16
        )


def mix_strands(tok_ext, complement, starts, ends, embed, inv, gain, taps):
    vocab, width = embed.shape
    count = starts.shape[0]
    span = taps.shape[0]
    smem = pl.BlockSpec(memory_space=pltpu.SMEM)
    vmem = pl.BlockSpec(memory_space=pltpu.VMEM)
    return pl.pallas_call(
        mix_kernel,
        out_shape=jax.ShapeDtypeStruct((count, width), jnp.bfloat16),
        in_specs=[smem] * 4 + [vmem] * 4,
        out_specs=vmem,
        scratch_shapes=[
            pltpu.VMEM((vocab * SUB, LANES), jnp.float32),
            pltpu.VMEM((2 * count * SUB, LANES), jnp.float32),
            pltpu.VMEM((2 * count * SUB, LANES), jnp.float32),
            pltpu.VMEM(((span + SUB) * SUB, LANES), jnp.float32),
            pltpu.VMEM((count * SUB, LANES), jnp.float32),
        ],
        compiler_params=pltpu.CompilerParams(vmem_limit_bytes=32 << 20),
        cost_estimate=pl.CostEstimate(flops=2 * 2 * count * span * width, bytes_accessed=4 << 20, transcendentals=0),
    )(tok_ext, complement, starts, ends, embed, inv, gain, taps)


def exchange_kernel(s_ref, w_ref, member_ref, out_ref,
                    sbuf, wbuf, out1, in1, zout, zin, pbuf, rbuf,
                    w_send, w_recv, s_send, s_recv, r_send, r_recv, a_send, a_recv):
    me = lax.axis_index("ctx")
    ch = lax.axis_index("ch")
    peers = lax.axis_size("ctx")
    y = lax.rem(me, 4)
    zh = lax.rem(lax.div(me, 4), 4)
    x = lax.div(me, 16)
    zl = lax.div(ch, 2)
    core = lax.rem(ch, 2)

    def ring(v, by):
        return lax.rem(v + by, 4)

    xp, xm, x2 = ring(x, 1), ring(x, 3), ring(x, 2)
    zp, zm, z2 = ring(zh, 1), ring(zh, 3), ring(zh, 2)
    yp, ym, y2 = ring(y, 1), ring(y, 3), ring(y, 2)
    core_peer = zl * 2 + 1 - core
    z_peer = (1 - zl) * 2 + core

    barrier = pltpu.get_barrier_semaphore()

    def hello(d, carry):
        pl.semaphore_signal(
            barrier, inc=1, device_id={"ctx": lax.rem(me + d, peers)}, device_id_type=MESH
        )
        return carry

    lax.fori_loop(1, peers, hello, 0)
    for other in (core_peer, z_peer):
        pl.semaphore_signal(barrier, inc=1, device_id={"ch": other}, device_id_type=MESH)
    pl.semaphore_wait(barrier, peers + 1)

    cols = w_ref.shape[0]
    half = cols // 2
    rows = s_ref.shape[0]
    parts = 4
    chunk = rows // parts

    def at_ctx(cx, cz, cy):
        return {"ctx": cx * 16 + cz * 4 + cy}

    def w_rows(cx, cz, lo=0, count=cols):
        return wbuf.at[pl.ds(pl.multiple_of((cx * 4 + cz) * cols + lo, half), count), :]

    def w_copy(label, src, dst, to):
        return pltpu.make_async_remote_copy(
            src_ref=src, dst_ref=dst, send_sem=w_send.at[label], recv_sem=w_recv.at[label],
            device_id=to, device_id_type=MESH,
        )

    z_of = (zh, zm, zp, z2)
    plus, minus = at_ctx(xp, zh, y), at_ctx(xm, zh, y)
    up, down = at_ctx(x, zp, y), at_ctx(x, zm, y)
    own = w_rows(x, zh)
    sent = {
        0: (w_ref, own, up),
        1: (w_ref, own, down),
        2: (w_rows(x, zm, 0, half), w_rows(x, zm, 0, half), up),
        3: (w_rows(x, zp, half, half), w_rows(x, zp, half, half), down),
    }
    got = {
        0: w_rows(x, zm),
        1: w_rows(x, zp),
        2: w_rows(x, z2, 0, half),
        3: w_rows(x, z2, half, half),
    }
    for dz in range(4):
        base = 4 + 3 * dz
        here = w_rows(x, z_of[dz])
        src = w_ref if dz == 0 else here
        sent[base] = (src, here, plus)
        sent[base + 1] = (src, here, minus)
        relay = w_rows(xm if dz < 2 else xp, z_of[dz])
        sent[base + 2] = (relay, relay, plus if dz < 2 else minus)
        got[base] = w_rows(xm, z_of[dz])
        got[base + 1] = w_rows(xp, z_of[dz])
        got[base + 2] = w_rows(x2, z_of[dz])

    def w_start(*labels):
        for n in labels:
            w_copy(n, *sent[n]).start()

    def w_wait(*labels):
        for n in labels:
            w_copy(n, got[n], got[n], plus).wait_recv()

    def s_rows(cy, k):
        return sbuf.at[pl.ds(pl.multiple_of(cy * rows + k * chunk, chunk), chunk), :]

    s_plus, s_minus = at_ctx(x, zh, yp), at_ctx(x, zh, ym)

    def s_copy(k, kind, src, dst, to):
        return pltpu.make_async_remote_copy(
            src_ref=src, dst_ref=dst, send_sem=s_send.at[3 * k + kind],
            recv_sem=s_recv.at[3 * k + kind], device_id=to, device_id_type=MESH,
        )

    def s_sent(k, kind):
        if kind < 2:
            return s_copy(
                k, kind, s_ref.at[pl.ds(k * chunk, chunk), :], s_rows(y, k),
                s_plus if kind == 0 else s_minus,
            )
        relay = s_rows(ym if k % 2 == 0 else yp, k)
        return s_copy(k, kind, relay, relay, s_plus if k % 2 == 0 else s_minus)

    def s_wait(k, kind):
        there = s_rows((ym, yp, y2)[kind], k)
        s_copy(k, kind, there, there, s_plus).wait_recv()

    w_start(0, 1, 4, 5)
    for k in range(parts):
        s_sent(k, 0).start()
        s_sent(k, 1).start()
    wbuf[pl.ds(pl.multiple_of((x * 4 + zh) * cols, cols), cols), :] = w_ref[...]
    sbuf[pl.ds(pl.multiple_of(y * rows, rows), rows), :] = s_ref[...]
    w_wait(0)
    w_start(2, 7, 8)
    w_wait(1)
    w_start(3, 10, 11)
    w_wait(4)
    w_start(6)
    for k in range(parts):
        s_wait(k, k % 2)
        s_sent(k, 2).start()
    w_wait(2, 3)
    w_start(13, 14)
    w_wait(7)
    w_start(9)
    w_wait(11)
    w_start(12)
    w_wait(14)
    w_start(15)
    for k in range(parts):
        s_wait(k, 1 - k % 2)
        s_wait(k, 2)
    w_wait(5, 6, 8, 9, 10, 12, 13, 15)

    group = 4 * cols
    total = parts * rows
    tile = rows

    def product(g, t):
        lhs = sbuf[pl.ds(pl.multiple_of(t * tile, tile), tile), :]
        rhs = wbuf[pl.ds(pl.multiple_of(g * group, group), group), :]
        return lax.dot_general(
            lhs, rhs, (((1,), (1,)), ((), ())), preferred_element_type=jnp.float32
        )

    def tile_of(ref, *lead, t):
        return ref.at[(*lead, pl.ds(pl.multiple_of(t * tile, tile), tile), slice(None))]

    def core_copy(slot):
        return pltpu.make_async_remote_copy(
            src_ref=out1.at[slot], dst_ref=in1.at[slot], send_sem=r_send.at[slot],
            recv_sem=r_recv.at[slot], device_id={"ch": core_peer}, device_id_type=MESH,
        )

    z_copy = pltpu.make_async_remote_copy(
        src_ref=zout, dst_ref=zin, send_sem=r_send.at[2], recv_sem=r_recv.at[2],
        device_id={"ch": z_peer}, device_id_type=MESH,
    )
    for slot, g in ((0, 2 * (1 - zl) + 1 - core), (1, 2 * zl + 1 - core)):
        def give(t, carry, slot=slot, g=g):
            tile_of(out1, slot, t=t)[...] = product(g, t)
            return carry

        lax.fori_loop(0, total // tile, give, 0)
        core_copy(slot).start()
    core_copy(0).wait_recv()

    def pass_on(t, carry):
        summed = product(2 * (1 - zl) + core, t) + tile_of(in1, 0, t=t)[...]
        tile_of(zout, t=t)[...] = summed.astype(jnp.bfloat16)
        return carry

    lax.fori_loop(0, total // tile, pass_on, 0)
    z_copy.start()
    core_copy(1).wait_recv()

    def keep(t, carry):
        ref = tile_of(in1, 1, t=t)
        ref[...] = product(2 * zl + core, t) + ref[...]
        return carry

    lax.fori_loop(0, total // tile, keep, 0)
    z_copy.wait_recv()

    def sum_up(t, acc):
        scores = tile_of(in1, 1, t=t)[...] + tile_of(zin, t=t)[...].astype(jnp.float32)
        active = jnp.maximum(scores, 0.0) + jnp.log1p(jnp.exp(-jnp.abs(scores)))
        high = active.astype(jnp.bfloat16)
        low = (active - high.astype(jnp.float32)).astype(jnp.bfloat16)
        picks = member_ref[t]
        return (
            acc
            + jnp.dot(picks, high, preferred_element_type=jnp.float32)
            + jnp.dot(picks, low, preferred_element_type=jnp.float32)
        )

    slots = member_ref.shape[1]
    sums = lax.fori_loop(0, total // tile, sum_up, jnp.zeros((slots, group), jnp.float32))
    wide = group // LANES
    for h in range(wide):
        pbuf[pl.ds(h, slots, stride=wide), :] = sums[:, h * LANES : (h + 1) * LANES]

    def to_owner(d, carry):
        dest = lax.rem(me + d, peers)
        pltpu.make_async_remote_copy(
            src_ref=pbuf.at[pl.ds(pl.multiple_of(dest * SUB, SUB), SUB), :],
            dst_ref=rbuf.at[pl.ds(pl.multiple_of(me * SUB, SUB), SUB), :],
            send_sem=a_send, recv_sem=a_recv, device_id={"ctx": dest}, device_id_type=MESH,
        ).start()
        return carry

    lax.fori_loop(1, peers, to_owner, 0)
    mine = pl.ds(pl.multiple_of(me * SUB, SUB), SUB)
    rbuf[mine, :] = pbuf[mine, :]
    most = pl.ds(0, (peers - 1) * SUB)
    all_of = pltpu.make_async_remote_copy(
        src_ref=pbuf.at[most, :], dst_ref=rbuf.at[most, :], send_sem=a_send, recv_sem=a_recv,
        device_id={"ctx": lax.rem(me + 1, peers)}, device_id_type=MESH,
    )
    all_of.wait_recv()
    for q in range(4):
        acc = rbuf[pl.ds(q * SUB, SUB), :]
        for m in range(1, peers // 4):
            acc = acc + rbuf[pl.ds((4 * m + q) * SUB, SUB), :]
        out_ref[pl.ds(q * SUB, SUB), :] = acc
    all_of.wait_send()
    for n in range(16):
        w_copy(n, *sent[n]).wait_send()
    for k in range(parts):
        for kind in range(3):
            s_sent(k, kind).wait_send()
    core_copy(0).wait_send()
    core_copy(1).wait_send()
    z_copy.wait_send()


def exchange(strand_mean, w_rows, member):
    rows, width = strand_mean.shape
    cols = w_rows.shape[0]
    vmem = pl.BlockSpec(memory_space=pltpu.VMEM)
    total, group = 4 * rows, 4 * cols
    return pl.pallas_call(
        exchange_kernel,
        out_shape=jax.ShapeDtypeStruct((4 * SUB, LANES), jnp.float32),
        in_specs=[vmem] * 3,
        out_specs=vmem,
        scratch_shapes=[
            pltpu.VMEM((total, width), jnp.bfloat16),
            pltpu.VMEM((16 * cols, width), jnp.bfloat16),
            pltpu.VMEM((2, total, group), jnp.float32),
            pltpu.VMEM((2, total, group), jnp.float32),
            pltpu.VMEM((total, group), jnp.bfloat16),
            pltpu.VMEM((total, group), jnp.bfloat16),
            pltpu.VMEM((64 * SUB, LANES), jnp.float32),
            pltpu.VMEM((64 * SUB, LANES), jnp.float32),
            pltpu.SemaphoreType.DMA((16,)),
            pltpu.SemaphoreType.DMA((16,)),
            pltpu.SemaphoreType.DMA((12,)),
            pltpu.SemaphoreType.DMA((12,)),
            pltpu.SemaphoreType.DMA((3,)),
            pltpu.SemaphoreType.DMA((3,)),
            pltpu.SemaphoreType.DMA,
            pltpu.SemaphoreType.DMA,
        ],
        compiler_params=pltpu.CompilerParams(
            vmem_limit_bytes=48 << 20, collective_id=0, has_side_effects=True
        ),
    )(strand_mean, w_rows, member)


def body(tokens, complement, seg_lengths, owner, embed, norm_gain, taps, w_out):
    row_count = tokens.shape[0]
    vocab_size, width = embed.shape
    ch_count = lax.axis_size("ch")
    place = lax.axis_index("ctx")
    full_width = width * ch_count
    seg_count = seg_lengths.shape[0]
    block_total = owner.shape[0]
    per_block = seg_count // block_total
    near = 4
    out_cols = w_out.shape[1]

    power = lax.psum(jnp.sum(jnp.square(embed.astype(jnp.float32)), axis=1), "ch")
    inv = lax.rsqrt(power / full_width + norm_eps)[:, None]

    seg_ids = jnp.arange(seg_count, dtype=jnp.int32)
    seg_ends = jnp.sum(
        jnp.where(seg_ids[None, :] <= seg_ids[:, None], seg_lengths[None, :], 0), axis=1
    )
    seg_starts = seg_ends - seg_lengths
    own_pos = place * row_count + jnp.arange(row_count, dtype=jnp.int32)
    inside = (seg_starts[None, :] <= own_pos[:, None]) & (own_pos[:, None] < seg_ends[None, :])
    first_pos = jnp.sum(jnp.where(inside, seg_starts[None, :], 0), axis=1)
    end_pos = jnp.sum(jnp.where(inside, seg_ends[None, :], 0), axis=1)
    base = place * row_count
    starts = jnp.maximum(first_pos - base, -row_count)
    ends = jnp.minimum(end_pos - base, 2 * row_count)

    tok_ext = jnp.concatenate(
        [passed_along(tokens, "ctx", 1), tokens, passed_along(tokens, "ctx", -1)]
    )
    strand_mean = mix_strands(
        tok_ext, complement, starts, ends, embed, inv, norm_gain[None, :], taps
    )
    slots = jnp.arange(seg_count, dtype=jnp.int32)
    block_ids = jnp.arange(block_total, dtype=jnp.int32)
    holder = jnp.sum(
        jnp.where(owner[None, :] == (slots // per_block)[:, None], block_ids[None, :], 0), axis=1
    )
    seg_at = holder * per_block + slots % per_block
    same_seg = seg_at[:, None] == slots[None, :]
    slot_start = jnp.sum(jnp.where(same_seg, seg_starts[None, :], 0), axis=1)
    slot_end = jnp.sum(jnp.where(same_seg, seg_ends[None, :], 0), axis=1)
    group_pos = (place // near) * (near * row_count) + jnp.arange(near * row_count, dtype=jnp.int32)
    group_pos = group_pos.reshape(near, 1, row_count)
    member = (slot_start[None, :, None] <= group_pos) & (group_pos < slot_end[None, :, None])
    sums = exchange(strand_mean, w_out.T, member.astype(jnp.bfloat16))
    sums = sums.reshape(near, per_block, near, out_cols)
    totals = sums.transpose(1, 2, 0, 3).reshape(per_block, width)
    own_lengths = lax.dynamic_slice_in_dim(slot_end - slot_start, place * per_block, per_block)
    return totals / own_lengths.astype(jnp.float32)[:, None]


def solution(mesh):
    in_specs = (P("ctx"), P(), P(), P(), P(None, "ch"), P("ch"), P(None, "ch"), P("ch", "ctx"))
    out_specs = P("ctx", "ch")
    return jax.shard_map(body, mesh=mesh, in_specs=in_specs, out_specs=out_specs, check_vma=False)
```

```python
import jax
import jax.numpy as jnp
from jax import lax
from jax.experimental import pallas as pl
from jax.experimental.pallas import tpu as pltpu
from jax.sharding import PartitionSpec as P

norm_eps = 1e-06
LANES = 128
SUB = 8
PAD = 8
SPAN = 128
TAPROWS = 152
BASE = 143
MESH = pl.DeviceIdType.MESH
f32 = jnp.float32
bf16 = jnp.bfloat16


def rows3(ref, k, n):
    return ref[pl.ds(pl.multiple_of(k * SUB, SUB), n * SUB), :].reshape(n, SUB, LANES)

def put3(ref, k, v):
    n = v.shape[0]
    ref[pl.ds(pl.multiple_of(k * SUB, SUB), n * SUB), :] = v.reshape(n * SUB, LANES)

def prep_taps(taps_ref, tv, dv, tr, dr):
    span = taps_ref.shape[0]
    edge = jnp.zeros((PAD * SUB, LANES), jnp.float32)
    tv[pl.ds(0, PAD * SUB), :] = edge
    for e in range(2):
        tv[pl.ds((PAD + span + 8 * e) * SUB, 8 * SUB), :] = edge
    for s in range(SUB):
        tv[pl.ds(PAD * SUB + s, span, stride=SUB), :] = taps_ref[:, s * LANES:(s + 1) * LANES]
    dv[pl.ds(0, PAD * SUB), :] = edge
    dv[pl.ds(PAD * SUB, (TAPROWS - PAD) * SUB), :] = (
        tv[pl.ds(0, (TAPROWS - PAD) * SUB), :] - tv[pl.ds(PAD * SUB, (TAPROWS - PAD) * SUB), :])
    def flip(k8, carry):
        for u in range(8):
            k = k8 * 8 + u
            put3(tr, TAPROWS - 1 - k, rows3(tv, k, 1))
            put3(dr, TAPROWS - 1 - k, rows3(dv, k, 1))
        return carry
    lax.fori_loop(0, TAPROWS // 8, flip, 0)

def conv_block(i, count, ext_f, ext_r, tv, dv, tr, dr, sv, ev, res):
    p0 = i * 16
    zero8 = jnp.zeros((8, SUB, LANES), jnp.float32)
    idx16 = lax.broadcasted_iota(jnp.int32, (16, SUB, LANES), 0)
    far_lags = SPAN // 16
    s0 = rows3(sv, p0, 1)
    e0 = rows3(ev, p0 + 15, 1)

    def fwd_far(j, acc):
        lag = j * 16
        q0 = p0 - lag
        rows = jnp.where(idx16 >= s0 - q0, rows3(ext_f, count + q0, 16), 0.0)
        x0, x1 = rows[:8], rows[8:]
        xs = x0 + x1
        a, b, c = acc
        for u in range(8):
            a = a + rows3(tv, PAD + lag - u, 8) * xs[u:u + 1]
            b = b + rows3(dv, PAD + lag - u, 8) * x1[u:u + 1]
            c = c + rows3(dv, PAD + 8 + lag - u, 8) * x0[u:u + 1]
        return a, b, c

    def rev_far(j, acc):
        lag = j * 16
        q0 = p0 + lag
        rows = jnp.where(idx16 < e0 - q0, rows3(ext_r, q0, 16), 0.0)
        x0, x1 = rows[:8], rows[8:]
        xs = x0 + x1
        a, b, c = acc
        for u in range(8):
            a = a + rows3(tr, BASE - lag - u, 8) * xs[u:u + 1]
            b = b + rows3(dr, BASE - lag - u, 8) * x0[u:u + 1]
            c = c + rows3(dr, BASE - 8 - lag - u, 8) * x1[u:u + 1]
        return a, b, c

    a, b, c = lax.fori_loop(1, far_lags + 1, fwd_far, (zero8,) * 3, unroll=2)
    far_f = (a + b, a - c)
    a, b, c = lax.fori_loop(1, far_lags + 1, rev_far, (zero8,) * 3, unroll=2)
    far_r = (a - c, a + b)
    xf = (rows3(ext_f, count + p0, 8), rows3(ext_f, count + p0 + 8, 8))
    xr = (rows3(ext_r, p0, 8), rows3(ext_r, p0 + 8, 8))
    idx8 = lax.broadcasted_iota(jnp.int32, (8, SUB, LANES), 0)
    mid = rows3(sv, p0 + 8, 1)
    m = jnp.where(idx8 >= mid - p0, xf[0], 0.0)
    mid_f = zero8
    for u in range(8):
        mid_f = mid_f + rows3(tv, PAD + 8 - u, 8) * m[u:u + 1]
    mid = rows3(ev, p0 + 7, 1)
    m = jnp.where(idx8 < mid - p0 - 8, xr[1], 0.0)
    mid_r = zero8
    for u in range(8):
        mid_r = mid_r + rows3(tr, BASE - 8 - u, 8) * m[u:u + 1]
    for h in range(2):
        pb = p0 + 8 * h
        start = rows3(sv, pb, 8)
        end = rows3(ev, pb, 8)
        mix_f = jnp.where(start < p0, far_f[h], 0.0)
        mix_r = jnp.where(end > p0 + 16, far_r[h], 0.0)
        if h == 1:
            mix_f = mix_f + jnp.where(start < pb, mid_f, 0.0)
        else:
            mix_r = mix_r + jnp.where(end > pb + 8, mid_r, 0.0)
        for u in range(8):
            mix_f = mix_f + jnp.where(start <= pb + u, rows3(tv, PAD - u, 8) * xf[h][u:u + 1], 0.0)
            mix_r = mix_r + jnp.where(end > pb + u, rows3(tr, BASE - u, 8) * xr[h][u:u + 1], 0.0)
        gated_f = (xf[h] * mix_f).astype(jnp.bfloat16).astype(jnp.float32)
        gated_r = (xr[h] * mix_r).astype(jnp.bfloat16).astype(jnp.float32)
        put3(res, pb, (gated_f + gated_r) * 0.5)


def score_kernel(tok_ref, comp_ref, lens_ref, owner_ref, embed_ref, gain_ref, taps_ref, w_ref,
                 out_ref, sbuf, wbuf, out1, in1, zout, zin, pbuf, rbuf, member, scale,
                 tk, pw, ext_f, ext_r, tv, dv, tr, dr, sv, ev, res,
                 w_send, w_recv, s_send, s_recv, r_send, r_recv, a_send, a_recv,
                 t_send, t_recv, p_send, p_recv):
    me = lax.axis_index("ctx")
    ch = lax.axis_index("ch")
    peers = lax.axis_size("ctx")
    y = lax.rem(me, 4)
    zh = lax.rem(lax.div(me, 4), 4)
    x = lax.div(me, 16)
    zl = lax.div(ch, 2)
    core = lax.rem(ch, 2)

    def ring(v, by):
        return lax.rem(v + by, 4)

    xp, xm, x2 = ring(x, 1), ring(x, 3), ring(x, 2)
    zp, zm, z2 = ring(zh, 1), ring(zh, 3), ring(zh, 2)
    yp, ym, y2 = ring(y, 1), ring(y, 3), ring(y, 2)
    core_peer = zl * 2 + 1 - core
    z_peer = (1 - zl) * 2 + core

    barrier = pltpu.get_barrier_semaphore()

    def hello(d, carry):
        pl.semaphore_signal(
            barrier, inc=1, device_id={"ctx": lax.rem(me + d, peers)}, device_id_type=MESH
        )
        return carry

    lax.fori_loop(1, peers, hello, 0)
    for d in range(1, 4):
        pl.semaphore_signal(
            barrier, inc=1, device_id={"ch": lax.rem(ch + d, 4)}, device_id_type=MESH
        )

    cols = w_ref.shape[0]
    half = cols // 2
    rows = sbuf.shape[0] // 4
    vocab, width = embed_ref.shape
    segs = lens_ref.shape[1]

    fold = jnp.zeros((vocab, LANES), f32)
    for s in range(SUB):
        piece = embed_ref[:, s * LANES : (s + 1) * LANES].astype(f32)
        fold = fold + piece * piece
    pw[ch] = jnp.broadcast_to(jnp.sum(fold.T, axis=0, keepdims=True), (SUB, vocab))
    tk[1] = jnp.broadcast_to(tok_ref[...], (SUB, rows))

    def iota(shape, dim):
        return lax.broadcasted_iota(jnp.int32, shape, dim)

    lens = jnp.broadcast_to(lens_ref[...], (SUB, segs)).astype(f32)
    upto = (iota((segs, segs), 0) <= iota((segs, segs), 1)).astype(bf16)
    ends_row = jnp.dot(lens.astype(bf16), upto, preferred_element_type=f32)
    starts_row = (ends_row - lens)[0:1]
    ends_row = ends_row[0:1]
    first = me * rows
    pos = (iota((rows, segs), 0) + first).astype(f32)
    start_col = jnp.max(jnp.where(starts_row <= pos, starts_row, 0.0), axis=1, keepdims=True)
    end_col = jnp.min(jnp.where(ends_row > pos, ends_row, 1e9), axis=1, keepdims=True)
    start_col = jnp.broadcast_to(start_col, (rows, LANES)).astype(jnp.int32) - first
    end_col = jnp.broadcast_to(end_col, (rows, LANES)).astype(jnp.int32) - first
    for s in range(SUB):
        sv[pl.ds(s, rows, stride=SUB), :] = start_col
        ev[pl.ds(s, rows, stride=SUB), :] = end_col

    blocks = owner_ref.shape[1]
    spread = ((iota((blocks, segs), 1) >> 2) == iota((blocks, segs), 0)).astype(bf16)
    owners = jnp.broadcast_to(owner_ref[...], (SUB, blocks)).astype(f32).astype(bf16)
    owner_row = jnp.dot(owners, spread, preferred_element_type=f32)[0:1].astype(jnp.int32)
    slot, seg = iota((segs, segs), 0), iota((segs, segs), 1)
    same = (owner_row == (slot >> 2)) & ((slot & 3) == (seg & 3))
    slot_start = jnp.sum(jnp.where(same, starts_row, 0.0), axis=1, keepdims=True)
    slot_end = jnp.sum(jnp.where(same, ends_row, 0.0), axis=1, keepdims=True)
    total = 4 * rows
    spot = (iota((segs, total), 1) + lax.div(me, 4) * total).astype(f32)
    member[...] = ((slot_start <= spot) & (spot < slot_end)).astype(f32).astype(bf16)
    scale[...] = jnp.broadcast_to(slot_end - slot_start, (segs, LANES))

    prep_taps(taps_ref, tv, dv, tr, dr)
    pl.semaphore_wait(barrier, peers + 2)
    parts = 4
    chunk = rows // parts

    def at_ctx(cx, cz, cy):
        return {"ctx": cx * 16 + cz * 4 + cy}

    def w_rows(cx, cz, lo=0, count=cols):
        return wbuf.at[pl.ds(pl.multiple_of((cx * 4 + cz) * cols + lo, half), count), :]

    def w_copy(label, src, dst, to):
        return pltpu.make_async_remote_copy(
            src_ref=src, dst_ref=dst, send_sem=w_send.at[label], recv_sem=w_recv.at[label],
            device_id=to, device_id_type=MESH,
        )

    z_of = (zh, zm, zp, z2)
    plus, minus = at_ctx(xp, zh, y), at_ctx(xm, zh, y)
    up, down = at_ctx(x, zp, y), at_ctx(x, zm, y)
    own = w_rows(x, zh)
    sent = {
        0: (w_ref, own, up),
        1: (w_ref, own, down),
        2: (w_rows(x, zm, 0, half), w_rows(x, zm, 0, half), up),
        3: (w_rows(x, zp, half, half), w_rows(x, zp, half, half), down),
    }
    got = {
        0: w_rows(x, zm),
        1: w_rows(x, zp),
        2: w_rows(x, z2, 0, half),
        3: w_rows(x, z2, half, half),
    }
    for dz in range(4):
        base = 4 + 3 * dz
        here = w_rows(x, z_of[dz])
        src = w_ref if dz == 0 else here
        sent[base] = (src, here, plus)
        sent[base + 1] = (src, here, minus)
        relay = w_rows(xm if dz < 2 else xp, z_of[dz])
        sent[base + 2] = (relay, relay, plus if dz < 2 else minus)
        got[base] = w_rows(xm, z_of[dz])
        got[base + 1] = w_rows(xp, z_of[dz])
        got[base + 2] = w_rows(x2, z_of[dz])

    def w_start(*labels):
        for n in labels:
            w_copy(n, *sent[n]).start()

    def w_wait(*labels):
        for n in labels:
            w_copy(n, got[n], got[n], plus).wait_recv()

    def s_rows(cy, k):
        return sbuf.at[pl.ds(pl.multiple_of(cy * rows + k * chunk, chunk), chunk), :]

    s_plus, s_minus = at_ctx(x, zh, yp), at_ctx(x, zh, ym)

    def s_copy(k, kind, src, dst, to):
        return pltpu.make_async_remote_copy(
            src_ref=src, dst_ref=dst, send_sem=s_send.at[3 * k + kind],
            recv_sem=s_recv.at[3 * k + kind], device_id=to, device_id_type=MESH,
        )

    def s_sent(k, kind):
        if kind < 2:
            return s_copy(
                k, kind, s_rows(y, k), s_rows(y, k),
                s_plus if kind == 0 else s_minus,
            )
        relay = s_rows(ym if k % 2 == 0 else yp, k)
        return s_copy(k, kind, relay, relay, s_plus if k % 2 == 0 else s_minus)

    def s_wait(k, kind):
        there = s_rows((ym, yp, y2)[kind], k)
        s_copy(k, kind, there, there, s_plus).wait_recv()

    def token_copy(slot, to):
        return pltpu.make_async_remote_copy(
            src_ref=tk.at[1], dst_ref=tk.at[slot], send_sem=t_send.at[slot // 2],
            recv_sem=t_recv.at[slot // 2], device_id={"ctx": to}, device_id_type=MESH,
        )

    def power_copy(d):
        return pltpu.make_async_remote_copy(
            src_ref=pw.at[ch], dst_ref=pw.at[ch], send_sem=p_send.at[d - 1],
            recv_sem=p_recv.at[d - 1], device_id={"ch": lax.rem(ch + d, 4)}, device_id_type=MESH,
        )

    def power_got(d):
        there = pw.at[lax.rem(ch + 4 - d, 4)]
        return pltpu.make_async_remote_copy(
            src_ref=there, dst_ref=there, send_sem=p_send.at[d - 1],
            recv_sem=p_recv.at[d - 1], device_id={"ch": lax.rem(ch + d, 4)}, device_id_type=MESH,
        )

    after, before = lax.rem(me + 1, peers), lax.rem(me + peers - 1, peers)
    for d in range(1, 4):
        power_copy(d).start()
    token_copy(0, after).start()
    token_copy(2, before).start()
    w_start(0, 1, 4, 5)
    wbuf[pl.ds(pl.multiple_of((x * 4 + zh) * cols, cols), cols), :] = w_ref[...]

    token_copy(0, after).wait_recv()
    token_copy(2, before).wait_recv()
    for d in range(1, 4):
        power_got(d).wait_recv()
    power = (pw[0] + pw[1]) + (pw[2] + pw[3])
    inv = lax.rsqrt(power / (4 * width) + norm_eps).T[:, 0:1]
    letters = iota((rows, vocab), 1)
    picks_f, picks_r = [], []
    for q in range(3):
        ids = tk[q].astype(f32).T[:, 0:1].astype(jnp.int32)
        hit = letters == ids
        if q < 2:
            picks_f.append(hit.astype(f32).astype(bf16))
        if q > 0:
            other = jnp.sum(
                jnp.where(hit, comp_ref[...].astype(f32), 0.0), axis=1, keepdims=True
            ).astype(jnp.int32)
            picks_r.append((letters == other).astype(f32).astype(bf16))
    for s in range(SUB):
        lanes = slice(s * LANES, (s + 1) * LANES)
        table = (embed_ref[:, lanes].astype(f32) * inv * gain_ref[:, lanes]).astype(bf16)
        for q in range(2):
            at = pl.ds(q * rows * SUB + s, rows, stride=SUB)
            ext_f[at, :] = jnp.dot(picks_f[q], table, preferred_element_type=f32)
            ext_r[at, :] = jnp.dot(picks_r[q], table, preferred_element_type=f32)

    w_wait(0)
    w_start(2, 7, 8)
    w_wait(1)
    w_start(3, 10, 11)
    w_wait(4)
    w_start(6)
    for k in range(parts):
        def two(i, carry, k=k):
            conv_block(2 * k + i, rows, ext_f, ext_r, tv, dv, tr, dr, sv, ev, res)
            return carry

        lax.fori_loop(0, chunk // 16, two, 0)
        at = pl.ds(pl.multiple_of(y * rows + k * chunk, chunk), chunk)
        for s in range(SUB):
            got_rows = res[pl.ds(k * chunk * SUB + s, chunk, stride=SUB), :]
            sbuf[at, s * LANES : (s + 1) * LANES] = got_rows.astype(bf16)
        s_sent(k, 0).start()
        s_sent(k, 1).start()
        if k == 0:
            w_wait(2, 3)
            w_start(13, 14)
        elif k == 1:
            w_wait(7)
            w_start(9)
        elif k == 2:
            w_wait(11)
            w_start(12)
        else:
            w_wait(14)
            w_start(15)
        if k > 0:
            s_wait(k - 1, (k - 1) % 2)
            s_sent(k - 1, 2).start()
    s_wait(parts - 1, (parts - 1) % 2)
    s_sent(parts - 1, 2).start()
    for k in range(parts):
        s_wait(k, 1 - k % 2)
        s_wait(k, 2)
    w_wait(5, 6, 8, 9, 10, 12, 13, 15)

    group = 4 * cols

    def product(g):
        rhs = wbuf[pl.ds(pl.multiple_of(g * group, group), group), :]
        return lax.dot_general(
            sbuf[...], rhs, (((1,), (1,)), ((), ())), preferred_element_type=f32
        )

    def core_copy(slot):
        return pltpu.make_async_remote_copy(
            src_ref=out1.at[slot], dst_ref=in1.at[slot], send_sem=r_send.at[slot],
            recv_sem=r_recv.at[slot], device_id={"ch": core_peer}, device_id_type=MESH,
        )

    z_copy = pltpu.make_async_remote_copy(
        src_ref=zout, dst_ref=zin, send_sem=r_send.at[2], recv_sem=r_recv.at[2],
        device_id={"ch": z_peer}, device_id_type=MESH,
    )
    out1[0] = product(2 * (1 - zl) + 1 - core)
    core_copy(0).start()
    out1[1] = product(2 * zl + 1 - core)
    core_copy(1).start()
    own_part = product(2 * (1 - zl) + core)
    core_copy(0).wait_recv()
    zout[...] = (own_part + in1[0]).astype(bf16)
    z_copy.start()
    own_part = product(2 * zl + core)
    core_copy(1).wait_recv()
    in1[1] = own_part + in1[1]
    z_copy.wait_recv()

    def sum_up(t, acc):
        at = pl.ds(pl.multiple_of(t * rows, rows), rows)
        scores = in1[1, at, :] + zin[at, :].astype(f32)
        active = jnp.maximum(scores, 0.0) + jnp.log1p(jnp.exp(-jnp.abs(scores)))
        high = active.astype(bf16)
        low = (active - high.astype(f32)).astype(bf16)
        picks = member[:, pl.ds(pl.multiple_of(t * rows, rows), rows)]
        return (
            acc
            + jnp.dot(picks, high, preferred_element_type=f32)
            + jnp.dot(picks, low, preferred_element_type=f32)
        )

    sums = lax.fori_loop(0, 4, sum_up, jnp.zeros((segs, group), f32))
    wide = group // LANES
    for h in range(wide):
        pbuf[pl.ds(h, segs, stride=wide), :] = sums[:, h * LANES : (h + 1) * LANES] / scale[...]

    def to_owner(d, carry):
        dest = lax.rem(me + d, peers)
        pltpu.make_async_remote_copy(
            src_ref=pbuf.at[pl.ds(pl.multiple_of(dest * SUB, SUB), SUB), :],
            dst_ref=rbuf.at[pl.ds(pl.multiple_of(me * SUB, SUB), SUB), :],
            send_sem=a_send, recv_sem=a_recv, device_id={"ctx": dest}, device_id_type=MESH,
        ).start()
        return carry

    lax.fori_loop(1, peers, to_owner, 0)
    mine = pl.ds(pl.multiple_of(me * SUB, SUB), SUB)
    rbuf[mine, :] = pbuf[mine, :]
    most = pl.ds(0, (peers - 1) * SUB)
    all_of = pltpu.make_async_remote_copy(
        src_ref=pbuf.at[most, :], dst_ref=rbuf.at[most, :], send_sem=a_send, recv_sem=a_recv,
        device_id={"ctx": lax.rem(me + 1, peers)}, device_id_type=MESH,
    )
    all_of.wait_recv()
    for q in range(4):
        acc = rbuf[pl.ds(q * SUB, SUB), :]
        for m in range(1, peers // 4):
            acc = acc + rbuf[pl.ds((4 * m + q) * SUB, SUB), :]
        out_ref[pl.ds(q * SUB, SUB), :] = acc
    all_of.wait_send()
    for n in range(16):
        w_copy(n, *sent[n]).wait_send()
    for k in range(parts):
        for kind in range(3):
            s_sent(k, kind).wait_send()
    for d in range(1, 4):
        power_copy(d).wait_send()
    token_copy(0, after).wait_send()
    token_copy(2, before).wait_send()
    core_copy(0).wait_send()
    core_copy(1).wait_send()
    z_copy.wait_send()


def body(tokens, complement, seg_lengths, owner, embed, norm_gain, taps, w_out):
    rows = tokens.shape[0]
    vocab, width = embed.shape
    cols = w_out.shape[1]
    segs = seg_lengths.shape[0]
    per_block = segs // owner.shape[0]
    total, group = 4 * rows, 4 * cols
    peers = owner.shape[0]
    vmem = pl.BlockSpec(memory_space=pltpu.VMEM)

    def tiles(count, dtype=f32):
        return pltpu.VMEM((count * SUB, LANES), dtype)

    def sems(count):
        return pltpu.SemaphoreType.DMA((count,))

    sums = pl.pallas_call(
        score_kernel,
        out_shape=jax.ShapeDtypeStruct((4 * SUB, LANES), f32),
        in_specs=[vmem] * 8,
        out_specs=vmem,
        scratch_shapes=[
            pltpu.VMEM((total, width), bf16),
            pltpu.VMEM((16 * cols, width), bf16),
            pltpu.VMEM((2, total, group), f32),
            pltpu.VMEM((2, total, group), f32),
            pltpu.VMEM((total, group), bf16),
            pltpu.VMEM((total, group), bf16),
            tiles(peers),
            tiles(peers),
            pltpu.VMEM((segs, total), bf16),
            pltpu.VMEM((segs, LANES), f32),
            pltpu.VMEM((3, SUB, rows), jnp.int32),
            pltpu.VMEM((4, SUB, vocab), f32),
            tiles(2 * rows),
            tiles(2 * rows),
            tiles(TAPROWS),
            tiles(TAPROWS),
            tiles(TAPROWS),
            tiles(TAPROWS),
            tiles(rows, jnp.int32),
            tiles(rows, jnp.int32),
            tiles(rows),
            sems(16),
            sems(16),
            sems(12),
            sems(12),
            sems(3),
            sems(3),
            pltpu.SemaphoreType.DMA,
            pltpu.SemaphoreType.DMA,
            sems(2),
            sems(2),
            sems(3),
            sems(3),
        ],
        compiler_params=pltpu.CompilerParams(
            vmem_limit_bytes=56 << 20, collective_id=0, has_side_effects=True
        ),
    )(
        tokens[None, :], complement[None, :], seg_lengths[None, :], owner[None, :],
        embed, norm_gain[None, :], taps, w_out.T,
    )
    sums = sums.reshape(4, per_block, 4, cols)
    return sums.transpose(1, 2, 0, 3).reshape(per_block, width)


def solution(mesh):
    in_specs = (P("ctx"), P(), P(), P(), P(None, "ch"), P("ch"), P(None, "ch"), P("ch", "ctx"))
    out_specs = P("ctx", "ch")
    return jax.shard_map(body, mesh=mesh, in_specs=in_specs, out_specs=out_specs, check_vma=False)
```

```python
import jax
import jax.numpy as jnp
from jax import lax
from jax.experimental import pallas as pl
from jax.experimental.pallas import tpu as pltpu
from jax.sharding import PartitionSpec as P

norm_eps = 1e-06
LANES = 128
SUB = 8
PAD = 8
SPAN = 128
TAPROWS = 152
BASE = 143
MESH = pl.DeviceIdType.MESH
f32 = jnp.float32
bf16 = jnp.bfloat16


def rows3(ref, k, n):
    return ref[pl.ds(pl.multiple_of(k * SUB, SUB), n * SUB), :].reshape(n, SUB, LANES)

def put3(ref, k, v):
    n = v.shape[0]
    ref[pl.ds(pl.multiple_of(k * SUB, SUB), n * SUB), :] = v.reshape(n * SUB, LANES)

def prep_taps(taps_ref, tv, dv, tr, dr):
    span = taps_ref.shape[0]
    edge = jnp.zeros((PAD * SUB, LANES), jnp.float32)
    tv[pl.ds(0, PAD * SUB), :] = edge
    for e in range(2):
        tv[pl.ds((PAD + span + 8 * e) * SUB, 8 * SUB), :] = edge
    for s in range(SUB):
        tv[pl.ds(PAD * SUB + s, span, stride=SUB), :] = taps_ref[:, s * LANES:(s + 1) * LANES]
    dv[pl.ds(0, PAD * SUB), :] = edge
    dv[pl.ds(PAD * SUB, (TAPROWS - PAD) * SUB), :] = (
        tv[pl.ds(0, (TAPROWS - PAD) * SUB), :] - tv[pl.ds(PAD * SUB, (TAPROWS - PAD) * SUB), :])
    def flip(k8, carry):
        for u in range(8):
            k = k8 * 8 + u
            put3(tr, TAPROWS - 1 - k, rows3(tv, k, 1))
            put3(dr, TAPROWS - 1 - k, rows3(dv, k, 1))
        return carry
    lax.fori_loop(0, TAPROWS // 8, flip, 0)

def conv_block(i, count, ext_f, ext_r, tv, dv, tr, dr, sv, ev, res):
    p0 = i * 16
    zero8 = jnp.zeros((8, SUB, LANES), jnp.float32)
    idx16 = lax.broadcasted_iota(jnp.int32, (16, SUB, LANES), 0)
    far_lags = SPAN // 16
    s0 = rows3(sv, p0, 1)
    e0 = rows3(ev, p0 + 15, 1)

    def fwd_far(j, acc):
        lag = j * 16
        q0 = p0 - lag
        rows = jnp.where(idx16 >= s0 - q0, rows3(ext_f, count + q0, 16), 0.0)
        x0, x1 = rows[:8], rows[8:]
        xs = x0 + x1
        a, b, c = acc
        for u in range(8):
            a = a + rows3(tv, PAD + lag - u, 8) * xs[u:u + 1]
            b = b + rows3(dv, PAD + lag - u, 8) * x1[u:u + 1]
            c = c + rows3(dv, PAD + 8 + lag - u, 8) * x0[u:u + 1]
        return a, b, c

    def rev_far(j, acc):
        lag = j * 16
        q0 = p0 + lag
        rows = jnp.where(idx16 < e0 - q0, rows3(ext_r, q0, 16), 0.0)
        x0, x1 = rows[:8], rows[8:]
        xs = x0 + x1
        a, b, c = acc
        for u in range(8):
            a = a + rows3(tr, BASE - lag - u, 8) * xs[u:u + 1]
            b = b + rows3(dr, BASE - lag - u, 8) * x0[u:u + 1]
            c = c + rows3(dr, BASE - 8 - lag - u, 8) * x1[u:u + 1]
        return a, b, c

    a, b, c = lax.fori_loop(1, far_lags + 1, fwd_far, (zero8,) * 3, unroll=2)
    far_f = (a + b, a - c)
    a, b, c = lax.fori_loop(1, far_lags + 1, rev_far, (zero8,) * 3, unroll=2)
    far_r = (a - c, a + b)
    xf = (rows3(ext_f, count + p0, 8), rows3(ext_f, count + p0 + 8, 8))
    xr = (rows3(ext_r, p0, 8), rows3(ext_r, p0 + 8, 8))
    idx8 = lax.broadcasted_iota(jnp.int32, (8, SUB, LANES), 0)
    mid = rows3(sv, p0 + 8, 1)
    m = jnp.where(idx8 >= mid - p0, xf[0], 0.0)
    mid_f = zero8
    for u in range(8):
        mid_f = mid_f + rows3(tv, PAD + 8 - u, 8) * m[u:u + 1]
    mid = rows3(ev, p0 + 7, 1)
    m = jnp.where(idx8 < mid - p0 - 8, xr[1], 0.0)
    mid_r = zero8
    for u in range(8):
        mid_r = mid_r + rows3(tr, BASE - 8 - u, 8) * m[u:u + 1]
    for h in range(2):
        pb = p0 + 8 * h
        start = rows3(sv, pb, 8)
        end = rows3(ev, pb, 8)
        mix_f = jnp.where(start < p0, far_f[h], 0.0)
        mix_r = jnp.where(end > p0 + 16, far_r[h], 0.0)
        if h == 1:
            mix_f = mix_f + jnp.where(start < pb, mid_f, 0.0)
        else:
            mix_r = mix_r + jnp.where(end > pb + 8, mid_r, 0.0)
        near_f = [rows3(tv, PAD + d, 1) for d in range(8)]
        sums_f, sums_r = [], []
        for r in range(8):
            sum_f, sum_r = mix_f[r : r + 1], mix_r[r : r + 1]
            for u in range(8):
                if u < r:
                    term = near_f[r - u] * xf[h][u : u + 1]
                    sum_f = sum_f + jnp.where(start[r : r + 1] <= pb + u, term, 0.0)
                elif u > r:
                    term = near_f[u - r] * xr[h][u : u + 1]
                    sum_r = sum_r + jnp.where(end[r : r + 1] > pb + u, term, 0.0)
            sums_f.append(sum_f + near_f[0] * xf[h][r : r + 1])
            sums_r.append(sum_r + near_f[0] * xr[h][r : r + 1])
        mix_f = jnp.concatenate(sums_f, axis=0)
        mix_r = jnp.concatenate(sums_r, axis=0)
        gated_f = (xf[h] * mix_f).astype(jnp.bfloat16).astype(jnp.float32)
        gated_r = (xr[h] * mix_r).astype(jnp.bfloat16).astype(jnp.float32)
        put3(res, pb, (gated_f + gated_r) * 0.5)


def score_kernel(tok_ref, comp_ref, lens_ref, owner_ref, gain_ref, embed_hbm, taps_hbm, w_hbm,
                 out_ref, embed_ref, taps_ref, sbuf, wbuf, out1, in1, zout, zin, kept,
                 pbuf, xbuf, abuf, rbuf, obuf, member, scale, tk, pw, gain8,
                 ext_f, ext_r, inv_f, inv_r, tv, dv, tr, dr, sv, ev, res,
                 l_sem, w_send, w_recv, s_send, s_recv, r_send, r_recv, z_send, z_recv,
                 x_send, x_recv, a_send, a_recv, t_send, t_recv, p_send, p_recv):
    me = lax.axis_index("ctx")
    ch = lax.axis_index("ch")
    peers = lax.axis_size("ctx")
    y = lax.rem(me, 4)
    zh = lax.rem(lax.div(me, 4), 4)
    x = lax.div(me, 16)
    zl = lax.div(ch, 2)
    core = lax.rem(ch, 2)

    def ring(v, by):
        return lax.rem(v + by, 4)

    def at_ctx(cx, cz, cy):
        return {"ctx": cx * 16 + cz * 4 + cy}

    xp, xm, x2 = ring(x, 1), ring(x, 3), ring(x, 2)
    zp, zm, z2 = ring(zh, 1), ring(zh, 3), ring(zh, 2)
    yp, ym, y2 = ring(y, 1), ring(y, 3), ring(y, 2)
    core_peer = zl * 2 + 1 - core
    z_peer = (1 - zl) * 2 + core
    after, before = lax.rem(me + 1, peers), lax.rem(me + peers - 1, peers)

    barrier = pltpu.get_barrier_semaphore()

    def greet(to):
        pl.semaphore_signal(barrier, inc=1, device_id=to, device_id_type=MESH)

    for d in range(1, 4):
        greet({"ch": lax.rem(ch + d, 4)})
        greet(at_ctx(ring(x, d), zh, y))
    greet({"ctx": after})
    greet({"ctx": before})

    def plane(d):
        return at_ctx(x, ring(zh, lax.div(d, 4)), ring(y, lax.rem(d, 4)))

    def hello(d, carry):
        greet(plane(d))
        return carry

    lax.fori_loop(1, 16, hello, 0)

    cols = w_hbm.shape[0]
    half = cols // 2
    rows = sbuf.shape[0] // 4
    vocab, width = embed_ref.shape
    segs = lens_ref.shape[1]
    own_w = wbuf.at[pl.ds(pl.multiple_of((x * 4 + zh) * cols, cols), cols), :]
    fetch = [
        pltpu.make_async_copy(embed_hbm, embed_ref, l_sem.at[0]),
        pltpu.make_async_copy(w_hbm, own_w, l_sem.at[1]),
        pltpu.make_async_copy(taps_hbm, taps_ref, l_sem.at[2]),
    ]
    for copy in fetch:
        copy.start()

    def iota(shape, dim):
        return lax.broadcasted_iota(jnp.int32, shape, dim)

    lens = jnp.broadcast_to(lens_ref[...], (SUB, segs)).astype(f32)
    upto = (iota((segs, segs), 0) <= iota((segs, segs), 1)).astype(bf16)
    ends_row = jnp.dot(lens.astype(bf16), upto, preferred_element_type=f32)
    starts_row = (ends_row - lens)[0:1]
    ends_row = ends_row[0:1]
    letters = iota((rows, vocab), 1)

    def ids_of(slot):
        return tk[slot].astype(f32).T[:, 0:1].astype(jnp.int32)

    def other_of(ids):
        hit = jnp.where(letters == ids, comp_ref[...].astype(f32), 0.0)
        return jnp.sum(hit, axis=1, keepdims=True).astype(jnp.int32)

    def pick_rows(ids_a, ids_b, put_a, put_b):
        picks = jnp.concatenate([letters == ids_a, letters == ids_b], axis=0)
        picks = picks.astype(f32).astype(bf16)
        for n in range(width // (2 * LANES)):
            table = embed_ref[:, n * 2 * LANES : (n + 1) * 2 * LANES]
            found = jnp.dot(picks, table, preferred_element_type=f32)
            for m in range(2):
                lanes = slice(m * LANES, (m + 1) * LANES)
                for ref, at, part in (put_a + (found[:rows],), put_b + (found[rows:],)):
                    ref[pl.ds(at * SUB + 2 * n + m, rows, stride=SUB), :] = part[:, lanes]

    tk[1] = jnp.broadcast_to(tok_ref[...], (SUB, rows))
    own_ids = ids_of(1)
    own_other = other_of(own_ids)

    fetch[0].wait()
    fold = jnp.zeros((vocab, LANES), f32)
    for s in range(SUB):
        piece = embed_ref[:, s * LANES : (s + 1) * LANES].astype(f32)
        fold = fold + piece * piece
        gain8[s : s + 1, :] = gain_ref[:, s * LANES : (s + 1) * LANES]
    pw[ch] = jnp.broadcast_to(jnp.sum(fold.T, axis=0, keepdims=True), (SUB, vocab))
    fetch[1].wait()

    def w_rows(cx, cz, h=None):
        lo, count = (0, cols) if h is None else (h * half, half)
        return wbuf.at[pl.ds(pl.multiple_of((cx * 4 + cz) * cols + lo, half), count), :]

    z_of = (zh, zm, zp, z2)
    plus, minus = at_ctx(xp, zh, y), at_ctx(xm, zh, y)
    up, down = at_ctx(x, zp, y), at_ctx(x, zm, y)
    sent, got = {}, {}
    for h in range(2):
        own = w_rows(x, zh, h)
        sent["z", h, 0], got["z", h, 0] = (own, up), w_rows(x, zm, h)
        sent["z", h, 1], got["z", h, 1] = (own, down), w_rows(x, zp, h)
        for dz in range(4):
            here = w_rows(x, z_of[dz], h)
            sent["x", dz, h, 0], got["x", dz, h, 0] = (here, plus), w_rows(xm, z_of[dz], h)
            sent["x", dz, h, 1], got["x", dz, h, 1] = (here, minus), w_rows(xp, z_of[dz], h)
    sent["y", 0], got["y", 0] = (w_rows(x, zm, 0), up), w_rows(x, z2, 0)
    sent["y", 1], got["y", 1] = (w_rows(x, zp, 1), down), w_rows(x, z2, 1)
    for dz in range(4):
        sent["r", dz, 0], got["r", dz, 0] = (w_rows(xm, z_of[dz], 0), plus), w_rows(x2, z_of[dz], 0)
        sent["r", dz, 1], got["r", dz, 1] = (w_rows(xp, z_of[dz], 1), minus), w_rows(x2, z_of[dz], 1)
    number = {name: n for n, name in enumerate(sent)}

    def w_copy(name, ref, to):
        n = number[name]
        return pltpu.make_async_remote_copy(
            src_ref=ref, dst_ref=ref, send_sem=w_send.at[n], recv_sem=w_recv.at[n],
            device_id=to, device_id_type=MESH,
        )

    seen = set()

    def w_start(*names):
        for name in names:
            w_copy(name, *sent[name]).start()

    def w_wait(*names):
        for name in names:
            seen.add(name)
            w_copy(name, got[name], plus).wait_recv()

    def both(dz, h):
        w_start(("x", dz, h, 0), ("x", dz, h, 1))

    def relay(dz):
        w_wait(("x", dz, 0, 0))
        w_start(("r", dz, 0))
        w_wait(("x", dz, 1, 1))
        w_start(("r", dz, 1))

    def step_a():
        w_wait(("z", 0, 0))
        both(1, 0)
        w_start(("y", 0))
        w_wait(("z", 0, 1))
        both(2, 0)

    def step_b():
        w_wait(("z", 1, 1))
        w_start(("y", 1))
        both(2, 1)
        w_wait(("z", 1, 0))
        both(1, 1)

    def step_c():
        w_wait(("y", 0))
        both(3, 0)
        w_wait(("y", 1))
        both(3, 1)

    def token_copy(slot, to):
        return pltpu.make_async_remote_copy(
            src_ref=tk.at[1], dst_ref=tk.at[slot], send_sem=t_send.at[slot // 2],
            recv_sem=t_recv.at[slot // 2], device_id={"ctx": to}, device_id_type=MESH,
        )

    def power_copy(d, ref):
        return pltpu.make_async_remote_copy(
            src_ref=ref, dst_ref=ref, send_sem=p_send.at[d - 1], recv_sem=p_recv.at[d - 1],
            device_id={"ch": lax.rem(ch + d, 4)}, device_id_type=MESH,
        )

    pl.semaphore_wait(barrier, 23)
    token_copy(0, after).start()
    token_copy(2, before).start()
    for d in range(1, 4):
        power_copy(d, pw.at[ch]).start()
    w_start(("z", 0, 0), ("z", 0, 1))
    both(0, 0)
    both(0, 1)
    w_start(("z", 1, 0), ("z", 1, 1))

    pick_rows(own_ids, own_other, (ext_f, rows), (ext_r, 0))
    first = me * rows
    pos = (iota((rows, segs), 0) + first).astype(f32)
    start_col = jnp.max(jnp.where(starts_row <= pos, starts_row, 0.0), axis=1, keepdims=True)
    end_col = jnp.min(jnp.where(ends_row > pos, ends_row, 1e9), axis=1, keepdims=True)
    start_col = jnp.broadcast_to(start_col, (rows, LANES)).astype(jnp.int32) - first
    end_col = jnp.broadcast_to(end_col, (rows, LANES)).astype(jnp.int32) - first
    for s in range(SUB):
        sv[pl.ds(s, rows, stride=SUB), :] = start_col
        ev[pl.ds(s, rows, stride=SUB), :] = end_col
    fetch[2].wait()
    prep_taps(taps_ref, tv, dv, tr, dr)

    token_copy(0, after).wait_recv()
    token_copy(2, before).wait_recv()
    last_ids = ids_of(0)
    next_other = other_of(ids_of(2))
    pick_rows(last_ids, next_other, (ext_f, 0), (ext_r, rows))

    for d in range(1, 4):
        power_copy(d, pw.at[lax.rem(ch + 4 - d, 4)]).wait_recv()
    power = (pw[0] + pw[1]) + (pw[2] + pw[3])
    inv_row = lax.rsqrt(power / (4 * width) + norm_eps)[0:1]
    for ref, at, ids in (
        (inv_f, 0, last_ids), (inv_f, rows, own_ids), (inv_r, 0, own_other), (inv_r, rows, next_other),
    ):
        col = jnp.sum(jnp.where(letters == ids, inv_row, 0.0), axis=1, keepdims=True)
        col = jnp.broadcast_to(col, (rows, LANES))
        for s in range(SUB):
            ref[pl.ds(at * SUB + s, rows, stride=SUB), :] = col

    def scale_rows(i, carry):
        for ext, inv in ((ext_f, inv_f), (ext_r, inv_r)):
            value = rows3(ext, i * 16, 16) * rows3(inv, i * 16, 16) * gain8[...][None]
            put3(ext, i * 16, value.astype(bf16).astype(f32))
        return carry

    lax.fori_loop(0, 2 * rows // 16, scale_rows, 0)
    relay(0)

    chunk = 16
    parts = rows // chunk
    direct = parts - 2

    def s_rows(cy, k):
        return sbuf.at[pl.ds(pl.multiple_of(cy * rows + k * chunk, chunk), chunk), :]

    def s_copy(k, kind, ref, cy):
        return pltpu.make_async_remote_copy(
            src_ref=ref, dst_ref=ref, send_sem=s_send.at[3 * k + kind],
            recv_sem=s_recv.at[3 * k + kind], device_id=at_ctx(x, zh, cy), device_id_type=MESH,
        )

    def s_relay(k):
        side = lax.rem(k, 2)
        there = s_rows(ring(y, 3 - 2 * side), k)
        s_copy(k, side, there, yp).wait_recv()
        s_copy(k, 2, there, ring(y, 1 + 2 * side)).start()

    steps = {0: step_a, 2: step_b, 3: lambda: relay(1), 4: step_c, 5: lambda: relay(2), 7: lambda: relay(3)}

    def sixteen(i, carry):
        conv_block(i, rows, ext_f, ext_r, tv, dv, tr, dr, sv, ev, res)
        at = pl.ds(pl.multiple_of(y * rows + i * chunk, chunk), chunk)
        for s in range(SUB):
            block = res[pl.ds(i * chunk * SUB + s, chunk, stride=SUB), :]
            sbuf[at, s * LANES : (s + 1) * LANES] = block.astype(bf16)
        s_copy(i, 0, s_rows(y, i), yp).start()
        s_copy(i, 1, s_rows(y, i), ym).start()

        @pl.when(i >= direct)
        def _():
            s_copy(i, 2, s_rows(y, i), y2).start()

        @pl.when(i >= 2)
        def _():
            s_relay(i - 2)

        for when, step in steps.items():
            pl.when(i == when)(step)
        return carry

    lax.fori_loop(0, parts, sixteen, 0)

    blocks = owner_ref.shape[1]
    spread = ((iota((blocks, segs), 1) >> 2) == iota((blocks, segs), 0)).astype(bf16)
    owners = jnp.broadcast_to(owner_ref[...], (SUB, blocks)).astype(f32).astype(bf16)
    owner_row = jnp.dot(owners, spread, preferred_element_type=f32)[0:1].astype(jnp.int32)
    slot, seg = iota((segs, segs), 0), iota((segs, segs), 1)
    same = (owner_row == (slot >> 2)) & ((slot & 3) == (seg & 3))
    slot_start = jnp.sum(jnp.where(same, starts_row, 0.0), axis=1, keepdims=True)
    slot_end = jnp.sum(jnp.where(same, ends_row, 0.0), axis=1, keepdims=True)
    total = 4 * rows
    spot = (iota((segs, total), 1) + lax.div(me, 4) * total).astype(f32)
    member[...] = ((slot_start <= spot) & (spot < slot_end)).astype(f32).astype(bf16)
    scale[...] = jnp.broadcast_to(slot_end - slot_start, (segs, LANES))

    def s_finish(k, carry):
        side = lax.rem(k, 2)
        s_copy(k, 1 - side, s_rows(ring(y, 1 + 2 * side), k), yp).wait_recv()
        s_copy(k, 2, s_rows(y2, k), yp).wait_recv()

        @pl.when(k >= direct)
        def _():
            s_copy(k, side, s_rows(ring(y, 3 - 2 * side), k), yp).wait_recv()

        return carry

    lax.fori_loop(0, parts, s_finish, 0)
    w_wait(*[name for name in got if name not in seen])

    group = 4 * cols

    def product(g):
        rhs = wbuf[pl.ds(pl.multiple_of(g * group, group), group), :]
        return lax.dot_general(
            sbuf[...], rhs, (((1,), (1,)), ((), ())), preferred_element_type=f32
        )

    def core_copy(n):
        return pltpu.make_async_remote_copy(
            src_ref=out1.at[n], dst_ref=in1.at[n], send_sem=r_send.at[n],
            recv_sem=r_recv.at[n], device_id={"ch": core_peer}, device_id_type=MESH,
        )

    def z_copy(t):
        at = pl.ds(t * rows, rows)
        return pltpu.make_async_remote_copy(
            src_ref=zout.at[at, :], dst_ref=zin.at[at, :], send_sem=z_send.at[t],
            recv_sem=z_recv.at[t], device_id={"ch": z_peer}, device_id_type=MESH,
        )

    out1[0] = product(2 * (1 - zl) + 1 - core).astype(bf16)
    core_copy(0).start()
    kept[...] = product(2 * (1 - zl) + core)
    core_copy(0).wait_recv()
    for t in range(4):
        at = pl.ds(t * rows, rows)
        zout[at, :] = (kept[at, :] + in1[0, at, :].astype(f32)).astype(bf16)
        z_copy(t).start()
    out1[1] = product(2 * zl + 1 - core).astype(bf16)
    core_copy(1).start()
    kept[...] = product(2 * zl + core)
    core_copy(1).wait_recv()

    sums = jnp.zeros((segs, group), f32)
    for t in range(4):
        at = pl.ds(t * rows, rows)
        z_copy(t).wait_recv()
        scores = kept[at, :] + in1[1, at, :].astype(f32) + zin[at, :].astype(f32)
        active = jnp.maximum(scores, 0.0) + jnp.log1p(jnp.exp(-jnp.abs(scores)))
        high = active.astype(bf16)
        low = (active - high.astype(f32)).astype(bf16)
        picks = member[:, t * rows : (t + 1) * rows]
        sums = sums + jnp.dot(picks, high, preferred_element_type=f32)
        sums = sums + jnp.dot(picks, low, preferred_element_type=f32)
    wide = group // LANES
    for h in range(wide):
        pbuf[pl.ds(h, segs, stride=wide), :] = sums[:, h * LANES : (h + 1) * LANES] / scale[...]

    share = 16 * SUB

    def to_x(d):
        return pltpu.make_async_remote_copy(
            src_ref=pbuf.at[pl.ds(pl.multiple_of(ring(x, d) * share, share), share), :],
            dst_ref=xbuf.at[d - 1], send_sem=x_send.at[d - 1], recv_sem=x_recv.at[d - 1],
            device_id=at_ctx(ring(x, d), zh, y), device_id_type=MESH,
        )

    for d in range(1, 4):
        to_x(d).start()
    mine = pbuf[pl.ds(pl.multiple_of(x * share, share), share), :]
    for d in range(1, 4):
        to_x(d).wait_recv()
        mine = mine + xbuf[d - 1]
    abuf[...] = mine

    def tile_at(cz, cy):
        return pl.ds(pl.multiple_of((cz * 4 + cy) * SUB, SUB), SUB)

    def to_owner(d, carry):
        cz, cy = ring(zh, lax.div(d, 4)), ring(y, lax.rem(d, 4))
        pltpu.make_async_remote_copy(
            src_ref=abuf.at[tile_at(cz, cy), :], dst_ref=rbuf.at[tile_at(zh, y), :],
            send_sem=a_send, recv_sem=a_recv, device_id=plane(d), device_id_type=MESH,
        ).start()
        return carry

    lax.fori_loop(1, 16, to_owner, 0)
    rbuf[tile_at(zh, y), :] = abuf[tile_at(zh, y), :]
    most = pl.ds(0, 15 * SUB)
    all_of = pltpu.make_async_remote_copy(
        src_ref=abuf.at[most, :], dst_ref=rbuf.at[most, :], send_sem=a_send, recv_sem=a_recv,
        device_id=plane(1), device_id_type=MESH,
    )
    all_of.wait_recv()
    for q in range(4):
        acc = rbuf[pl.ds(q * SUB, SUB), :]
        for m in range(1, 4):
            acc = acc + rbuf[pl.ds((4 * m + q) * SUB, SUB), :]
        obuf[pl.ds(q * SUB, SUB), :] = acc
        obuf[pl.ds((4 + q) * SUB, SUB), :] = pltpu.roll(acc, LANES // 2, 1)
    count = out_ref.shape[0]
    left = iota((count, LANES), 1) < LANES // 2
    for hz in range(2):
        for q in range(2):
            plain = [obuf[pl.ds((2 * q + n) * SUB + hz, count, stride=2), :] for n in range(2)]
            moved = [obuf[pl.ds((4 + 2 * q + n) * SUB + hz, count, stride=2), :] for n in range(2)]
            for b in range(2):
                pair = (plain[0], moved[1]) if b == 0 else (moved[0], plain[1])
                lane = ((2 * hz + b) * 2 + q) * LANES
                out_ref[:, lane : lane + LANES] = jnp.where(left, *pair)

    all_of.wait_send()
    for name in sent:
        w_copy(name, *sent[name]).wait_send()

    def s_drain(k, carry):
        for kind in range(3):
            s_copy(k, kind, s_rows(y, k), yp).wait_send()
        return carry

    lax.fori_loop(0, parts, s_drain, 0)
    for d in range(1, 4):
        power_copy(d, pw.at[ch]).wait_send()
        to_x(d).wait_send()
    token_copy(0, after).wait_send()
    token_copy(2, before).wait_send()
    core_copy(0).wait_send()
    core_copy(1).wait_send()
    for t in range(4):
        z_copy(t).wait_send()


def body(tokens, complement, seg_lengths, owner, embed, norm_gain, taps, w_out):
    rows = tokens.shape[0]
    vocab, width = embed.shape
    cols = w_out.shape[1]
    segs = seg_lengths.shape[0]
    per_block = segs // owner.shape[0]
    total, group = 4 * rows, 4 * cols
    vmem = pl.BlockSpec(memory_space=pltpu.VMEM)
    hbm = pl.BlockSpec(memory_space=pl.ANY)

    def tiles(count, dtype=f32):
        return pltpu.VMEM((count * SUB, LANES), dtype)

    def sems(count):
        return pltpu.SemaphoreType.DMA((count,))

    return pl.pallas_call(
        score_kernel,
        out_shape=jax.ShapeDtypeStruct((per_block, width), f32),
        in_specs=[vmem] * 5 + [hbm] * 3,
        out_specs=vmem,
        scratch_shapes=[
            pltpu.VMEM((vocab, width), bf16),
            pltpu.VMEM((taps.shape[0], width), f32),
            pltpu.VMEM((total, width), bf16),
            pltpu.VMEM((16 * cols, width), bf16),
            pltpu.VMEM((2, total, group), bf16),
            pltpu.VMEM((2, total, group), bf16),
            pltpu.VMEM((total, group), bf16),
            pltpu.VMEM((total, group), bf16),
            pltpu.VMEM((total, group), f32),
            tiles(64),
            pltpu.VMEM((3, 16 * SUB, LANES), f32),
            tiles(16),
            tiles(16),
            tiles(8),
            pltpu.VMEM((segs, total), bf16),
            pltpu.VMEM((segs, LANES), f32),
            pltpu.VMEM((3, SUB, rows), jnp.int32),
            pltpu.VMEM((4, SUB, vocab), f32),
            tiles(1),
        ]
        + [tiles(2 * rows)] * 4
        + [tiles(TAPROWS)] * 4
        + [tiles(rows, jnp.int32)] * 2
        + [tiles(rows)]
        + [sems(3), sems(30), sems(30), sems(24), sems(24), sems(2), sems(2), sems(4), sems(4)]
        + [sems(3), sems(3), pltpu.SemaphoreType.DMA, pltpu.SemaphoreType.DMA]
        + [sems(2), sems(2), sems(3), sems(3)],
        compiler_params=pltpu.CompilerParams(
            vmem_limit_bytes=56 << 20, collective_id=0, has_side_effects=True
        ),
    )(
        tokens[None, :], complement[None, :], seg_lengths[None, :], owner[None, :],
        norm_gain[None, :], embed, taps, w_out.T,
    )


def solution(mesh):
    in_specs = (P("ctx"), P(), P(), P(), P(None, "ch"), P("ch"), P(None, "ch"), P("ch", "ctx"))
    out_specs = P("ctx", "ch")
    return jax.shard_map(body, mesh=mesh, in_specs=in_specs, out_specs=out_specs, check_vma=False)
```

```python
import jax
import jax.numpy as jnp
from jax import lax
from jax.experimental import pallas as pl
from jax.experimental.pallas import tpu as pltpu
from jax.sharding import PartitionSpec as P

norm_eps = 1e-06
LANES = 128
SUB = 8
PAD = 8
SPAN = 128
TAPROWS = 152
BASE = 143
MESH = pl.DeviceIdType.MESH
f32 = jnp.float32
bf16 = jnp.bfloat16


def rows3(ref, k, n):
    return ref[pl.ds(pl.multiple_of(k * SUB, SUB), n * SUB), :].reshape(n, SUB, LANES)

def put3(ref, k, v):
    n = v.shape[0]
    ref[pl.ds(pl.multiple_of(k * SUB, SUB), n * SUB), :] = v.reshape(n * SUB, LANES)

def prep_taps(taps_ref, tv, dv, tr, dr):
    span = taps_ref.shape[0]
    edge = jnp.zeros((PAD * SUB, LANES), jnp.float32)
    tv[pl.ds(0, PAD * SUB), :] = edge
    for e in range(2):
        tv[pl.ds((PAD + span + 8 * e) * SUB, 8 * SUB), :] = edge
    for s in range(SUB):
        tv[pl.ds(PAD * SUB + s, span, stride=SUB), :] = taps_ref[:, s * LANES:(s + 1) * LANES]
    dv[pl.ds(0, PAD * SUB), :] = edge
    dv[pl.ds(PAD * SUB, (TAPROWS - PAD) * SUB), :] = (
        tv[pl.ds(0, (TAPROWS - PAD) * SUB), :] - tv[pl.ds(PAD * SUB, (TAPROWS - PAD) * SUB), :])
    def flip(k8, carry):
        for u in range(8):
            k = k8 * 8 + u
            put3(tr, TAPROWS - 1 - k, rows3(tv, k, 1))
            put3(dr, TAPROWS - 1 - k, rows3(dv, k, 1))
        return carry
    lax.fori_loop(0, TAPROWS // 8, flip, 0)

def conv_block(i, count, ext_f, ext_r, tv, dv, tr, dr, sv, ev, res):
    p0 = i * 16
    zero8 = jnp.zeros((8, SUB, LANES), jnp.float32)
    idx16 = lax.broadcasted_iota(jnp.int32, (16, SUB, LANES), 0)
    far_lags = SPAN // 16
    s0 = rows3(sv, p0, 1)
    e0 = rows3(ev, p0 + 15, 1)

    def fwd_far(j, acc):
        lag = j * 16
        q0 = p0 - lag
        rows = jnp.where(idx16 >= s0 - q0, rows3(ext_f, count + q0, 16), 0.0)
        x0, x1 = rows[:8], rows[8:]
        xs = x0 + x1
        a, b, c = acc
        for u in range(8):
            a = a + rows3(tv, PAD + lag - u, 8) * xs[u:u + 1]
            b = b + rows3(dv, PAD + lag - u, 8) * x1[u:u + 1]
            c = c + rows3(dv, PAD + 8 + lag - u, 8) * x0[u:u + 1]
        return a, b, c

    def rev_far(j, acc):
        lag = j * 16
        q0 = p0 + lag
        rows = jnp.where(idx16 < e0 - q0, rows3(ext_r, q0, 16), 0.0)
        x0, x1 = rows[:8], rows[8:]
        xs = x0 + x1
        a, b, c = acc
        for u in range(8):
            a = a + rows3(tr, BASE - lag - u, 8) * xs[u:u + 1]
            b = b + rows3(dr, BASE - lag - u, 8) * x0[u:u + 1]
            c = c + rows3(dr, BASE - 8 - lag - u, 8) * x1[u:u + 1]
        return a, b, c

    a, b, c = lax.fori_loop(1, far_lags + 1, fwd_far, (zero8,) * 3, unroll=2)
    far_f = (a + b, a - c)
    a, b, c = lax.fori_loop(1, far_lags + 1, rev_far, (zero8,) * 3, unroll=2)
    far_r = (a - c, a + b)
    xf = (rows3(ext_f, count + p0, 8), rows3(ext_f, count + p0 + 8, 8))
    xr = (rows3(ext_r, p0, 8), rows3(ext_r, p0 + 8, 8))
    idx8 = lax.broadcasted_iota(jnp.int32, (8, SUB, LANES), 0)
    mid = rows3(sv, p0 + 8, 1)
    m = jnp.where(idx8 >= mid - p0, xf[0], 0.0)
    mid_f = zero8
    for u in range(8):
        mid_f = mid_f + rows3(tv, PAD + 8 - u, 8) * m[u:u + 1]
    mid = rows3(ev, p0 + 7, 1)
    m = jnp.where(idx8 < mid - p0 - 8, xr[1], 0.0)
    mid_r = zero8
    for u in range(8):
        mid_r = mid_r + rows3(tr, BASE - 8 - u, 8) * m[u:u + 1]
    for h in range(2):
        pb = p0 + 8 * h
        start = rows3(sv, pb, 8)
        end = rows3(ev, pb, 8)
        mix_f = jnp.where(start < p0, far_f[h], 0.0)
        mix_r = jnp.where(end > p0 + 16, far_r[h], 0.0)
        if h == 1:
            mix_f = mix_f + jnp.where(start < pb, mid_f, 0.0)
        else:
            mix_r = mix_r + jnp.where(end > pb + 8, mid_r, 0.0)
        near_f = [rows3(tv, PAD + d, 1) for d in range(8)]
        sums_f, sums_r = [], []
        for r in range(8):
            sum_f, sum_r = mix_f[r : r + 1], mix_r[r : r + 1]
            for u in range(8):
                if u < r:
                    term = near_f[r - u] * xf[h][u : u + 1]
                    sum_f = sum_f + jnp.where(start[r : r + 1] <= pb + u, term, 0.0)
                elif u > r:
                    term = near_f[u - r] * xr[h][u : u + 1]
                    sum_r = sum_r + jnp.where(end[r : r + 1] > pb + u, term, 0.0)
            sums_f.append(sum_f + near_f[0] * xf[h][r : r + 1])
            sums_r.append(sum_r + near_f[0] * xr[h][r : r + 1])
        mix_f = jnp.concatenate(sums_f, axis=0)
        mix_r = jnp.concatenate(sums_r, axis=0)
        gated_f = (xf[h] * mix_f).astype(jnp.bfloat16).astype(jnp.float32)
        gated_r = (xr[h] * mix_r).astype(jnp.bfloat16).astype(jnp.float32)
        put3(res, pb, (gated_f + gated_r) * 0.5)


def score_kernel(tok_ref, comp_ref, lens_ref, owner_ref, gain_ref, embed_hbm, taps_hbm, w_hbm,
                 out_ref, embed_ref, taps_ref, sbuf, wbuf, out1, in1, zout, zin, kept,
                 pbuf, xbuf, abuf, rbuf, obuf, member, scale, tk, pw, gain8,
                 ext_f, ext_r, inv_f, inv_r, tv, dv, tr, dr, sv, ev, res,
                 l_sem, w_send, w_recv, s_send, s_recv, r_send, r_recv, z_send, z_recv,
                 x_send, x_recv, a_send, a_recv, t_send, t_recv, p_send, p_recv):
    me = lax.axis_index("ctx")
    ch = lax.axis_index("ch")
    peers = lax.axis_size("ctx")
    y = lax.rem(me, 4)
    zh = lax.rem(lax.div(me, 4), 4)
    x = lax.div(me, 16)
    zl = lax.div(ch, 2)
    core = lax.rem(ch, 2)

    def ring(v, by):
        return lax.rem(v + by, 4)

    def at_ctx(cx, cz, cy):
        return {"ctx": cx * 16 + cz * 4 + cy}

    xp, xm, x2 = ring(x, 1), ring(x, 3), ring(x, 2)
    zp, zm, z2 = ring(zh, 1), ring(zh, 3), ring(zh, 2)
    yp, ym, y2 = ring(y, 1), ring(y, 3), ring(y, 2)
    core_peer = zl * 2 + 1 - core
    z_peer = (1 - zl) * 2 + core
    after, before = lax.rem(me + 1, peers), lax.rem(me + peers - 1, peers)

    barrier = pltpu.get_barrier_semaphore()

    def greet(to):
        pl.semaphore_signal(barrier, inc=1, device_id=to, device_id_type=MESH)

    for d in range(1, 4):
        greet({"ch": lax.rem(ch + d, 4)})
        greet(at_ctx(ring(x, d), zh, y))
    greet({"ctx": after})
    greet({"ctx": before})

    def plane(d):
        return at_ctx(x, ring(zh, lax.div(d, 4)), ring(y, lax.rem(d, 4)))

    def hello(d, carry):
        greet(plane(d))
        return carry

    lax.fori_loop(1, 16, hello, 0)

    cols = w_hbm.shape[0]
    half = cols // 2
    rows = sbuf.shape[0] // 4
    vocab, width = embed_ref.shape
    segs = lens_ref.shape[1]
    own_w = wbuf.at[pl.ds(pl.multiple_of((x * 4 + zh) * cols, cols), cols), :]
    fetch = [
        pltpu.make_async_copy(embed_hbm, embed_ref, l_sem.at[0]),
        pltpu.make_async_copy(w_hbm, own_w, l_sem.at[1]),
        pltpu.make_async_copy(taps_hbm, taps_ref, l_sem.at[2]),
    ]
    for copy in fetch:
        copy.start()

    def iota(shape, dim):
        return lax.broadcasted_iota(jnp.int32, shape, dim)

    lens = jnp.broadcast_to(lens_ref[...], (SUB, segs)).astype(f32)
    upto = (iota((segs, segs), 0) <= iota((segs, segs), 1)).astype(bf16)
    ends_row = jnp.dot(lens.astype(bf16), upto, preferred_element_type=f32)
    starts_row = (ends_row - lens)[0:1]
    ends_row = ends_row[0:1]
    letters = iota((rows, vocab), 1)

    def ids_of(slot):
        return tk[slot].astype(f32).T[:, 0:1].astype(jnp.int32)

    def other_of(ids):
        hit = jnp.where(letters == ids, comp_ref[...].astype(f32), 0.0)
        return jnp.sum(hit, axis=1, keepdims=True).astype(jnp.int32)

    def pick_rows(ids_a, ids_b, put_a, put_b):
        picks = jnp.concatenate([letters == ids_a, letters == ids_b], axis=0)
        picks = picks.astype(f32).astype(bf16)
        for n in range(width // (2 * LANES)):
            table = embed_ref[:, n * 2 * LANES : (n + 1) * 2 * LANES]
            found = jnp.dot(picks, table, preferred_element_type=f32)
            for m in range(2):
                lanes = slice(m * LANES, (m + 1) * LANES)
                for ref, at, part in (put_a + (found[:rows],), put_b + (found[rows:],)):
                    ref[pl.ds(at * SUB + 2 * n + m, rows, stride=SUB), :] = part[:, lanes]

    tk[1] = jnp.broadcast_to(tok_ref[...], (SUB, rows))
    own_ids = ids_of(1)
    own_other = other_of(own_ids)

    fetch[0].wait()
    fold = jnp.zeros((vocab, LANES), f32)
    for s in range(SUB):
        piece = embed_ref[:, s * LANES : (s + 1) * LANES].astype(f32)
        fold = fold + piece * piece
        gain8[s : s + 1, :] = gain_ref[:, s * LANES : (s + 1) * LANES]
    pw[ch] = jnp.broadcast_to(jnp.sum(fold.T, axis=0, keepdims=True), (SUB, vocab))
    fetch[1].wait()

    def w_rows(cx, cz, h=None):
        lo, count = (0, cols) if h is None else (h * half, half)
        return wbuf.at[pl.ds(pl.multiple_of((cx * 4 + cz) * cols + lo, half), count), :]

    z_of = (zh, zm, zp, z2)
    plus, minus = at_ctx(xp, zh, y), at_ctx(xm, zh, y)
    up, down = at_ctx(x, zp, y), at_ctx(x, zm, y)
    sent, got = {}, {}
    for h in range(2):
        own = w_rows(x, zh, h)
        sent["z", h, 0], got["z", h, 0] = (own, up), w_rows(x, zm, h)
        sent["z", h, 1], got["z", h, 1] = (own, down), w_rows(x, zp, h)
        for dz in range(4):
            here = w_rows(x, z_of[dz], h)
            sent["x", dz, h, 0], got["x", dz, h, 0] = (here, plus), w_rows(xm, z_of[dz], h)
            sent["x", dz, h, 1], got["x", dz, h, 1] = (here, minus), w_rows(xp, z_of[dz], h)
    sent["y", 0], got["y", 0] = (w_rows(x, zm, 0), up), w_rows(x, z2, 0)
    sent["y", 1], got["y", 1] = (w_rows(x, zp, 1), down), w_rows(x, z2, 1)
    for dz in range(4):
        sent["r", dz, 0], got["r", dz, 0] = (w_rows(xm, z_of[dz], 0), plus), w_rows(x2, z_of[dz], 0)
        sent["r", dz, 1], got["r", dz, 1] = (w_rows(xp, z_of[dz], 1), minus), w_rows(x2, z_of[dz], 1)
    number = {name: n for n, name in enumerate(sent)}

    def w_copy(name, ref, to):
        n = number[name]
        return pltpu.make_async_remote_copy(
            src_ref=ref, dst_ref=ref, send_sem=w_send.at[n], recv_sem=w_recv.at[n],
            device_id=to, device_id_type=MESH,
        )

    seen = set()

    def w_start(*names):
        for name in names:
            w_copy(name, *sent[name]).start()

    def w_wait(*names):
        for name in names:
            seen.add(name)
            w_copy(name, got[name], plus).wait_recv()

    def both(dz, h):
        w_start(("x", dz, h, 0), ("x", dz, h, 1))

    def relay(dz):
        w_wait(("x", dz, 0, 0))
        w_start(("r", dz, 0))
        w_wait(("x", dz, 1, 1))
        w_start(("r", dz, 1))

    def step_a():
        w_wait(("z", 0, 0))
        both(1, 0)
        w_start(("y", 0))
        w_wait(("z", 0, 1))
        both(2, 0)

    def step_b():
        w_wait(("z", 1, 1))
        w_start(("y", 1))
        both(2, 1)
        w_wait(("z", 1, 0))
        both(1, 1)

    def step_c():
        w_wait(("y", 0))
        both(3, 0)
        w_wait(("y", 1))
        both(3, 1)

    def token_copy(slot, to):
        return pltpu.make_async_remote_copy(
            src_ref=tk.at[1], dst_ref=tk.at[slot], send_sem=t_send.at[slot // 2],
            recv_sem=t_recv.at[slot // 2], device_id={"ctx": to}, device_id_type=MESH,
        )

    def power_copy(d, ref):
        return pltpu.make_async_remote_copy(
            src_ref=ref, dst_ref=ref, send_sem=p_send.at[d - 1], recv_sem=p_recv.at[d - 1],
            device_id={"ch": lax.rem(ch + d, 4)}, device_id_type=MESH,
        )

    pl.semaphore_wait(barrier, 23)
    token_copy(0, after).start()
    token_copy(2, before).start()
    for d in range(1, 4):
        power_copy(d, pw.at[ch]).start()
    w_start(("z", 0, 0), ("z", 0, 1))
    both(0, 0)
    both(0, 1)
    w_start(("z", 1, 0), ("z", 1, 1))

    pick_rows(own_ids, own_other, (ext_f, rows), (ext_r, 0))
    first = me * rows
    pos = (iota((rows, segs), 0) + first).astype(f32)
    start_col = jnp.max(jnp.where(starts_row <= pos, starts_row, 0.0), axis=1, keepdims=True)
    end_col = jnp.min(jnp.where(ends_row > pos, ends_row, 1e9), axis=1, keepdims=True)
    start_col = jnp.broadcast_to(start_col, (rows, LANES)).astype(jnp.int32) - first
    end_col = jnp.broadcast_to(end_col, (rows, LANES)).astype(jnp.int32) - first
    for s in range(SUB):
        sv[pl.ds(s, rows, stride=SUB), :] = start_col
        ev[pl.ds(s, rows, stride=SUB), :] = end_col
    fetch[2].wait()
    prep_taps(taps_ref, tv, dv, tr, dr)

    token_copy(0, after).wait_recv()
    token_copy(2, before).wait_recv()
    last_ids = ids_of(0)
    next_other = other_of(ids_of(2))
    pick_rows(last_ids, next_other, (ext_f, 0), (ext_r, rows))

    for d in range(1, 4):
        power_copy(d, pw.at[lax.rem(ch + 4 - d, 4)]).wait_recv()
    power = (pw[0] + pw[1]) + (pw[2] + pw[3])
    inv_row = lax.rsqrt(power / (4 * width) + norm_eps)[0:1]
    for ref, at, ids in (
        (inv_f, 0, last_ids), (inv_f, rows, own_ids), (inv_r, 0, own_other), (inv_r, rows, next_other),
    ):
        col = jnp.sum(jnp.where(letters == ids, inv_row, 0.0), axis=1, keepdims=True)
        col = jnp.broadcast_to(col, (rows, LANES))
        for s in range(SUB):
            ref[pl.ds(at * SUB + s, rows, stride=SUB), :] = col

    def scale_rows(i, carry):
        for ext, inv in ((ext_f, inv_f), (ext_r, inv_r)):
            value = rows3(ext, i * 16, 16) * rows3(inv, i * 16, 16) * gain8[...][None]
            put3(ext, i * 16, value.astype(bf16).astype(f32))
        return carry

    lax.fori_loop(0, 2 * rows // 16, scale_rows, 0)
    relay(0)

    chunk = 16
    parts = rows // chunk

    def s_rows(cy, k):
        return sbuf.at[pl.ds(pl.multiple_of(cy * rows + k * chunk, chunk), chunk), :]

    def s_copy(k, kind, ref, cy):
        return pltpu.make_async_remote_copy(
            src_ref=ref, dst_ref=ref, send_sem=s_send.at[3 * k + kind],
            recv_sem=s_recv.at[3 * k + kind], device_id=at_ctx(x, zh, cy), device_id_type=MESH,
        )

    steps = {1: step_a, 3: step_b, 5: step_c, 6: lambda: relay(2), 7: lambda: relay(1)}

    def sixteen(i, carry):
        conv_block(i, rows, ext_f, ext_r, tv, dv, tr, dr, sv, ev, res)
        at = pl.ds(pl.multiple_of(y * rows + i * chunk, chunk), chunk)
        for s in range(SUB):
            block = res[pl.ds(i * chunk * SUB + s, chunk, stride=SUB), :]
            sbuf[at, s * LANES : (s + 1) * LANES] = block.astype(bf16)
        s_copy(i, 0, s_rows(y, i), yp).start()
        s_copy(i, 1, s_rows(y, i), ym).start()

        s_copy(i, 2, s_rows(y, i), y2).start()
        for when, step in steps.items():
            pl.when(i == when)(step)
        return carry

    lax.fori_loop(0, parts, sixteen, 0)

    blocks = owner_ref.shape[1]
    spread = ((iota((blocks, segs), 1) >> 2) == iota((blocks, segs), 0)).astype(bf16)
    owners = jnp.broadcast_to(owner_ref[...], (SUB, blocks)).astype(f32).astype(bf16)
    owner_row = jnp.dot(owners, spread, preferred_element_type=f32)[0:1].astype(jnp.int32)
    slot, seg = iota((segs, segs), 0), iota((segs, segs), 1)
    same = (owner_row == (slot >> 2)) & ((slot & 3) == (seg & 3))
    slot_start = jnp.sum(jnp.where(same, starts_row, 0.0), axis=1, keepdims=True)
    slot_end = jnp.sum(jnp.where(same, ends_row, 0.0), axis=1, keepdims=True)
    total = 4 * rows
    spot = (iota((segs, total), 1) + lax.div(me, 4) * total).astype(f32)
    member[...] = ((slot_start <= spot) & (spot < slot_end)).astype(f32).astype(bf16)
    scale[...] = jnp.broadcast_to(slot_end - slot_start, (segs, LANES))

    relay(3)

    def s_finish(k, carry):
        for kind, cy in enumerate((ym, yp, y2)):
            s_copy(k, kind, s_rows(cy, k), yp).wait_recv()
        return carry

    lax.fori_loop(0, parts, s_finish, 0)
    w_wait(*[name for name in got if name not in seen])

    group = 4 * cols

    def product(g):
        rhs = wbuf[pl.ds(pl.multiple_of(g * group, group), group), :]
        return lax.dot_general(
            sbuf[...], rhs, (((1,), (1,)), ((), ())), preferred_element_type=f32
        )

    def core_copy(n):
        return pltpu.make_async_remote_copy(
            src_ref=out1.at[n], dst_ref=in1.at[n], send_sem=r_send.at[n],
            recv_sem=r_recv.at[n], device_id={"ch": core_peer}, device_id_type=MESH,
        )

    def z_copy(h, t):
        at = pl.ds(t * 2 * rows, 2 * rows)
        return pltpu.make_async_remote_copy(
            src_ref=zout.at[h, at, :], dst_ref=zin.at[h, at, :], send_sem=z_send.at[2 * h + t],
            recv_sem=z_recv.at[2 * h + t], device_id={"ch": z_peer}, device_id_type=MESH,
        )

    out1[0] = product(2 * (1 - zl) + 1 - core).astype(bf16)
    core_copy(0).start()
    kept[...] = product(2 * (1 - zl) + core)
    core_copy(0).wait_recv()
    for h in range(2):
        lanes = slice(h * LANES, (h + 1) * LANES)
        for t in range(2):
            at = pl.ds(t * 2 * rows, 2 * rows)
            zout[h, at, :] = (kept[at, lanes] + in1[0, at, lanes].astype(f32)).astype(bf16)
            z_copy(h, t).start()
    out1[1] = product(2 * zl + 1 - core).astype(bf16)
    core_copy(1).start()
    kept[...] = product(2 * zl + core)
    core_copy(1).wait_recv()

    share = 16 * SUB // 2

    def to_x(h, d):
        n = 3 * h + d - 1
        return pltpu.make_async_remote_copy(
            src_ref=pbuf.at[h, pl.ds(pl.multiple_of(ring(x, d) * share, share), share), :],
            dst_ref=xbuf.at[n], send_sem=x_send.at[n], recv_sem=x_recv.at[n],
            device_id=at_ctx(ring(x, d), zh, y), device_id_type=MESH,
        )

    for h in range(2):
        lanes = slice(h * LANES, (h + 1) * LANES)
        highs, lows = [], []
        for t in range(2):
            at = pl.ds(t * 2 * rows, 2 * rows)
            z_copy(h, t).wait_recv()
            scores = kept[at, lanes] + in1[1, at, lanes].astype(f32) + zin[h, at, :].astype(f32)
            active = jnp.maximum(scores, 0.0) + jnp.log1p(jnp.exp(-jnp.abs(scores)))
            highs.append(active.astype(bf16))
            lows.append((active - highs[-1].astype(f32)).astype(bf16))
        halves = jnp.concatenate(
            [jnp.concatenate(highs, axis=0), jnp.concatenate(lows, axis=0)], axis=1
        )
        sums = jnp.dot(member[...], halves, preferred_element_type=f32)
        pbuf[h] = (sums[:, :LANES] + sums[:, LANES:]) / scale[...]
        for d in range(1, 4):
            to_x(h, d).start()
    for h in range(2):
        mine = pbuf[h, pl.ds(pl.multiple_of(x * share, share), share), :]
        for d in range(1, 4):
            to_x(h, d).wait_recv()
            mine = mine + xbuf[3 * h + d - 1]
        abuf[pl.ds(h, share, stride=2), :] = mine

    def tile_at(cz, cy):
        return pl.ds(pl.multiple_of((cz * 4 + cy) * SUB, SUB), SUB)

    def to_owner(d, carry):
        cz, cy = ring(zh, lax.div(d, 4)), ring(y, lax.rem(d, 4))
        pltpu.make_async_remote_copy(
            src_ref=abuf.at[tile_at(cz, cy), :], dst_ref=rbuf.at[tile_at(zh, y), :],
            send_sem=a_send, recv_sem=a_recv, device_id=plane(d), device_id_type=MESH,
        ).start()
        return carry

    lax.fori_loop(1, 16, to_owner, 0)
    rbuf[tile_at(zh, y), :] = abuf[tile_at(zh, y), :]
    most = pl.ds(0, 15 * SUB)
    all_of = pltpu.make_async_remote_copy(
        src_ref=abuf.at[most, :], dst_ref=rbuf.at[most, :], send_sem=a_send, recv_sem=a_recv,
        device_id=plane(1), device_id_type=MESH,
    )
    all_of.wait_recv()
    for q in range(4):
        acc = rbuf[pl.ds(q * SUB, SUB), :]
        for m in range(1, 4):
            acc = acc + rbuf[pl.ds((4 * m + q) * SUB, SUB), :]
        obuf[pl.ds(q * SUB, SUB), :] = acc
        obuf[pl.ds((4 + q) * SUB, SUB), :] = pltpu.roll(acc, LANES // 2, 1)
    count = out_ref.shape[0]
    left = iota((count, LANES), 1) < LANES // 2
    for hz in range(2):
        for q in range(2):
            plain = [obuf[pl.ds((2 * q + n) * SUB + hz, count, stride=2), :] for n in range(2)]
            moved = [obuf[pl.ds((4 + 2 * q + n) * SUB + hz, count, stride=2), :] for n in range(2)]
            for b in range(2):
                pair = (plain[0], moved[1]) if b == 0 else (moved[0], plain[1])
                lane = ((2 * hz + b) * 2 + q) * LANES
                out_ref[:, lane : lane + LANES] = jnp.where(left, *pair)

    all_of.wait_send()
    for name in sent:
        w_copy(name, *sent[name]).wait_send()

    def s_drain(k, carry):
        for kind in range(3):
            s_copy(k, kind, s_rows(y, k), yp).wait_send()
        return carry

    lax.fori_loop(0, parts, s_drain, 0)
    for d in range(1, 4):
        power_copy(d, pw.at[ch]).wait_send()
        to_x(0, d).wait_send()
        to_x(1, d).wait_send()
    token_copy(0, after).wait_send()
    token_copy(2, before).wait_send()
    core_copy(0).wait_send()
    core_copy(1).wait_send()
    for n in range(4):
        z_copy(n // 2, n % 2).wait_send()


def body(tokens, complement, seg_lengths, owner, embed, norm_gain, taps, w_out):
    rows = tokens.shape[0]
    vocab, width = embed.shape
    cols = w_out.shape[1]
    segs = seg_lengths.shape[0]
    per_block = segs // owner.shape[0]
    total, group = 4 * rows, 4 * cols
    vmem = pl.BlockSpec(memory_space=pltpu.VMEM)
    hbm = pl.BlockSpec(memory_space=pl.ANY)

    def tiles(count, dtype=f32):
        return pltpu.VMEM((count * SUB, LANES), dtype)

    def sems(count):
        return pltpu.SemaphoreType.DMA((count,))

    return pl.pallas_call(
        score_kernel,
        out_shape=jax.ShapeDtypeStruct((per_block, width), f32),
        in_specs=[vmem] * 5 + [hbm] * 3,
        out_specs=vmem,
        scratch_shapes=[
            pltpu.VMEM((vocab, width), bf16),
            pltpu.VMEM((taps.shape[0], width), f32),
            pltpu.VMEM((total, width), bf16),
            pltpu.VMEM((16 * cols, width), bf16),
            pltpu.VMEM((2, total, group), bf16),
            pltpu.VMEM((2, total, group), bf16),
            pltpu.VMEM((2, total, LANES), bf16),
            pltpu.VMEM((2, total, LANES), bf16),
            pltpu.VMEM((total, group), f32),
            pltpu.VMEM((2, segs, LANES), f32),
            pltpu.VMEM((6, 8 * SUB, LANES), f32),
            tiles(16),
            tiles(16),
            tiles(8),
            pltpu.VMEM((segs, total), bf16),
            pltpu.VMEM((segs, LANES), f32),
            pltpu.VMEM((3, SUB, rows), jnp.int32),
            pltpu.VMEM((4, SUB, vocab), f32),
            tiles(1),
        ]
        + [tiles(2 * rows)] * 4
        + [tiles(TAPROWS)] * 4
        + [tiles(rows, jnp.int32)] * 2
        + [tiles(rows)]
        + [sems(3), sems(30), sems(30), sems(24), sems(24), sems(2), sems(2), sems(4), sems(4)]
        + [sems(6), sems(6), pltpu.SemaphoreType.DMA, pltpu.SemaphoreType.DMA]
        + [sems(2), sems(2), sems(3), sems(3)],
        compiler_params=pltpu.CompilerParams(
            vmem_limit_bytes=56 << 20, collective_id=0, has_side_effects=True
        ),
    )(
        tokens[None, :], complement[None, :], seg_lengths[None, :], owner[None, :],
        norm_gain[None, :], embed, taps, w_out.T,
    )


def solution(mesh):
    in_specs = (P("ctx"), P(), P(), P(), P(None, "ch"), P("ch"), P(None, "ch"), P("ch", "ctx"))
    out_specs = P("ctx", "ch")
    return jax.shard_map(body, mesh=mesh, in_specs=in_specs, out_specs=out_specs, check_vma=False)
```

```python
import jax
import jax.numpy as jnp
from jax import lax
from jax.experimental import pallas as pl
from jax.experimental.pallas import tpu as pltpu
from jax.sharding import PartitionSpec as P

norm_eps = 1e-06
LANES = 128
SUB = 8
PAD = 8
SPAN = 128
TAPROWS = 152
BASE = 143
MESH = pl.DeviceIdType.MESH
f32 = jnp.float32
bf16 = jnp.bfloat16


def rows3(ref, k, n):
    return ref[pl.ds(pl.multiple_of(k * SUB, SUB), n * SUB), :].reshape(n, SUB, LANES)

def put3(ref, k, v):
    n = v.shape[0]
    ref[pl.ds(pl.multiple_of(k * SUB, SUB), n * SUB), :] = v.reshape(n * SUB, LANES)

def prep_taps(taps_ref, tv, dv, tr, dr):
    span = taps_ref.shape[0]
    edge = jnp.zeros((PAD * SUB, LANES), jnp.float32)
    tv[pl.ds(0, PAD * SUB), :] = edge
    for e in range(2):
        tv[pl.ds((PAD + span + 8 * e) * SUB, 8 * SUB), :] = edge
    for s in range(SUB):
        tv[pl.ds(PAD * SUB + s, span, stride=SUB), :] = taps_ref[:, s * LANES:(s + 1) * LANES]
    dv[pl.ds(0, PAD * SUB), :] = edge
    dv[pl.ds(PAD * SUB, (TAPROWS - PAD) * SUB), :] = (
        tv[pl.ds(0, (TAPROWS - PAD) * SUB), :] - tv[pl.ds(PAD * SUB, (TAPROWS - PAD) * SUB), :])
    def flip(k8, carry):
        for u in range(8):
            k = k8 * 8 + u
            put3(tr, TAPROWS - 1 - k, rows3(tv, k, 1))
            put3(dr, TAPROWS - 1 - k, rows3(dv, k, 1))
        return carry
    lax.fori_loop(0, TAPROWS // 8, flip, 0)

def conv_block(i, count, ext_f, ext_r, tv, dv, tr, dr, sv, ev, res):
    p0 = i * 16
    zero8 = jnp.zeros((8, SUB, LANES), jnp.float32)
    idx16 = lax.broadcasted_iota(jnp.int32, (16, SUB, LANES), 0)
    far_lags = SPAN // 16
    s0 = rows3(sv, p0, 1)
    e0 = rows3(ev, p0 + 15, 1)

    def fwd_far(j, acc):
        lag = j * 16
        q0 = p0 - lag
        rows = jnp.where(idx16 >= s0 - q0, rows3(ext_f, count + q0, 16), 0.0)
        x0, x1 = rows[:8], rows[8:]
        xs = x0 + x1
        a, b, c = acc
        for u in range(8):
            a = a + rows3(tv, PAD + lag - u, 8) * xs[u:u + 1]
            b = b + rows3(dv, PAD + lag - u, 8) * x1[u:u + 1]
            c = c + rows3(dv, PAD + 8 + lag - u, 8) * x0[u:u + 1]
        return a, b, c

    def rev_far(j, acc):
        lag = j * 16
        q0 = p0 + lag
        rows = jnp.where(idx16 < e0 - q0, rows3(ext_r, q0, 16), 0.0)
        x0, x1 = rows[:8], rows[8:]
        xs = x0 + x1
        a, b, c = acc
        for u in range(8):
            a = a + rows3(tr, BASE - lag - u, 8) * xs[u:u + 1]
            b = b + rows3(dr, BASE - lag - u, 8) * x0[u:u + 1]
            c = c + rows3(dr, BASE - 8 - lag - u, 8) * x1[u:u + 1]
        return a, b, c

    def part(value, lo, term):
        pieces = [value[:lo], value[lo : lo + term.shape[0]] + term, value[lo + term.shape[0] :]]
        return jnp.concatenate([piece for piece in pieces if piece.shape[0]], axis=0)

    a, b, c = lax.fori_loop(1, far_lags, fwd_far, (zero8,) * 3, unroll=7)
    far_f = [a + b, a - c]
    rows = jnp.where(idx16 >= s0 - (p0 - SPAN), rows3(ext_f, count + p0 - SPAN, 16), 0.0)
    for u in range(8):
        far_f[0] = far_f[0] + rows3(tv, PAD + SPAN - 8 - u, 8) * rows[8 + u : 9 + u]
        if u:
            tap = rows3(tv, PAD + SPAN - u, u)
            far_f[0] = part(far_f[0], 0, tap * rows[u : u + 1])
            far_f[1] = part(far_f[1], 0, tap * rows[8 + u : 9 + u])
    a, b, c = lax.fori_loop(1, far_lags, rev_far, (zero8,) * 3, unroll=7)
    far_r = [a - c, a + b]
    rows = jnp.where(idx16 < e0 - (p0 + SPAN), rows3(ext_r, p0 + SPAN, 16), 0.0)
    for u in range(8):
        far_r[1] = far_r[1] + rows3(tr, BASE - SPAN + 8 - u, 8) * rows[u : u + 1]
        if u < 7:
            tap = rows3(tr, BASE - SPAN + 1, 7 - u)
            far_r[0] = part(far_r[0], u + 1, tap * rows[u : u + 1])
            far_r[1] = part(far_r[1], u + 1, tap * rows[8 + u : 9 + u])
    xf = (rows3(ext_f, count + p0, 8), rows3(ext_f, count + p0 + 8, 8))
    xr = (rows3(ext_r, p0, 8), rows3(ext_r, p0 + 8, 8))
    idx8 = lax.broadcasted_iota(jnp.int32, (8, SUB, LANES), 0)
    mid = rows3(sv, p0 + 8, 1)
    m = jnp.where(idx8 >= mid - p0, xf[0], 0.0)
    mid_f = zero8
    for u in range(8):
        mid_f = mid_f + rows3(tv, PAD + 8 - u, 8) * m[u:u + 1]
    mid = rows3(ev, p0 + 7, 1)
    m = jnp.where(idx8 < mid - p0 - 8, xr[1], 0.0)
    mid_r = zero8
    for u in range(8):
        mid_r = mid_r + rows3(tr, BASE - 8 - u, 8) * m[u:u + 1]
    for h in range(2):
        pb = p0 + 8 * h
        start = rows3(sv, pb, 8)
        end = rows3(ev, pb, 8)
        mix_f = jnp.where(start < p0, far_f[h], 0.0)
        mix_r = jnp.where(end > p0 + 16, far_r[h], 0.0)
        if h == 1:
            mix_f = mix_f + jnp.where(start < pb, mid_f, 0.0)
        else:
            mix_r = mix_r + jnp.where(end > pb + 8, mid_r, 0.0)
        near_f = [rows3(tv, PAD + d, 1) for d in range(8)]
        sums_f, sums_r = [], []
        for r in range(8):
            sum_f, sum_r = mix_f[r : r + 1], mix_r[r : r + 1]
            for u in range(8):
                if u < r:
                    term = near_f[r - u] * xf[h][u : u + 1]
                    sum_f = sum_f + jnp.where(start[r : r + 1] <= pb + u, term, 0.0)
                elif u > r:
                    term = near_f[u - r] * xr[h][u : u + 1]
                    sum_r = sum_r + jnp.where(end[r : r + 1] > pb + u, term, 0.0)
            sums_f.append(sum_f + near_f[0] * xf[h][r : r + 1])
            sums_r.append(sum_r + near_f[0] * xr[h][r : r + 1])
        mix_f = jnp.concatenate(sums_f, axis=0)
        mix_r = jnp.concatenate(sums_r, axis=0)
        gated_f = (xf[h] * mix_f).astype(jnp.bfloat16).astype(jnp.float32)
        gated_r = (xr[h] * mix_r).astype(jnp.bfloat16).astype(jnp.float32)
        put3(res, pb, (gated_f + gated_r) * 0.5)


def score_kernel(tok_ref, comp_ref, lens_ref, owner_ref, gain_ref, embed_hbm, taps_hbm, w_hbm,
                 out_ref, embed_ref, taps_ref, sbuf, wbuf, out1, in1, zout, zin, kept,
                 pbuf, xbuf, abuf, rbuf, obuf, member, scale, tk, pw, gain8,
                 ext_f, ext_r, inv_f, inv_r, tv, dv, tr, dr, sv, ev, res,
                 l_sem, w_send, w_recv, s_send, s_recv, r_send, r_recv, z_send, z_recv,
                 x_send, x_recv, a_send, a_recv, t_send, t_recv, p_send, p_recv):
    me = lax.axis_index("ctx")
    ch = lax.axis_index("ch")
    peers = lax.axis_size("ctx")
    y = lax.rem(me, 4)
    zh = lax.rem(lax.div(me, 4), 4)
    x = lax.div(me, 16)
    zl = lax.div(ch, 2)
    core = lax.rem(ch, 2)

    def ring(v, by):
        return lax.rem(v + by, 4)

    def at_ctx(cx, cz, cy):
        return {"ctx": cx * 16 + cz * 4 + cy}

    xp, xm, x2 = ring(x, 1), ring(x, 3), ring(x, 2)
    zp, zm, z2 = ring(zh, 1), ring(zh, 3), ring(zh, 2)
    yp, ym, y2 = ring(y, 1), ring(y, 3), ring(y, 2)
    core_peer = zl * 2 + 1 - core
    z_peer = (1 - zl) * 2 + core
    after, before = lax.rem(me + 1, peers), lax.rem(me + peers - 1, peers)

    barrier = pltpu.get_barrier_semaphore()

    def greet(to):
        pl.semaphore_signal(barrier, inc=1, device_id=to, device_id_type=MESH)

    for d in range(1, 4):
        greet({"ch": lax.rem(ch + d, 4)})
        greet(at_ctx(ring(x, d), zh, y))
    greet({"ctx": after})
    greet({"ctx": before})

    def plane(d):
        return at_ctx(x, ring(zh, lax.div(d, 4)), ring(y, lax.rem(d, 4)))

    def hello(d, carry):
        greet(plane(d))
        return carry

    lax.fori_loop(1, 16, hello, 0)

    cols = w_hbm.shape[0]
    half = cols // 2
    rows = sbuf.shape[0] // 4
    vocab, width = embed_ref.shape
    segs = lens_ref.shape[1]
    own_w = wbuf.at[pl.ds(pl.multiple_of((x * 4 + zh) * cols, cols), cols), :]
    fetch = [
        pltpu.make_async_copy(embed_hbm, embed_ref, l_sem.at[0]),
        pltpu.make_async_copy(w_hbm, own_w, l_sem.at[1]),
        pltpu.make_async_copy(taps_hbm, taps_ref, l_sem.at[2]),
    ]
    for copy in fetch:
        copy.start()

    def iota(shape, dim):
        return lax.broadcasted_iota(jnp.int32, shape, dim)

    lens = jnp.broadcast_to(lens_ref[...], (SUB, segs)).astype(f32)
    upto = (iota((segs, segs), 0) <= iota((segs, segs), 1)).astype(bf16)
    ends_row = jnp.dot(lens.astype(bf16), upto, preferred_element_type=f32)
    starts_row = (ends_row - lens)[0:1]
    ends_row = ends_row[0:1]
    letters = iota((rows, vocab), 1)

    def ids_of(slot):
        return tk[slot].astype(f32).T[:, 0:1].astype(jnp.int32)

    def other_of(ids):
        hit = jnp.where(letters == ids, comp_ref[...].astype(f32), 0.0)
        return jnp.sum(hit, axis=1, keepdims=True).astype(jnp.int32)

    def pick_rows(ids_a, ids_b, put_a, put_b):
        picks = jnp.concatenate([letters == ids_a, letters == ids_b], axis=0)
        picks = picks.astype(f32).astype(bf16)
        for n in range(width // (2 * LANES)):
            table = embed_ref[:, n * 2 * LANES : (n + 1) * 2 * LANES]
            found = jnp.dot(picks, table, preferred_element_type=f32)
            for m in range(2):
                lanes = slice(m * LANES, (m + 1) * LANES)
                for ref, at, part in (put_a + (found[:rows],), put_b + (found[rows:],)):
                    ref[pl.ds(at * SUB + 2 * n + m, rows, stride=SUB), :] = part[:, lanes]

    tk[1] = jnp.broadcast_to(tok_ref[...], (SUB, rows))
    own_ids = ids_of(1)
    own_other = other_of(own_ids)

    fetch[0].wait()
    fold = jnp.zeros((vocab, LANES), f32)
    for s in range(SUB):
        piece = embed_ref[:, s * LANES : (s + 1) * LANES].astype(f32)
        fold = fold + piece * piece
        gain8[s : s + 1, :] = gain_ref[:, s * LANES : (s + 1) * LANES]
    pw[ch] = jnp.broadcast_to(jnp.sum(fold.T, axis=0, keepdims=True), (SUB, vocab))
    fetch[1].wait()

    def w_rows(cx, cz, h=None):
        lo, count = (0, cols) if h is None else (h * half, half)
        return wbuf.at[pl.ds(pl.multiple_of((cx * 4 + cz) * cols + lo, half), count), :]

    z_of = (zh, zm, zp, z2)
    plus, minus = at_ctx(xp, zh, y), at_ctx(xm, zh, y)
    up, down = at_ctx(x, zp, y), at_ctx(x, zm, y)
    sent, got = {}, {}
    for h in range(2):
        own = w_rows(x, zh, h)
        sent["z", h, 0], got["z", h, 0] = (own, up), w_rows(x, zm, h)
        sent["z", h, 1], got["z", h, 1] = (own, down), w_rows(x, zp, h)
        for dz in range(4):
            here = w_rows(x, z_of[dz], h)
            sent["x", dz, h, 0], got["x", dz, h, 0] = (here, plus), w_rows(xm, z_of[dz], h)
            sent["x", dz, h, 1], got["x", dz, h, 1] = (here, minus), w_rows(xp, z_of[dz], h)
    sent["y", 0], got["y", 0] = (w_rows(x, zm, 0), up), w_rows(x, z2, 0)
    sent["y", 1], got["y", 1] = (w_rows(x, zp, 1), down), w_rows(x, z2, 1)
    for dz in range(4):
        sent["r", dz, 0], got["r", dz, 0] = (w_rows(xm, z_of[dz], 0), plus), w_rows(x2, z_of[dz], 0)
        sent["r", dz, 1], got["r", dz, 1] = (w_rows(xp, z_of[dz], 1), minus), w_rows(x2, z_of[dz], 1)
    number = {name: n for n, name in enumerate(sent)}

    def w_copy(name, ref, to):
        n = number[name]
        return pltpu.make_async_remote_copy(
            src_ref=ref, dst_ref=ref, send_sem=w_send.at[n], recv_sem=w_recv.at[n],
            device_id=to, device_id_type=MESH,
        )

    seen = set()

    def w_start(*names):
        for name in names:
            w_copy(name, *sent[name]).start()

    def w_wait(*names):
        for name in names:
            seen.add(name)
            w_copy(name, got[name], plus).wait_recv()

    def both(dz, h):
        w_start(("x", dz, h, 0), ("x", dz, h, 1))

    def relay(dz):
        w_wait(("x", dz, 0, 0))
        w_start(("r", dz, 0))
        w_wait(("x", dz, 1, 1))
        w_start(("r", dz, 1))

    def step_a():
        w_wait(("z", 0, 0))
        both(1, 0)
        w_start(("y", 0))
        w_wait(("z", 0, 1))
        both(2, 0)

    def step_b():
        w_wait(("z", 1, 1))
        w_start(("y", 1))
        both(2, 1)
        w_wait(("z", 1, 0))
        both(1, 1)

    def step_c():
        w_wait(("y", 0))
        both(3, 0)
        w_wait(("y", 1))
        both(3, 1)

    def token_copy(slot, to):
        return pltpu.make_async_remote_copy(
            src_ref=tk.at[1], dst_ref=tk.at[slot], send_sem=t_send.at[slot // 2],
            recv_sem=t_recv.at[slot // 2], device_id={"ctx": to}, device_id_type=MESH,
        )

    def power_copy(d, ref):
        return pltpu.make_async_remote_copy(
            src_ref=ref, dst_ref=ref, send_sem=p_send.at[d - 1], recv_sem=p_recv.at[d - 1],
            device_id={"ch": lax.rem(ch + d, 4)}, device_id_type=MESH,
        )

    pl.semaphore_wait(barrier, 23)
    token_copy(0, after).start()
    token_copy(2, before).start()
    for d in range(1, 4):
        power_copy(d, pw.at[ch]).start()
    w_start(("z", 0, 0), ("z", 0, 1))
    both(0, 0)
    both(0, 1)
    w_start(("z", 1, 0), ("z", 1, 1))

    pick_rows(own_ids, own_other, (ext_f, rows), (ext_r, 0))
    first = me * rows
    pos = (iota((rows, segs), 0) + first).astype(f32)
    start_col = jnp.max(jnp.where(starts_row <= pos, starts_row, 0.0), axis=1, keepdims=True)
    end_col = jnp.min(jnp.where(ends_row > pos, ends_row, 1e9), axis=1, keepdims=True)
    start_col = jnp.broadcast_to(start_col, (rows, LANES)).astype(jnp.int32) - first
    end_col = jnp.broadcast_to(end_col, (rows, LANES)).astype(jnp.int32) - first
    for s in range(SUB):
        sv[pl.ds(s, rows, stride=SUB), :] = start_col
        ev[pl.ds(s, rows, stride=SUB), :] = end_col
    fetch[2].wait()
    prep_taps(taps_ref, tv, dv, tr, dr)

    token_copy(0, after).wait_recv()
    token_copy(2, before).wait_recv()
    last_ids = ids_of(0)
    next_other = other_of(ids_of(2))
    pick_rows(last_ids, next_other, (ext_f, 0), (ext_r, rows))

    for d in range(1, 4):
        power_copy(d, pw.at[lax.rem(ch + 4 - d, 4)]).wait_recv()
    power = (pw[0] + pw[1]) + (pw[2] + pw[3])
    inv_row = lax.rsqrt(power / (4 * width) + norm_eps)[0:1]
    for ref, at, ids in (
        (inv_f, 0, last_ids), (inv_f, rows, own_ids), (inv_r, 0, own_other), (inv_r, rows, next_other),
    ):
        col = jnp.sum(jnp.where(letters == ids, inv_row, 0.0), axis=1, keepdims=True)
        col = jnp.broadcast_to(col, (rows, LANES))
        for s in range(SUB):
            ref[pl.ds(at * SUB + s, rows, stride=SUB), :] = col

    def scale_rows(i, carry):
        for ext, inv in ((ext_f, inv_f), (ext_r, inv_r)):
            value = rows3(ext, i * 16, 16) * rows3(inv, i * 16, 16) * gain8[...][None]
            put3(ext, i * 16, value.astype(bf16).astype(f32))
        return carry

    lax.fori_loop(0, 2 * rows // 16, scale_rows, 0)
    relay(0)

    chunk = 16
    parts = rows // chunk

    def s_rows(cy, k):
        return sbuf.at[pl.ds(pl.multiple_of(cy * rows + k * chunk, chunk), chunk), :]

    def s_copy(k, kind, ref, cy):
        return pltpu.make_async_remote_copy(
            src_ref=ref, dst_ref=ref, send_sem=s_send.at[3 * k + kind],
            recv_sem=s_recv.at[3 * k + kind], device_id=at_ctx(x, zh, cy), device_id_type=MESH,
        )

    steps = {0: step_a, 2: step_b, 4: step_c, 6: lambda: relay(2), 7: lambda: relay(1)}

    def sixteen(i, carry):
        conv_block(i, rows, ext_f, ext_r, tv, dv, tr, dr, sv, ev, res)
        at = pl.ds(pl.multiple_of(y * rows + i * chunk, chunk), chunk)
        for s in range(SUB):
            block = res[pl.ds(i * chunk * SUB + s, chunk, stride=SUB), :]
            sbuf[at, s * LANES : (s + 1) * LANES] = block.astype(bf16)
        s_copy(i, 0, s_rows(y, i), yp).start()
        s_copy(i, 1, s_rows(y, i), ym).start()

        s_copy(i, 2, s_rows(y, i), y2).start()
        for when, step in steps.items():
            pl.when(i == when)(step)
        return carry

    lax.fori_loop(0, parts, sixteen, 0)

    blocks = owner_ref.shape[1]
    spread = ((iota((blocks, segs), 1) >> 2) == iota((blocks, segs), 0)).astype(bf16)
    owners = jnp.broadcast_to(owner_ref[...], (SUB, blocks)).astype(f32).astype(bf16)
    owner_row = jnp.dot(owners, spread, preferred_element_type=f32)[0:1].astype(jnp.int32)
    slot, seg = iota((segs, segs), 0), iota((segs, segs), 1)
    same = (owner_row == (slot >> 2)) & ((slot & 3) == (seg & 3))
    slot_start = jnp.sum(jnp.where(same, starts_row, 0.0), axis=1, keepdims=True)
    slot_end = jnp.sum(jnp.where(same, ends_row, 0.0), axis=1, keepdims=True)
    total = 4 * rows
    spot = (iota((segs, total), 1) + lax.div(me, 4) * total).astype(f32)
    member[...] = ((slot_start <= spot) & (spot < slot_end)).astype(f32).astype(bf16)
    scale[...] = jnp.broadcast_to(slot_end - slot_start, (segs, LANES))

    relay(3)

    def s_finish(k, carry):
        for kind, cy in enumerate((ym, yp, y2)):
            s_copy(k, kind, s_rows(cy, k), yp).wait_recv()
        return carry

    lax.fori_loop(0, parts, s_finish, 0)
    w_wait(*[name for name in got if name not in seen])

    group = 4 * cols

    def product(g, h):
        rhs = wbuf[pl.ds(pl.multiple_of(g * group + h * LANES, LANES), LANES), :]
        return lax.dot_general(
            sbuf[...], rhs, (((1,), (1,)), ((), ())), preferred_element_type=f32
        )

    def core_copy(n):
        return pltpu.make_async_remote_copy(
            src_ref=out1.at[n], dst_ref=in1.at[n], send_sem=r_send.at[n],
            recv_sem=r_recv.at[n], device_id={"ch": core_peer}, device_id_type=MESH,
        )

    def z_copy(h, t):
        at = pl.ds(t * 2 * rows, 2 * rows)
        return pltpu.make_async_remote_copy(
            src_ref=zout.at[h, at, :], dst_ref=zin.at[h, at, :], send_sem=z_send.at[2 * h + t],
            recv_sem=z_recv.at[2 * h + t], device_id={"ch": z_peer}, device_id_type=MESH,
        )

    for h in range(2):
        out1[h] = product(2 * (1 - zl) + 1 - core, h).astype(bf16)
        core_copy(h).start()
    for h in range(2):
        kept[h] = product(2 * (1 - zl) + core, h)
        core_copy(h).wait_recv()
        for t in range(2):
            at = pl.ds(t * 2 * rows, 2 * rows)
            zout[h, at, :] = (kept[h, at, :] + in1[h, at, :].astype(f32)).astype(bf16)
            z_copy(h, t).start()
    for h in range(2):
        out1[2 + h] = product(2 * zl + 1 - core, h).astype(bf16)
        core_copy(2 + h).start()
    for h in range(2):
        kept[h] = product(2 * zl + core, h)

    share = 16 * SUB // 2

    def to_x(h, d):
        n = 3 * h + d - 1
        return pltpu.make_async_remote_copy(
            src_ref=pbuf.at[h, pl.ds(pl.multiple_of(ring(x, d) * share, share), share), :],
            dst_ref=xbuf.at[n], send_sem=x_send.at[n], recv_sem=x_recv.at[n],
            device_id=at_ctx(ring(x, d), zh, y), device_id_type=MESH,
        )

    for h in range(2):
        highs, lows = [], []
        core_copy(2 + h).wait_recv()
        for t in range(2):
            at = pl.ds(t * 2 * rows, 2 * rows)
            z_copy(h, t).wait_recv()
            scores = kept[h, at, :] + in1[2 + h, at, :].astype(f32) + zin[h, at, :].astype(f32)
            active = jnp.maximum(scores, 0.0) + jnp.log1p(jnp.exp(-jnp.abs(scores)))
            highs.append(active.astype(bf16))
            lows.append((active - highs[-1].astype(f32)).astype(bf16))
        halves = jnp.concatenate(
            [jnp.concatenate(highs, axis=0), jnp.concatenate(lows, axis=0)], axis=1
        )
        sums = jnp.dot(member[...], halves, preferred_element_type=f32)
        pbuf[h] = (sums[:, :LANES] + sums[:, LANES:]) / scale[...]
        for d in range(1, 4):
            to_x(h, d).start()
    for h in range(2):
        mine = pbuf[h, pl.ds(pl.multiple_of(x * share, share), share), :]
        for d in range(1, 4):
            to_x(h, d).wait_recv()
            mine = mine + xbuf[3 * h + d - 1]
        abuf[pl.ds(h, share, stride=2), :] = mine

    def tile_at(cz, cy):
        return pl.ds(pl.multiple_of((cz * 4 + cy) * SUB, SUB), SUB)

    def to_owner(d, carry):
        cz, cy = ring(zh, lax.div(d, 4)), ring(y, lax.rem(d, 4))
        pltpu.make_async_remote_copy(
            src_ref=abuf.at[tile_at(cz, cy), :], dst_ref=rbuf.at[tile_at(zh, y), :],
            send_sem=a_send, recv_sem=a_recv, device_id=plane(d), device_id_type=MESH,
        ).start()
        return carry

    lax.fori_loop(1, 16, to_owner, 0)
    rbuf[tile_at(zh, y), :] = abuf[tile_at(zh, y), :]
    most = pl.ds(0, 15 * SUB)
    all_of = pltpu.make_async_remote_copy(
        src_ref=abuf.at[most, :], dst_ref=rbuf.at[most, :], send_sem=a_send, recv_sem=a_recv,
        device_id=plane(1), device_id_type=MESH,
    )
    all_of.wait_recv()
    for q in range(4):
        acc = rbuf[pl.ds(q * SUB, SUB), :]
        for m in range(1, 4):
            acc = acc + rbuf[pl.ds((4 * m + q) * SUB, SUB), :]
        obuf[pl.ds(q * SUB, SUB), :] = acc
        obuf[pl.ds((4 + q) * SUB, SUB), :] = pltpu.roll(acc, LANES // 2, 1)
    count = out_ref.shape[0]
    left = iota((count, LANES), 1) < LANES // 2
    for hz in range(2):
        for q in range(2):
            plain = [obuf[pl.ds((2 * q + n) * SUB + hz, count, stride=2), :] for n in range(2)]
            moved = [obuf[pl.ds((4 + 2 * q + n) * SUB + hz, count, stride=2), :] for n in range(2)]
            for b in range(2):
                pair = (plain[0], moved[1]) if b == 0 else (moved[0], plain[1])
                lane = ((2 * hz + b) * 2 + q) * LANES
                out_ref[:, lane : lane + LANES] = jnp.where(left, *pair)

    all_of.wait_send()
    for name in sent:
        w_copy(name, *sent[name]).wait_send()

    def s_drain(k, carry):
        for kind in range(3):
            s_copy(k, kind, s_rows(y, k), yp).wait_send()
        return carry

    lax.fori_loop(0, parts, s_drain, 0)
    for d in range(1, 4):
        power_copy(d, pw.at[ch]).wait_send()
        to_x(0, d).wait_send()
        to_x(1, d).wait_send()
    token_copy(0, after).wait_send()
    token_copy(2, before).wait_send()
    for n in range(4):
        core_copy(n).wait_send()
        z_copy(n // 2, n % 2).wait_send()


def body(tokens, complement, seg_lengths, owner, embed, norm_gain, taps, w_out):
    rows = tokens.shape[0]
    vocab, width = embed.shape
    cols = w_out.shape[1]
    segs = seg_lengths.shape[0]
    per_block = segs // owner.shape[0]
    total, group = 4 * rows, 4 * cols
    vmem = pl.BlockSpec(memory_space=pltpu.VMEM)
    hbm = pl.BlockSpec(memory_space=pl.ANY)

    def tiles(count, dtype=f32):
        return pltpu.VMEM((count * SUB, LANES), dtype)

    def sems(count):
        return pltpu.SemaphoreType.DMA((count,))

    return pl.pallas_call(
        score_kernel,
        out_shape=jax.ShapeDtypeStruct((per_block, width), f32),
        in_specs=[vmem] * 5 + [hbm] * 3,
        out_specs=vmem,
        scratch_shapes=[
            pltpu.VMEM((vocab, width), bf16),
            pltpu.VMEM((taps.shape[0], width), f32),
            pltpu.VMEM((total, width), bf16),
            pltpu.VMEM((16 * cols, width), bf16),
            pltpu.VMEM((4, total, LANES), bf16),
            pltpu.VMEM((4, total, LANES), bf16),
            pltpu.VMEM((2, total, LANES), bf16),
            pltpu.VMEM((2, total, LANES), bf16),
            pltpu.VMEM((2, total, LANES), f32),
            pltpu.VMEM((2, segs, LANES), f32),
            pltpu.VMEM((6, 8 * SUB, LANES), f32),
            tiles(16),
            tiles(16),
            tiles(8),
            pltpu.VMEM((segs, total), bf16),
            pltpu.VMEM((segs, LANES), f32),
            pltpu.VMEM((3, SUB, rows), jnp.int32),
            pltpu.VMEM((4, SUB, vocab), f32),
            tiles(1),
        ]
        + [tiles(2 * rows)] * 4
        + [tiles(TAPROWS)] * 4
        + [tiles(rows, jnp.int32)] * 2
        + [tiles(rows)]
        + [sems(3), sems(30), sems(30), sems(24), sems(24), sems(4), sems(4), sems(4), sems(4)]
        + [sems(6), sems(6), pltpu.SemaphoreType.DMA, pltpu.SemaphoreType.DMA]
        + [sems(2), sems(2), sems(3), sems(3)],
        compiler_params=pltpu.CompilerParams(
            vmem_limit_bytes=56 << 20, collective_id=0, has_side_effects=True
        ),
    )(
        tokens[None, :], complement[None, :], seg_lengths[None, :], owner[None, :],
        norm_gain[None, :], embed, taps, w_out.T,
    )


def solution(mesh):
    in_specs = (P("ctx"), P(), P(), P(), P(None, "ch"), P("ch"), P(None, "ch"), P("ch", "ctx"))
    out_specs = P("ctx", "ch")
    return jax.shard_map(body, mesh=mesh, in_specs=in_specs, out_specs=out_specs, check_vma=False)
```

```python
import jax
import jax.numpy as jnp
from jax import lax
from jax.experimental import pallas as pl
from jax.experimental.pallas import tpu as pltpu
from jax.sharding import PartitionSpec as P

norm_eps = 1e-06
LANES = 128
SUB = 8
PAD = 8
SPAN = 128
TAPROWS = 152
BASE = 143
MESH = pl.DeviceIdType.MESH
f32 = jnp.float32
bf16 = jnp.bfloat16


def rows3(ref, k, n):
    return ref[pl.ds(pl.multiple_of(k * SUB, SUB), n * SUB), :].reshape(n, SUB, LANES)

def put3(ref, k, v):
    n = v.shape[0]
    ref[pl.ds(pl.multiple_of(k * SUB, SUB), n * SUB), :] = v.reshape(n * SUB, LANES)

def prep_taps(taps_ref, tv, dv, tr, dr):
    span = taps_ref.shape[0]
    edge = jnp.zeros((PAD * SUB, LANES), jnp.float32)
    tv[pl.ds(0, PAD * SUB), :] = edge
    for e in range(2):
        tv[pl.ds((PAD + span + 8 * e) * SUB, 8 * SUB), :] = edge
    for s in range(SUB):
        tv[pl.ds(PAD * SUB + s, span, stride=SUB), :] = taps_ref[:, s * LANES:(s + 1) * LANES]
    dv[pl.ds(0, PAD * SUB), :] = edge
    dv[pl.ds(PAD * SUB, (TAPROWS - PAD) * SUB), :] = (
        tv[pl.ds(0, (TAPROWS - PAD) * SUB), :] - tv[pl.ds(PAD * SUB, (TAPROWS - PAD) * SUB), :])
    def flip(k8, carry):
        for u in range(8):
            k = k8 * 8 + u
            put3(tr, TAPROWS - 1 - k, rows3(tv, k, 1))
            put3(dr, TAPROWS - 1 - k, rows3(dv, k, 1))
        return carry
    lax.fori_loop(0, TAPROWS // 8, flip, 0)

def conv_block(i, count, ext_f, ext_r, tv, dv, tr, dr, sv, ev, res):
    p0 = i * 16
    zero8 = jnp.zeros((8, SUB, LANES), jnp.float32)
    idx16 = lax.broadcasted_iota(jnp.int32, (16, SUB, LANES), 0)
    far_lags = SPAN // 16
    s0 = rows3(sv, p0, 1)
    e0 = rows3(ev, p0 + 15, 1)

    def fwd_far(j, acc):
        lag = j * 16
        q0 = p0 - lag
        rows = jnp.where(idx16 >= s0 - q0, rows3(ext_f, count + q0, 16), 0.0)
        x0, x1 = rows[:8], rows[8:]
        xs = x0 + x1
        a, b, c = acc
        for u in range(8):
            a = a + rows3(tv, PAD + lag - u, 8) * xs[u:u + 1]
            b = b + rows3(dv, PAD + lag - u, 8) * x1[u:u + 1]
            c = c + rows3(dv, PAD + 8 + lag - u, 8) * x0[u:u + 1]
        return a, b, c

    def rev_far(j, acc):
        lag = j * 16
        q0 = p0 + lag
        rows = jnp.where(idx16 < e0 - q0, rows3(ext_r, q0, 16), 0.0)
        x0, x1 = rows[:8], rows[8:]
        xs = x0 + x1
        a, b, c = acc
        for u in range(8):
            a = a + rows3(tr, BASE - lag - u, 8) * xs[u:u + 1]
            b = b + rows3(dr, BASE - lag - u, 8) * x0[u:u + 1]
            c = c + rows3(dr, BASE - 8 - lag - u, 8) * x1[u:u + 1]
        return a, b, c

    def part(value, lo, term):
        pieces = [value[:lo], value[lo : lo + term.shape[0]] + term, value[lo + term.shape[0] :]]
        return jnp.concatenate([piece for piece in pieces if piece.shape[0]], axis=0)

    a, b, c = lax.fori_loop(1, far_lags, fwd_far, (zero8,) * 3, unroll=7)
    far_f = [a + b, a - c]
    rows = jnp.where(idx16 >= s0 - (p0 - SPAN), rows3(ext_f, count + p0 - SPAN, 16), 0.0)
    for u in range(8):
        far_f[0] = far_f[0] + rows3(tv, PAD + SPAN - 8 - u, 8) * rows[8 + u : 9 + u]
        if u:
            tap = rows3(tv, PAD + SPAN - u, u)
            far_f[0] = part(far_f[0], 0, tap * rows[u : u + 1])
            far_f[1] = part(far_f[1], 0, tap * rows[8 + u : 9 + u])
    a, b, c = lax.fori_loop(1, far_lags, rev_far, (zero8,) * 3, unroll=7)
    far_r = [a - c, a + b]
    rows = jnp.where(idx16 < e0 - (p0 + SPAN), rows3(ext_r, p0 + SPAN, 16), 0.0)
    for u in range(8):
        far_r[1] = far_r[1] + rows3(tr, BASE - SPAN + 8 - u, 8) * rows[u : u + 1]
        if u < 7:
            tap = rows3(tr, BASE - SPAN + 1, 7 - u)
            far_r[0] = part(far_r[0], u + 1, tap * rows[u : u + 1])
            far_r[1] = part(far_r[1], u + 1, tap * rows[8 + u : 9 + u])
    xf = (rows3(ext_f, count + p0, 8), rows3(ext_f, count + p0 + 8, 8))
    xr = (rows3(ext_r, p0, 8), rows3(ext_r, p0 + 8, 8))
    idx8 = lax.broadcasted_iota(jnp.int32, (8, SUB, LANES), 0)
    mid = rows3(sv, p0 + 8, 1)
    m = jnp.where(idx8 >= mid - p0, xf[0], 0.0)
    mid_f = zero8
    for u in range(8):
        mid_f = mid_f + rows3(tv, PAD + 8 - u, 8) * m[u:u + 1]
    mid = rows3(ev, p0 + 7, 1)
    m = jnp.where(idx8 < mid - p0 - 8, xr[1], 0.0)
    mid_r = zero8
    for u in range(8):
        mid_r = mid_r + rows3(tr, BASE - 8 - u, 8) * m[u:u + 1]
    for h in range(2):
        pb = p0 + 8 * h
        start = rows3(sv, pb, 8)
        end = rows3(ev, pb, 8)
        mix_f = jnp.where(start < p0, far_f[h], 0.0)
        mix_r = jnp.where(end > p0 + 16, far_r[h], 0.0)
        if h == 1:
            mix_f = mix_f + jnp.where(start < pb, mid_f, 0.0)
        else:
            mix_r = mix_r + jnp.where(end > pb + 8, mid_r, 0.0)
        near_f = [rows3(tv, PAD + d, 1) for d in range(8)]
        sums_f, sums_r = [], []
        for r in range(8):
            sum_f, sum_r = mix_f[r : r + 1], mix_r[r : r + 1]
            for u in range(8):
                if u < r:
                    term = near_f[r - u] * xf[h][u : u + 1]
                    sum_f = sum_f + jnp.where(start[r : r + 1] <= pb + u, term, 0.0)
                elif u > r:
                    term = near_f[u - r] * xr[h][u : u + 1]
                    sum_r = sum_r + jnp.where(end[r : r + 1] > pb + u, term, 0.0)
            sums_f.append(sum_f + near_f[0] * xf[h][r : r + 1])
            sums_r.append(sum_r + near_f[0] * xr[h][r : r + 1])
        mix_f = jnp.concatenate(sums_f, axis=0)
        mix_r = jnp.concatenate(sums_r, axis=0)
        gated_f = (xf[h] * mix_f).astype(jnp.bfloat16).astype(jnp.float32)
        gated_r = (xr[h] * mix_r).astype(jnp.bfloat16).astype(jnp.float32)
        put3(res, pb, (gated_f + gated_r) * 0.5)


def score_kernel(tok_ref, comp_ref, lens_ref, owner_ref, gain_ref, embed_hbm, taps_hbm, w_hbm,
                 out_ref, embed_ref, taps_ref, sbuf, wbuf, out1, in1, zout, zin, kept,
                 pbuf, xbuf, abuf, rbuf, obuf, member, scale, tk, pw, gain8,
                 ext_f, ext_r, inv_f, inv_r, tv, dv, tr, dr, sv, ev, res,
                 l_sem, w_send, w_recv, s_send, s_recv, r_send, r_recv, z_send, z_recv,
                 x_send, x_recv, a_send, a_recv, t_send, t_recv, p_send, p_recv):
    me = lax.axis_index("ctx")
    ch = lax.axis_index("ch")
    peers = lax.axis_size("ctx")
    y = lax.rem(me, 4)
    zh = lax.rem(lax.div(me, 4), 4)
    x = lax.div(me, 16)
    zl = lax.div(ch, 2)
    core = lax.rem(ch, 2)

    def ring(v, by):
        return lax.rem(v + by, 4)

    def at_ctx(cx, cz, cy):
        return {"ctx": cx * 16 + cz * 4 + cy}

    xp, xm, x2 = ring(x, 1), ring(x, 3), ring(x, 2)
    zp, zm, z2 = ring(zh, 1), ring(zh, 3), ring(zh, 2)
    yp, ym, y2 = ring(y, 1), ring(y, 3), ring(y, 2)
    core_peer = zl * 2 + 1 - core
    z_peer = (1 - zl) * 2 + core
    after, before = lax.rem(me + 1, peers), lax.rem(me + peers - 1, peers)

    barrier = pltpu.get_barrier_semaphore()

    def greet(to):
        pl.semaphore_signal(barrier, inc=1, device_id=to, device_id_type=MESH)

    for d in range(1, 4):
        greet({"ch": lax.rem(ch + d, 4)})
        greet(at_ctx(ring(x, d), zh, y))
    greet({"ctx": after})
    greet({"ctx": before})

    def plane(d):
        return at_ctx(x, ring(zh, lax.div(d, 4)), ring(y, lax.rem(d, 4)))

    def hello(d, carry):
        greet(plane(d))
        return carry

    lax.fori_loop(1, 16, hello, 0)

    cols = w_hbm.shape[0]
    half = cols // 2
    rows = sbuf.shape[0] // 4
    vocab, width = embed_ref.shape
    segs = lens_ref.shape[1]
    own_w = wbuf.at[pl.ds(pl.multiple_of((x * 4 + zh) * cols, cols), cols), :]
    fetch = [
        pltpu.make_async_copy(embed_hbm, embed_ref, l_sem.at[0]),
        pltpu.make_async_copy(w_hbm, own_w, l_sem.at[1]),
        pltpu.make_async_copy(taps_hbm, taps_ref, l_sem.at[2]),
    ]
    for copy in fetch:
        copy.start()

    def iota(shape, dim):
        return lax.broadcasted_iota(jnp.int32, shape, dim)

    lens = jnp.broadcast_to(lens_ref[...], (SUB, segs)).astype(f32)
    upto = (iota((segs, segs), 0) <= iota((segs, segs), 1)).astype(bf16)
    ends_row = jnp.dot(lens.astype(bf16), upto, preferred_element_type=f32)
    starts_row = (ends_row - lens)[0:1]
    ends_row = ends_row[0:1]
    letters = iota((rows, vocab), 1)

    def ids_of(slot):
        return tk[slot].astype(f32).T[:, 0:1].astype(jnp.int32)

    def other_of(ids):
        hit = jnp.where(letters == ids, comp_ref[...].astype(f32), 0.0)
        return jnp.sum(hit, axis=1, keepdims=True).astype(jnp.int32)

    def pick_rows(ids_a, ids_b, put_a, put_b):
        picks = jnp.concatenate([letters == ids_a, letters == ids_b], axis=0)
        picks = picks.astype(f32).astype(bf16)
        for n in range(width // (2 * LANES)):
            table = embed_ref[:, n * 2 * LANES : (n + 1) * 2 * LANES]
            found = jnp.dot(picks, table, preferred_element_type=f32)
            for m in range(2):
                lanes = slice(m * LANES, (m + 1) * LANES)
                for ref, at, part in (put_a + (found[:rows],), put_b + (found[rows:],)):
                    ref[pl.ds(at * SUB + 2 * n + m, rows, stride=SUB), :] = part[:, lanes]

    tk[1] = jnp.broadcast_to(tok_ref[...], (SUB, rows))
    own_ids = ids_of(1)
    own_other = other_of(own_ids)

    fetch[0].wait()
    fold = jnp.zeros((vocab, LANES), f32)
    for s in range(SUB):
        piece = embed_ref[:, s * LANES : (s + 1) * LANES].astype(f32)
        fold = fold + piece * piece
        gain8[s : s + 1, :] = gain_ref[:, s * LANES : (s + 1) * LANES]
    pw[ch] = jnp.broadcast_to(jnp.sum(fold.T, axis=0, keepdims=True), (SUB, vocab))
    fetch[1].wait()

    def w_rows(cx, cz, h=None):
        lo, count = (0, cols) if h is None else (h * half, half)
        return wbuf.at[pl.ds(pl.multiple_of((cx * 4 + cz) * cols + lo, half), count), :]

    z_of = (zh, zm, zp, z2)
    plus, minus = at_ctx(xp, zh, y), at_ctx(xm, zh, y)
    up, down = at_ctx(x, zp, y), at_ctx(x, zm, y)
    sent, got = {}, {}
    for h in range(2):
        own = w_rows(x, zh, h)
        sent["z", h, 0], got["z", h, 0] = (own, up), w_rows(x, zm, h)
        sent["z", h, 1], got["z", h, 1] = (own, down), w_rows(x, zp, h)
        for dz in range(4):
            here = w_rows(x, z_of[dz], h)
            sent["x", dz, h, 0], got["x", dz, h, 0] = (here, plus), w_rows(xm, z_of[dz], h)
            sent["x", dz, h, 1], got["x", dz, h, 1] = (here, minus), w_rows(xp, z_of[dz], h)
    sent["y", 0], got["y", 0] = (w_rows(x, zm, 0), up), w_rows(x, z2, 0)
    sent["y", 1], got["y", 1] = (w_rows(x, zp, 1), down), w_rows(x, z2, 1)
    for dz in range(4):
        sent["r", dz, 0], got["r", dz, 0] = (w_rows(xm, z_of[dz], 0), plus), w_rows(x2, z_of[dz], 0)
        sent["r", dz, 1], got["r", dz, 1] = (w_rows(xp, z_of[dz], 1), minus), w_rows(x2, z_of[dz], 1)
    number = {name: n for n, name in enumerate(sent)}

    def w_copy(name, ref, to):
        n = number[name]
        return pltpu.make_async_remote_copy(
            src_ref=ref, dst_ref=ref, send_sem=w_send.at[n], recv_sem=w_recv.at[n],
            device_id=to, device_id_type=MESH,
        )

    seen = set()

    def w_start(*names):
        for name in names:
            w_copy(name, *sent[name]).start()

    def w_wait(*names):
        for name in names:
            seen.add(name)
            w_copy(name, got[name], plus).wait_recv()

    def both(dz, h):
        w_start(("x", dz, h, 0), ("x", dz, h, 1))

    def relay(dz):
        w_wait(("x", dz, 0, 0))
        w_start(("r", dz, 0))
        w_wait(("x", dz, 1, 1))
        w_start(("r", dz, 1))

    def step_a():
        w_wait(("z", 0, 0))
        both(1, 0)
        w_start(("y", 0))
        w_wait(("z", 0, 1))
        both(2, 0)

    def step_b():
        w_wait(("z", 1, 1))
        w_start(("y", 1))
        both(2, 1)
        w_wait(("z", 1, 0))
        both(1, 1)

    def step_c():
        w_wait(("y", 0))
        both(3, 0)
        w_wait(("y", 1))
        both(3, 1)

    def token_copy(slot, to):
        return pltpu.make_async_remote_copy(
            src_ref=tk.at[1], dst_ref=tk.at[slot], send_sem=t_send.at[slot // 2],
            recv_sem=t_recv.at[slot // 2], device_id={"ctx": to}, device_id_type=MESH,
        )

    def power_copy(d, ref):
        return pltpu.make_async_remote_copy(
            src_ref=ref, dst_ref=ref, send_sem=p_send.at[d - 1], recv_sem=p_recv.at[d - 1],
            device_id={"ch": lax.rem(ch + d, 4)}, device_id_type=MESH,
        )

    pl.semaphore_wait(barrier, 23)
    token_copy(0, after).start()
    token_copy(2, before).start()
    for d in range(1, 4):
        power_copy(d, pw.at[ch]).start()
    w_start(("z", 0, 0), ("z", 0, 1))
    both(0, 0)
    both(0, 1)
    w_start(("z", 1, 0), ("z", 1, 1))

    pick_rows(own_ids, own_other, (ext_f, rows), (ext_r, 0))
    first = me * rows
    pos = (iota((rows, segs), 0) + first).astype(f32)
    start_col = jnp.max(jnp.where(starts_row <= pos, starts_row, 0.0), axis=1, keepdims=True)
    end_col = jnp.min(jnp.where(ends_row > pos, ends_row, 1e9), axis=1, keepdims=True)
    start_col = jnp.broadcast_to(start_col, (rows, LANES)).astype(jnp.int32) - first
    end_col = jnp.broadcast_to(end_col, (rows, LANES)).astype(jnp.int32) - first
    for s in range(SUB):
        sv[pl.ds(s, rows, stride=SUB), :] = start_col
        ev[pl.ds(s, rows, stride=SUB), :] = end_col
    fetch[2].wait()
    prep_taps(taps_ref, tv, dv, tr, dr)

    token_copy(0, after).wait_recv()
    token_copy(2, before).wait_recv()
    last_ids = ids_of(0)
    next_other = other_of(ids_of(2))
    pick_rows(last_ids, next_other, (ext_f, 0), (ext_r, rows))

    for d in range(1, 4):
        power_copy(d, pw.at[lax.rem(ch + 4 - d, 4)]).wait_recv()
    power = (pw[0] + pw[1]) + (pw[2] + pw[3])
    inv_row = lax.rsqrt(power / (4 * width) + norm_eps)[0:1]
    for ref, at, ids in (
        (inv_f, 0, last_ids), (inv_f, rows, own_ids), (inv_r, 0, own_other), (inv_r, rows, next_other),
    ):
        col = jnp.sum(jnp.where(letters == ids, inv_row, 0.0), axis=1, keepdims=True)
        col = jnp.broadcast_to(col, (rows, LANES))
        for s in range(SUB):
            ref[pl.ds(at * SUB + s, rows, stride=SUB), :] = col

    def scale_rows(i, carry):
        for ext, inv in ((ext_f, inv_f), (ext_r, inv_r)):
            value = rows3(ext, i * 16, 16) * rows3(inv, i * 16, 16) * gain8[...][None]
            put3(ext, i * 16, value.astype(bf16).astype(f32))
        return carry

    lax.fori_loop(0, 2 * rows // 16, scale_rows, 0)
    relay(0)
    step_a()

    chunk = 16
    parts = rows // chunk

    def s_rows(cy, k):
        return sbuf.at[pl.ds(pl.multiple_of(cy * rows + k * chunk, chunk), chunk), :]

    def s_copy(k, kind, ref, cy):
        return pltpu.make_async_remote_copy(
            src_ref=ref, dst_ref=ref, send_sem=s_send.at[3 * k + kind],
            recv_sem=s_recv.at[3 * k + kind], device_id=at_ctx(x, zh, cy), device_id_type=MESH,
        )

    steps = {1: step_b, 3: step_c, 5: lambda: relay(2), 6: lambda: relay(1), 7: lambda: relay(3)}

    def sixteen(i, carry):
        conv_block(i, rows, ext_f, ext_r, tv, dv, tr, dr, sv, ev, res)
        at = pl.ds(pl.multiple_of(y * rows + i * chunk, chunk), chunk)
        for s in range(SUB):
            block = res[pl.ds(i * chunk * SUB + s, chunk, stride=SUB), :]
            sbuf[at, s * LANES : (s + 1) * LANES] = block.astype(bf16)
        for kind, cy in ((2, y2), (0, yp), (1, ym)):
            s_copy(i, kind, s_rows(y, i), cy).start()
        for when, step in steps.items():
            pl.when(i == when)(step)
        return carry

    lax.fori_loop(0, parts, sixteen, 0)

    blocks = owner_ref.shape[1]
    spread = ((iota((blocks, segs), 1) >> 2) == iota((blocks, segs), 0)).astype(bf16)
    owners = jnp.broadcast_to(owner_ref[...], (SUB, blocks)).astype(f32).astype(bf16)
    owner_row = jnp.dot(owners, spread, preferred_element_type=f32)[0:1].astype(jnp.int32)
    slot, seg = iota((segs, segs), 0), iota((segs, segs), 1)
    same = (owner_row == (slot >> 2)) & ((slot & 3) == (seg & 3))
    slot_start = jnp.sum(jnp.where(same, starts_row, 0.0), axis=1, keepdims=True)
    slot_end = jnp.sum(jnp.where(same, ends_row, 0.0), axis=1, keepdims=True)
    total = 4 * rows
    spot = (iota((segs, total), 1) + lax.div(me, 4) * total).astype(f32)
    member[...] = ((slot_start <= spot) & (spot < slot_end)).astype(f32).astype(bf16)
    scale[...] = jnp.broadcast_to(slot_end - slot_start, (segs, LANES))

    def s_finish(k, carry):
        for kind, cy in enumerate((ym, yp, y2)):
            s_copy(k, kind, s_rows(cy, k), yp).wait_recv()
        return carry

    lax.fori_loop(0, parts, s_finish, 0)
    w_wait(*[name for name in got if name not in seen])

    group = 4 * cols

    def product(g, h):
        rhs = wbuf[pl.ds(pl.multiple_of(g * group + h * LANES, LANES), LANES), :]
        return lax.dot_general(
            sbuf[...], rhs, (((1,), (1,)), ((), ())), preferred_element_type=f32
        )

    def core_copy(n):
        return pltpu.make_async_remote_copy(
            src_ref=out1.at[n], dst_ref=in1.at[n], send_sem=r_send.at[n],
            recv_sem=r_recv.at[n], device_id={"ch": core_peer}, device_id_type=MESH,
        )

    def z_copy(h, t):
        at = pl.ds(t * 2 * rows, 2 * rows)
        return pltpu.make_async_remote_copy(
            src_ref=zout.at[h, at, :], dst_ref=zin.at[h, at, :], send_sem=z_send.at[2 * h + t],
            recv_sem=z_recv.at[2 * h + t], device_id={"ch": z_peer}, device_id_type=MESH,
        )

    for h in range(2):
        out1[h] = product(2 * (1 - zl) + 1 - core, h).astype(bf16)
        core_copy(h).start()
    for h in range(2):
        kept[h] = product(2 * (1 - zl) + core, h)
        core_copy(h).wait_recv()
        for t in range(2):
            at = pl.ds(t * 2 * rows, 2 * rows)
            zout[h, at, :] = (kept[h, at, :] + in1[h, at, :].astype(f32)).astype(bf16)
            z_copy(h, t).start()
    for h in range(2):
        out1[2 + h] = product(2 * zl + 1 - core, h).astype(bf16)
        core_copy(2 + h).start()
    for h in range(2):
        kept[h] = product(2 * zl + core, h)

    share = 16 * SUB // 2

    def to_x(h, d):
        n = 3 * h + d - 1
        return pltpu.make_async_remote_copy(
            src_ref=pbuf.at[h, pl.ds(pl.multiple_of(ring(x, d) * share, share), share), :],
            dst_ref=xbuf.at[n], send_sem=x_send.at[n], recv_sem=x_recv.at[n],
            device_id=at_ctx(ring(x, d), zh, y), device_id_type=MESH,
        )

    for h in range(2):
        highs, lows = [], []
        core_copy(2 + h).wait_recv()
        for t in range(2):
            at = pl.ds(t * 2 * rows, 2 * rows)
            z_copy(h, t).wait_recv()
            scores = kept[h, at, :] + in1[2 + h, at, :].astype(f32) + zin[h, at, :].astype(f32)
            active = jnp.maximum(scores, 0.0) + jnp.log1p(jnp.exp(-jnp.abs(scores)))
            highs.append(active.astype(bf16))
            lows.append((active - highs[-1].astype(f32)).astype(bf16))
        halves = jnp.concatenate(
            [jnp.concatenate(highs, axis=0), jnp.concatenate(lows, axis=0)], axis=1
        )
        sums = jnp.dot(member[...], halves, preferred_element_type=f32)
        pbuf[h] = (sums[:, :LANES] + sums[:, LANES:]) / scale[...]
        for d in (2, 1, 3):
            to_x(h, d).start()
    for h in range(2):
        mine = pbuf[h, pl.ds(pl.multiple_of(x * share, share), share), :]
        for d in range(1, 4):
            to_x(h, d).wait_recv()
            mine = mine + xbuf[3 * h + d - 1]
        abuf[pl.ds(h, share, stride=2), :] = mine

    def tile_at(cz, cy):
        return pl.ds(pl.multiple_of((cz * 4 + cy) * SUB, SUB), SUB)

    def to_owner(d, carry):
        cz, cy = ring(zh, lax.div(d, 4)), ring(y, lax.rem(d, 4))
        pltpu.make_async_remote_copy(
            src_ref=abuf.at[tile_at(cz, cy), :], dst_ref=rbuf.at[tile_at(zh, y), :],
            send_sem=a_send, recv_sem=a_recv, device_id=plane(d), device_id_type=MESH,
        ).start()
        return carry

    lax.fori_loop(1, 16, to_owner, 0)
    rbuf[tile_at(zh, y), :] = abuf[tile_at(zh, y), :]
    most = pl.ds(0, 15 * SUB)
    all_of = pltpu.make_async_remote_copy(
        src_ref=abuf.at[most, :], dst_ref=rbuf.at[most, :], send_sem=a_send, recv_sem=a_recv,
        device_id=plane(1), device_id_type=MESH,
    )
    all_of.wait_recv()
    for q in range(4):
        acc = rbuf[pl.ds(q * SUB, SUB), :]
        for m in range(1, 4):
            acc = acc + rbuf[pl.ds((4 * m + q) * SUB, SUB), :]
        obuf[pl.ds(q * SUB, SUB), :] = acc
        obuf[pl.ds((4 + q) * SUB, SUB), :] = pltpu.roll(acc, LANES // 2, 1)
    count = out_ref.shape[0]
    left = iota((count, LANES), 1) < LANES // 2
    for hz in range(2):
        for q in range(2):
            plain = [obuf[pl.ds((2 * q + n) * SUB + hz, count, stride=2), :] for n in range(2)]
            moved = [obuf[pl.ds((4 + 2 * q + n) * SUB + hz, count, stride=2), :] for n in range(2)]
            for b in range(2):
                pair = (plain[0], moved[1]) if b == 0 else (moved[0], plain[1])
                lane = ((2 * hz + b) * 2 + q) * LANES
                out_ref[:, lane : lane + LANES] = jnp.where(left, *pair)

    all_of.wait_send()
    for name in sent:
        w_copy(name, *sent[name]).wait_send()

    def s_drain(k, carry):
        for kind in range(3):
            s_copy(k, kind, s_rows(y, k), yp).wait_send()
        return carry

    lax.fori_loop(0, parts, s_drain, 0)
    for d in range(1, 4):
        power_copy(d, pw.at[ch]).wait_send()
        to_x(0, d).wait_send()
        to_x(1, d).wait_send()
    token_copy(0, after).wait_send()
    token_copy(2, before).wait_send()
    for n in range(4):
        core_copy(n).wait_send()
        z_copy(n // 2, n % 2).wait_send()


def body(tokens, complement, seg_lengths, owner, embed, norm_gain, taps, w_out):
    rows = tokens.shape[0]
    vocab, width = embed.shape
    cols = w_out.shape[1]
    segs = seg_lengths.shape[0]
    per_block = segs // owner.shape[0]
    total, group = 4 * rows, 4 * cols
    vmem = pl.BlockSpec(memory_space=pltpu.VMEM)
    hbm = pl.BlockSpec(memory_space=pl.ANY)

    def tiles(count, dtype=f32):
        return pltpu.VMEM((count * SUB, LANES), dtype)

    def sems(count):
        return pltpu.SemaphoreType.DMA((count,))

    return pl.pallas_call(
        score_kernel,
        out_shape=jax.ShapeDtypeStruct((per_block, width), f32),
        in_specs=[vmem] * 5 + [hbm] * 3,
        out_specs=vmem,
        scratch_shapes=[
            pltpu.VMEM((vocab, width), bf16),
            pltpu.VMEM((taps.shape[0], width), f32),
            pltpu.VMEM((total, width), bf16),
            pltpu.VMEM((16 * cols, width), bf16),
            pltpu.VMEM((4, total, LANES), bf16),
            pltpu.VMEM((4, total, LANES), bf16),
            pltpu.VMEM((2, total, LANES), bf16),
            pltpu.VMEM((2, total, LANES), bf16),
            pltpu.VMEM((2, total, LANES), f32),
            pltpu.VMEM((2, segs, LANES), f32),
            pltpu.VMEM((6, 8 * SUB, LANES), f32),
            tiles(16),
            tiles(16),
            tiles(8),
            pltpu.VMEM((segs, total), bf16),
            pltpu.VMEM((segs, LANES), f32),
            pltpu.VMEM((3, SUB, rows), jnp.int32),
            pltpu.VMEM((4, SUB, vocab), f32),
            tiles(1),
        ]
        + [tiles(2 * rows)] * 4
        + [tiles(TAPROWS)] * 4
        + [tiles(rows, jnp.int32)] * 2
        + [tiles(rows)]
        + [sems(3), sems(30), sems(30), sems(24), sems(24), sems(4), sems(4), sems(4), sems(4)]
        + [sems(6), sems(6), pltpu.SemaphoreType.DMA, pltpu.SemaphoreType.DMA]
        + [sems(2), sems(2), sems(3), sems(3)],
        compiler_params=pltpu.CompilerParams(
            vmem_limit_bytes=56 << 20, collective_id=0, has_side_effects=True
        ),
    )(
        tokens[None, :], complement[None, :], seg_lengths[None, :], owner[None, :],
        norm_gain[None, :], embed, taps, w_out.T,
    )


def solution(mesh):
    in_specs = (P("ctx"), P(), P(), P(), P(None, "ch"), P("ch"), P(None, "ch"), P("ch", "ctx"))
    out_specs = P("ctx", "ch")
    return jax.shard_map(body, mesh=mesh, in_specs=in_specs, out_specs=out_specs, check_vma=False)
```

```python
import jax
import jax.numpy as jnp
from jax import lax
from jax.experimental import pallas as pl
from jax.experimental.pallas import tpu as pltpu
from jax.sharding import PartitionSpec as P

norm_eps = 1e-06
LANES = 128
SUB = 8
PAD = 8
SPAN = 128
TAPROWS = 152
BASE = 143
MESH = pl.DeviceIdType.MESH
f32 = jnp.float32
bf16 = jnp.bfloat16


def rows3(ref, k, n):
    return ref[pl.ds(pl.multiple_of(k * SUB, SUB), n * SUB), :].reshape(n, SUB, LANES)

def put3(ref, k, v):
    n = v.shape[0]
    ref[pl.ds(pl.multiple_of(k * SUB, SUB), n * SUB), :] = v.reshape(n * SUB, LANES)

def prep_taps(taps_ref, tv, dv, tr, dr):
    span = taps_ref.shape[0]
    edge = jnp.zeros((PAD * SUB, LANES), jnp.float32)
    tv[pl.ds(0, PAD * SUB), :] = edge
    for e in range(2):
        tv[pl.ds((PAD + span + 8 * e) * SUB, 8 * SUB), :] = edge
    for s in range(SUB):
        tv[pl.ds(PAD * SUB + s, span, stride=SUB), :] = taps_ref[:, s * LANES:(s + 1) * LANES]
    dv[pl.ds(0, PAD * SUB), :] = edge
    dv[pl.ds(PAD * SUB, (TAPROWS - PAD) * SUB), :] = (
        tv[pl.ds(0, (TAPROWS - PAD) * SUB), :] - tv[pl.ds(PAD * SUB, (TAPROWS - PAD) * SUB), :])
    def flip(k8, carry):
        for u in range(8):
            k = k8 * 8 + u
            put3(tr, TAPROWS - 1 - k, rows3(tv, k, 1))
            put3(dr, TAPROWS - 1 - k, rows3(dv, k, 1))
        return carry
    lax.fori_loop(0, TAPROWS // 8, flip, 0)

def conv_block(i, count, ext_f, ext_r, tv, dv, tr, dr, sv, ev, res):
    p0 = i * 16
    zero8 = jnp.zeros((8, SUB, LANES), jnp.float32)
    idx16 = lax.broadcasted_iota(jnp.int32, (16, SUB, LANES), 0)
    far_lags = SPAN // 16
    s0 = rows3(sv, p0, 1)
    e0 = rows3(ev, p0 + 15, 1)

    def fwd_far(j, acc):
        lag = j * 16
        q0 = p0 - lag
        rows = jnp.where(idx16 >= s0 - q0, rows3(ext_f, count + q0, 16), 0.0)
        x0, x1 = rows[:8], rows[8:]
        xs = x0 + x1
        a, b, c = acc
        for u in range(8):
            a = a + rows3(tv, PAD + lag - u, 8) * xs[u:u + 1]
            b = b + rows3(dv, PAD + lag - u, 8) * x1[u:u + 1]
            c = c + rows3(dv, PAD + 8 + lag - u, 8) * x0[u:u + 1]
        return a, b, c

    def rev_far(j, acc):
        lag = j * 16
        q0 = p0 + lag
        rows = jnp.where(idx16 < e0 - q0, rows3(ext_r, q0, 16), 0.0)
        x0, x1 = rows[:8], rows[8:]
        xs = x0 + x1
        a, b, c = acc
        for u in range(8):
            a = a + rows3(tr, BASE - lag - u, 8) * xs[u:u + 1]
            b = b + rows3(dr, BASE - lag - u, 8) * x0[u:u + 1]
            c = c + rows3(dr, BASE - 8 - lag - u, 8) * x1[u:u + 1]
        return a, b, c

    def part(value, lo, term):
        pieces = [value[:lo], value[lo : lo + term.shape[0]] + term, value[lo + term.shape[0] :]]
        return jnp.concatenate([piece for piece in pieces if piece.shape[0]], axis=0)

    a, b, c = lax.fori_loop(1, far_lags, fwd_far, (zero8,) * 3, unroll=7)
    far_f = [a + b, a - c]
    rows = jnp.where(idx16 >= s0 - (p0 - SPAN), rows3(ext_f, count + p0 - SPAN, 16), 0.0)
    for u in range(8):
        far_f[0] = far_f[0] + rows3(tv, PAD + SPAN - 8 - u, 8) * rows[8 + u : 9 + u]
        if u:
            tap = rows3(tv, PAD + SPAN - u, u)
            far_f[0] = part(far_f[0], 0, tap * rows[u : u + 1])
            far_f[1] = part(far_f[1], 0, tap * rows[8 + u : 9 + u])
    a, b, c = lax.fori_loop(1, far_lags, rev_far, (zero8,) * 3, unroll=7)
    far_r = [a - c, a + b]
    rows = jnp.where(idx16 < e0 - (p0 + SPAN), rows3(ext_r, p0 + SPAN, 16), 0.0)
    for u in range(8):
        far_r[1] = far_r[1] + rows3(tr, BASE - SPAN + 8 - u, 8) * rows[u : u + 1]
        if u < 7:
            tap = rows3(tr, BASE - SPAN + 1, 7 - u)
            far_r[0] = part(far_r[0], u + 1, tap * rows[u : u + 1])
            far_r[1] = part(far_r[1], u + 1, tap * rows[8 + u : 9 + u])
    xf = (rows3(ext_f, count + p0, 8), rows3(ext_f, count + p0 + 8, 8))
    xr = (rows3(ext_r, p0, 8), rows3(ext_r, p0 + 8, 8))
    idx8 = lax.broadcasted_iota(jnp.int32, (8, SUB, LANES), 0)
    mid = rows3(sv, p0 + 8, 1)
    m = jnp.where(idx8 >= mid - p0, xf[0], 0.0)
    mid_f = zero8
    for u in range(8):
        mid_f = mid_f + rows3(tv, PAD + 8 - u, 8) * m[u:u + 1]
    mid = rows3(ev, p0 + 7, 1)
    m = jnp.where(idx8 < mid - p0 - 8, xr[1], 0.0)
    mid_r = zero8
    for u in range(8):
        mid_r = mid_r + rows3(tr, BASE - 8 - u, 8) * m[u:u + 1]
    for h in range(2):
        pb = p0 + 8 * h
        start = rows3(sv, pb, 8)
        end = rows3(ev, pb, 8)
        mix_f = jnp.where(start < p0, far_f[h], 0.0)
        mix_r = jnp.where(end > p0 + 16, far_r[h], 0.0)
        if h == 1:
            mix_f = mix_f + jnp.where(start < pb, mid_f, 0.0)
        else:
            mix_r = mix_r + jnp.where(end > pb + 8, mid_r, 0.0)
        near_f = [rows3(tv, PAD + d, 1) for d in range(8)]
        sums_f, sums_r = [], []
        for r in range(8):
            sum_f, sum_r = mix_f[r : r + 1], mix_r[r : r + 1]
            for u in range(8):
                if u < r:
                    term = near_f[r - u] * xf[h][u : u + 1]
                    sum_f = sum_f + jnp.where(start[r : r + 1] <= pb + u, term, 0.0)
                elif u > r:
                    term = near_f[u - r] * xr[h][u : u + 1]
                    sum_r = sum_r + jnp.where(end[r : r + 1] > pb + u, term, 0.0)
            sums_f.append(sum_f + near_f[0] * xf[h][r : r + 1])
            sums_r.append(sum_r + near_f[0] * xr[h][r : r + 1])
        mix_f = jnp.concatenate(sums_f, axis=0)
        mix_r = jnp.concatenate(sums_r, axis=0)
        gated_f = (xf[h] * mix_f).astype(jnp.bfloat16).astype(jnp.float32)
        gated_r = (xr[h] * mix_r).astype(jnp.bfloat16).astype(jnp.float32)
        put3(res, pb, (gated_f + gated_r) * 0.5)


def score_kernel(tok_ref, comp_ref, lens_ref, owner_ref, gain_ref, embed_hbm, taps_hbm, w_hbm,
                 out_ref, embed_ref, taps_ref, sbuf, wbuf, out1, in1, zout, zin, kept,
                 pbuf, psend, xbuf, abuf, rbuf, obuf, member, scale, tk, pw, gain8,
                 ext_f, ext_r, inv_f, inv_r, tv, dv, tr, dr, sv, ev, res,
                 l_sem, w_send, w_recv, s_send, s_recv, r_send, r_recv, z_send, z_recv,
                 x_send, x_recv, a_send, a_recv, t_send, t_recv, p_send, p_recv):
    me = lax.axis_index("ctx")
    ch = lax.axis_index("ch")
    peers = lax.axis_size("ctx")
    y = lax.rem(me, 4)
    zh = lax.rem(lax.div(me, 4), 4)
    x = lax.div(me, 16)
    zl = lax.div(ch, 2)
    core = lax.rem(ch, 2)

    def ring(v, by):
        return lax.rem(v + by, 4)

    def at_ctx(cx, cz, cy):
        return {"ctx": cx * 16 + cz * 4 + cy}

    xp, xm, x2 = ring(x, 1), ring(x, 3), ring(x, 2)
    zp, zm, z2 = ring(zh, 1), ring(zh, 3), ring(zh, 2)
    yp, ym, y2 = ring(y, 1), ring(y, 3), ring(y, 2)
    core_peer = zl * 2 + 1 - core
    z_peer = (1 - zl) * 2 + core
    after, before = lax.rem(me + 1, peers), lax.rem(me + peers - 1, peers)

    barrier = pltpu.get_barrier_semaphore()

    def greet(to):
        pl.semaphore_signal(barrier, inc=1, device_id=to, device_id_type=MESH)

    for d in range(1, 4):
        greet({"ch": lax.rem(ch + d, 4)})
        greet(at_ctx(ring(x, d), zh, y))
    greet({"ctx": after})
    greet({"ctx": before})

    def plane(d):
        return at_ctx(x, ring(zh, lax.div(d, 4)), ring(y, lax.rem(d, 4)))

    def hello(d, carry):
        greet(plane(d))
        return carry

    lax.fori_loop(1, 16, hello, 0)

    cols = w_hbm.shape[0]
    half = cols // 2
    rows = sbuf.shape[0] // 4
    vocab, width = embed_ref.shape
    segs = lens_ref.shape[1]
    own_w = wbuf.at[pl.ds(pl.multiple_of((x * 4 + zh) * cols, cols), cols), :]
    fetch = [
        pltpu.make_async_copy(embed_hbm, embed_ref, l_sem.at[0]),
        pltpu.make_async_copy(w_hbm, own_w, l_sem.at[1]),
        pltpu.make_async_copy(taps_hbm, taps_ref, l_sem.at[2]),
    ]
    for copy in fetch:
        copy.start()

    def iota(shape, dim):
        return lax.broadcasted_iota(jnp.int32, shape, dim)

    lens = jnp.broadcast_to(lens_ref[...], (SUB, segs)).astype(f32)
    upto = (iota((segs, segs), 0) <= iota((segs, segs), 1)).astype(bf16)
    ends_row = jnp.dot(lens.astype(bf16), upto, preferred_element_type=f32)
    starts_row = (ends_row - lens)[0:1]
    ends_row = ends_row[0:1]
    letters = iota((rows, vocab), 1)

    def ids_of(slot):
        return tk[slot].astype(f32).T[:, 0:1].astype(jnp.int32)

    def other_of(ids):
        hit = jnp.where(letters == ids, comp_ref[...].astype(f32), 0.0)
        return jnp.sum(hit, axis=1, keepdims=True).astype(jnp.int32)

    def pick_rows(ids_a, ids_b, put_a, put_b):
        picks = jnp.concatenate([letters == ids_a, letters == ids_b], axis=0)
        picks = picks.astype(f32).astype(bf16)
        for n in range(width // (2 * LANES)):
            table = embed_ref[:, n * 2 * LANES : (n + 1) * 2 * LANES]
            found = jnp.dot(picks, table, preferred_element_type=f32)
            for m in range(2):
                lanes = slice(m * LANES, (m + 1) * LANES)
                for ref, at, part in (put_a + (found[:rows],), put_b + (found[rows:],)):
                    ref[pl.ds(at * SUB + 2 * n + m, rows, stride=SUB), :] = part[:, lanes]

    tk[1] = jnp.broadcast_to(tok_ref[...], (SUB, rows))
    own_ids = ids_of(1)
    own_other = other_of(own_ids)

    fetch[0].wait()
    fold = jnp.zeros((vocab, LANES), f32)
    for s in range(SUB):
        piece = embed_ref[:, s * LANES : (s + 1) * LANES].astype(f32)
        fold = fold + piece * piece
        gain8[s : s + 1, :] = gain_ref[:, s * LANES : (s + 1) * LANES]
    pw[ch] = jnp.broadcast_to(jnp.sum(fold.T, axis=0, keepdims=True), (SUB, vocab))
    fetch[1].wait()

    def w_rows(cx, cz, h=None):
        lo, count = (0, cols) if h is None else (h * half, half)
        return wbuf.at[pl.ds(pl.multiple_of((cx * 4 + cz) * cols + lo, half), count), :]

    z_of = (zh, zm, zp, z2)
    plus, minus = at_ctx(xp, zh, y), at_ctx(xm, zh, y)
    up, down = at_ctx(x, zp, y), at_ctx(x, zm, y)
    sent, got = {}, {}
    for h in range(2):
        own = w_rows(x, zh, h)
        sent["z", h, 0], got["z", h, 0] = (own, up), w_rows(x, zm, h)
        sent["z", h, 1], got["z", h, 1] = (own, down), w_rows(x, zp, h)
        for dz in range(4):
            here = w_rows(x, z_of[dz], h)
            sent["x", dz, h, 0], got["x", dz, h, 0] = (here, plus), w_rows(xm, z_of[dz], h)
            sent["x", dz, h, 1], got["x", dz, h, 1] = (here, minus), w_rows(xp, z_of[dz], h)
    sent["y", 0], got["y", 0] = (w_rows(x, zm, 0), up), w_rows(x, z2, 0)
    sent["y", 1], got["y", 1] = (w_rows(x, zp, 1), down), w_rows(x, z2, 1)
    for dz in range(4):
        sent["r", dz, 0], got["r", dz, 0] = (w_rows(xm, z_of[dz], 0), plus), w_rows(x2, z_of[dz], 0)
        sent["r", dz, 1], got["r", dz, 1] = (w_rows(xp, z_of[dz], 1), minus), w_rows(x2, z_of[dz], 1)
    number = {name: n for n, name in enumerate(sent)}

    def w_copy(name, ref, to):
        n = number[name]
        return pltpu.make_async_remote_copy(
            src_ref=ref, dst_ref=ref, send_sem=w_send.at[n], recv_sem=w_recv.at[n],
            device_id=to, device_id_type=MESH,
        )

    seen = set()

    def w_start(*names):
        for name in names:
            w_copy(name, *sent[name]).start()

    def w_wait(*names):
        for name in names:
            seen.add(name)
            w_copy(name, got[name], plus).wait_recv()

    def both(dz, h):
        w_start(("x", dz, h, 0), ("x", dz, h, 1))

    def relay(dz):
        w_wait(("x", dz, 0, 0))
        w_start(("r", dz, 0))
        w_wait(("x", dz, 1, 1))
        w_start(("r", dz, 1))

    def step_a():
        w_wait(("z", 0, 0))
        both(1, 0)
        w_start(("y", 0))
        w_wait(("z", 0, 1))
        both(2, 0)

    def step_b():
        w_wait(("z", 1, 1))
        w_start(("y", 1))
        both(2, 1)
        w_wait(("z", 1, 0))
        both(1, 1)

    def step_c():
        w_wait(("y", 0))
        both(3, 0)
        w_wait(("y", 1))
        both(3, 1)

    def token_copy(slot, to):
        return pltpu.make_async_remote_copy(
            src_ref=tk.at[1], dst_ref=tk.at[slot], send_sem=t_send.at[slot // 2],
            recv_sem=t_recv.at[slot // 2], device_id={"ctx": to}, device_id_type=MESH,
        )

    def power_copy(d, ref):
        return pltpu.make_async_remote_copy(
            src_ref=ref, dst_ref=ref, send_sem=p_send.at[d - 1], recv_sem=p_recv.at[d - 1],
            device_id={"ch": lax.rem(ch + d, 4)}, device_id_type=MESH,
        )

    pl.semaphore_wait(barrier, 23)
    token_copy(0, after).start()
    token_copy(2, before).start()
    for d in range(1, 4):
        power_copy(d, pw.at[ch]).start()
    w_start(("z", 0, 0), ("z", 0, 1))
    both(0, 0)
    both(0, 1)
    w_start(("z", 1, 0), ("z", 1, 1))

    pick_rows(own_ids, own_other, (ext_f, rows), (ext_r, 0))
    first = me * rows
    pos = (iota((rows, segs), 0) + first).astype(f32)
    start_col = jnp.max(jnp.where(starts_row <= pos, starts_row, 0.0), axis=1, keepdims=True)
    end_col = jnp.min(jnp.where(ends_row > pos, ends_row, 1e9), axis=1, keepdims=True)
    start_col = jnp.broadcast_to(start_col, (rows, LANES)).astype(jnp.int32) - first
    end_col = jnp.broadcast_to(end_col, (rows, LANES)).astype(jnp.int32) - first
    for s in range(SUB):
        sv[pl.ds(s, rows, stride=SUB), :] = start_col
        ev[pl.ds(s, rows, stride=SUB), :] = end_col
    fetch[2].wait()
    prep_taps(taps_ref, tv, dv, tr, dr)

    token_copy(0, after).wait_recv()
    token_copy(2, before).wait_recv()
    last_ids = ids_of(0)
    next_other = other_of(ids_of(2))
    pick_rows(last_ids, next_other, (ext_f, 0), (ext_r, rows))

    for d in range(1, 4):
        power_copy(d, pw.at[lax.rem(ch + 4 - d, 4)]).wait_recv()
    power = (pw[0] + pw[1]) + (pw[2] + pw[3])
    inv_row = lax.rsqrt(power / (4 * width) + norm_eps)[0:1]
    for ref, at, ids in (
        (inv_f, 0, last_ids), (inv_f, rows, own_ids), (inv_r, 0, own_other), (inv_r, rows, next_other),
    ):
        col = jnp.sum(jnp.where(letters == ids, inv_row, 0.0), axis=1, keepdims=True)
        col = jnp.broadcast_to(col, (rows, LANES))
        for s in range(SUB):
            ref[pl.ds(at * SUB + s, rows, stride=SUB), :] = col

    def scale_rows(i, carry):
        for ext, inv in ((ext_f, inv_f), (ext_r, inv_r)):
            value = rows3(ext, i * 16, 16) * rows3(inv, i * 16, 16) * gain8[...][None]
            put3(ext, i * 16, value.astype(bf16).astype(f32))
        return carry

    lax.fori_loop(0, 2 * rows // 16, scale_rows, 0)
    relay(0)
    step_a()

    chunk = 16
    parts = rows // chunk

    def s_rows(cy, k):
        return sbuf.at[pl.ds(pl.multiple_of(cy * rows + k * chunk, chunk), chunk), :]

    def s_copy(k, kind, ref, cy):
        return pltpu.make_async_remote_copy(
            src_ref=ref, dst_ref=ref, send_sem=s_send.at[3 * k + kind],
            recv_sem=s_recv.at[3 * k + kind], device_id=at_ctx(x, zh, cy), device_id_type=MESH,
        )

    steps = {1: step_b, 3: step_c, 5: lambda: relay(2), 6: lambda: relay(1), 7: lambda: relay(3)}

    def sixteen(i, carry):
        conv_block(i, rows, ext_f, ext_r, tv, dv, tr, dr, sv, ev, res)
        at = pl.ds(pl.multiple_of(y * rows + i * chunk, chunk), chunk)
        for s in range(SUB):
            block = res[pl.ds(i * chunk * SUB + s, chunk, stride=SUB), :]
            sbuf[at, s * LANES : (s + 1) * LANES] = block.astype(bf16)
        for kind, cy in ((2, y2), (0, yp), (1, ym)):
            s_copy(i, kind, s_rows(y, i), cy).start()
        for when, step in steps.items():
            pl.when(i == when)(step)
        return carry

    lax.fori_loop(0, parts, sixteen, 0)

    blocks = owner_ref.shape[1]
    spread = ((iota((blocks, segs), 1) >> 2) == iota((blocks, segs), 0)).astype(bf16)
    owners = jnp.broadcast_to(owner_ref[...], (SUB, blocks)).astype(f32).astype(bf16)
    owner_row = jnp.dot(owners, spread, preferred_element_type=f32)[0:1].astype(jnp.int32)
    slot, seg = iota((segs, segs), 0), iota((segs, segs), 1)
    same = (owner_row == (slot >> 2)) & ((slot & 3) == (seg & 3))
    slot_start = jnp.sum(jnp.where(same, starts_row, 0.0), axis=1, keepdims=True)
    slot_end = jnp.sum(jnp.where(same, ends_row, 0.0), axis=1, keepdims=True)
    total = 4 * rows
    spot = (iota((segs, total), 1) + lax.div(me, 4) * total).astype(f32)
    member[...] = ((slot_start <= spot) & (spot < slot_end)).astype(f32).astype(bf16)
    scale[...] = jnp.broadcast_to(slot_end - slot_start, (segs, LANES))

    def s_finish(k, carry):
        for kind, cy in enumerate((ym, yp, y2)):
            s_copy(k, kind, s_rows(cy, k), yp).wait_recv()
        return carry

    lax.fori_loop(0, parts, s_finish, 0)
    w_wait(*[name for name in got if name not in seen])

    group = 4 * cols

    def product(g, h):
        rhs = wbuf[pl.ds(pl.multiple_of(g * group + h * LANES, LANES), LANES), :]
        return lax.dot_general(
            sbuf[...], rhs, (((1,), (1,)), ((), ())), preferred_element_type=f32
        )

    def core_copy(n):
        return pltpu.make_async_remote_copy(
            src_ref=out1.at[n], dst_ref=in1.at[n], send_sem=r_send.at[n],
            recv_sem=r_recv.at[n], device_id={"ch": core_peer}, device_id_type=MESH,
        )

    def z_copy(h, t):
        at = pl.ds(t * 2 * rows, 2 * rows)
        return pltpu.make_async_remote_copy(
            src_ref=zout.at[h, at, :], dst_ref=zin.at[h, at, :], send_sem=z_send.at[2 * h + t],
            recv_sem=z_recv.at[2 * h + t], device_id={"ch": z_peer}, device_id_type=MESH,
        )

    for h in range(2):
        out1[h] = product(2 * (1 - zl) + 1 - core, h).astype(bf16)
        core_copy(h).start()
    for h in range(2):
        kept[h] = product(2 * (1 - zl) + core, h)
        core_copy(h).wait_recv()
        for t in range(2):
            at = pl.ds(t * 2 * rows, 2 * rows)
            zout[h, at, :] = (kept[h, at, :] + in1[h, at, :].astype(f32)).astype(bf16)
            z_copy(h, t).start()
    for h in range(2):
        out1[2 + h] = product(2 * zl + 1 - core, h).astype(bf16)
        core_copy(2 + h).start()
    for h in range(2):
        kept[h] = product(2 * zl + core, h)

    share = 16 * SUB // 2

    def to_x(h, d):
        n = 3 * h + d - 1
        return pltpu.make_async_remote_copy(
            src_ref=psend.at[h, pl.ds(pl.multiple_of(ring(x, d) * share, share), share), :],
            dst_ref=xbuf.at[n], send_sem=x_send.at[n], recv_sem=x_recv.at[n],
            device_id=at_ctx(ring(x, d), zh, y), device_id_type=MESH,
        )

    for h in range(2):
        highs, lows = [], []
        core_copy(2 + h).wait_recv()
        for t in range(2):
            at = pl.ds(t * 2 * rows, 2 * rows)
            z_copy(h, t).wait_recv()
            scores = kept[h, at, :] + in1[2 + h, at, :].astype(f32) + zin[h, at, :].astype(f32)
            active = jnp.maximum(scores, 0.0) + jnp.log1p(jnp.exp(-jnp.abs(scores)))
            highs.append(active.astype(bf16))
            lows.append((active - highs[-1].astype(f32)).astype(bf16))
        halves = jnp.concatenate(
            [jnp.concatenate(highs, axis=0), jnp.concatenate(lows, axis=0)], axis=1
        )
        sums = jnp.dot(member[...], halves, preferred_element_type=f32)
        pbuf[h] = (sums[:, :LANES] + sums[:, LANES:]) / scale[...]
        psend[h] = pbuf[h].astype(bf16)
        for d in (2, 1, 3):
            to_x(h, d).start()
    for h in range(2):
        mine = pbuf[h, pl.ds(pl.multiple_of(x * share, share), share), :]
        for d in range(1, 4):
            to_x(h, d).wait_recv()
            mine = mine + xbuf[3 * h + d - 1].astype(f32)
        abuf[pl.ds(h, share, stride=2), :] = mine

    def tile_at(cz, cy):
        return pl.ds(pl.multiple_of((cz * 4 + cy) * SUB, SUB), SUB)

    def to_owner(d, carry):
        cz, cy = ring(zh, lax.div(d, 4)), ring(y, lax.rem(d, 4))
        pltpu.make_async_remote_copy(
            src_ref=abuf.at[tile_at(cz, cy), :], dst_ref=rbuf.at[tile_at(zh, y), :],
            send_sem=a_send, recv_sem=a_recv, device_id=plane(d), device_id_type=MESH,
        ).start()
        return carry

    lax.fori_loop(1, 16, to_owner, 0)
    rbuf[tile_at(zh, y), :] = abuf[tile_at(zh, y), :]
    most = pl.ds(0, 15 * SUB)
    all_of = pltpu.make_async_remote_copy(
        src_ref=abuf.at[most, :], dst_ref=rbuf.at[most, :], send_sem=a_send, recv_sem=a_recv,
        device_id=plane(1), device_id_type=MESH,
    )
    all_of.wait_recv()
    for q in range(4):
        acc = rbuf[pl.ds(q * SUB, SUB), :]
        for m in range(1, 4):
            acc = acc + rbuf[pl.ds((4 * m + q) * SUB, SUB), :]
        obuf[pl.ds(q * SUB, SUB), :] = acc
        obuf[pl.ds((4 + q) * SUB, SUB), :] = pltpu.roll(acc, LANES // 2, 1)
    count = out_ref.shape[0]
    left = iota((count, LANES), 1) < LANES // 2
    for hz in range(2):
        for q in range(2):
            plain = [obuf[pl.ds((2 * q + n) * SUB + hz, count, stride=2), :] for n in range(2)]
            moved = [obuf[pl.ds((4 + 2 * q + n) * SUB + hz, count, stride=2), :] for n in range(2)]
            for b in range(2):
                pair = (plain[0], moved[1]) if b == 0 else (moved[0], plain[1])
                lane = ((2 * hz + b) * 2 + q) * LANES
                out_ref[:, lane : lane + LANES] = jnp.where(left, *pair)

    all_of.wait_send()
    for name in sent:
        w_copy(name, *sent[name]).wait_send()

    def s_drain(k, carry):
        for kind in range(3):
            s_copy(k, kind, s_rows(y, k), yp).wait_send()
        return carry

    lax.fori_loop(0, parts, s_drain, 0)
    for d in range(1, 4):
        power_copy(d, pw.at[ch]).wait_send()
        to_x(0, d).wait_send()
        to_x(1, d).wait_send()
    token_copy(0, after).wait_send()
    token_copy(2, before).wait_send()
    for n in range(4):
        core_copy(n).wait_send()
        z_copy(n // 2, n % 2).wait_send()


def body(tokens, complement, seg_lengths, owner, embed, norm_gain, taps, w_out):
    rows = tokens.shape[0]
    vocab, width = embed.shape
    cols = w_out.shape[1]
    segs = seg_lengths.shape[0]
    per_block = segs // owner.shape[0]
    total, group = 4 * rows, 4 * cols
    vmem = pl.BlockSpec(memory_space=pltpu.VMEM)
    hbm = pl.BlockSpec(memory_space=pl.ANY)

    def tiles(count, dtype=f32):
        return pltpu.VMEM((count * SUB, LANES), dtype)

    def sems(count):
        return pltpu.SemaphoreType.DMA((count,))

    return pl.pallas_call(
        score_kernel,
        out_shape=jax.ShapeDtypeStruct((per_block, width), f32),
        in_specs=[vmem] * 5 + [hbm] * 3,
        out_specs=vmem,
        scratch_shapes=[
            pltpu.VMEM((vocab, width), bf16),
            pltpu.VMEM((taps.shape[0], width), f32),
            pltpu.VMEM((total, width), bf16),
            pltpu.VMEM((16 * cols, width), bf16),
            pltpu.VMEM((4, total, LANES), bf16),
            pltpu.VMEM((4, total, LANES), bf16),
            pltpu.VMEM((2, total, LANES), bf16),
            pltpu.VMEM((2, total, LANES), bf16),
            pltpu.VMEM((2, total, LANES), f32),
            pltpu.VMEM((2, segs, LANES), f32),
            pltpu.VMEM((2, segs, LANES), bf16),
            pltpu.VMEM((6, 8 * SUB, LANES), bf16),
            tiles(16),
            tiles(16),
            tiles(8),
            pltpu.VMEM((segs, total), bf16),
            pltpu.VMEM((segs, LANES), f32),
            pltpu.VMEM((3, SUB, rows), jnp.int32),
            pltpu.VMEM((4, SUB, vocab), f32),
            tiles(1),
        ]
        + [tiles(2 * rows)] * 4
        + [tiles(TAPROWS)] * 4
        + [tiles(rows, jnp.int32)] * 2
        + [tiles(rows)]
        + [sems(3), sems(30), sems(30), sems(24), sems(24), sems(4), sems(4), sems(4), sems(4)]
        + [sems(6), sems(6), pltpu.SemaphoreType.DMA, pltpu.SemaphoreType.DMA]
        + [sems(2), sems(2), sems(3), sems(3)],
        compiler_params=pltpu.CompilerParams(
            vmem_limit_bytes=56 << 20, collective_id=0, has_side_effects=True
        ),
    )(
        tokens[None, :], complement[None, :], seg_lengths[None, :], owner[None, :],
        norm_gain[None, :], embed, taps, w_out.T,
    )


def solution(mesh):
    in_specs = (P("ctx"), P(), P(), P(), P(None, "ch"), P("ch"), P(None, "ch"), P("ch", "ctx"))
    out_specs = P("ctx", "ch")
    return jax.shard_map(body, mesh=mesh, in_specs=in_specs, out_specs=out_specs, check_vma=False)
```
